128 devices in a mesh: rep: 4 (over x_hi, core), shard: 32 (over y, x_lo, z).
Axes of the slice: x: 4 (x_hi: 2, x_lo: 2; x = x_hi * 2 + x_lo), y: 4, z: 4, core: 2. Of those that a mesh axis runs over, the one named last changes fastest.
Arguments:
- inputs: bfloat16 [128, 128, 1024], P(('rep', 'shard')), may hold values from -6 to 6
- lengths: int32 [128], P(('rep', 'shard')), may hold values from 32 to 128, as said below
- cotangent: bfloat16 [128, 128, 1024], P(('rep', 'shard')), may hold values from -6 to 6
- w_qkv: bfloat16 [1, 1024, 3072], P(None, 'shard'), may hold values from -0.1875 to 0.1875
- b_qv: bfloat16 [1, 2, 1024], P(None, None, 'shard'), may hold values from -4 to 4
- w_att: bfloat16 [1, 1024, 1024], P(None, 'shard'), may hold values from -1 to 1
- b_att: bfloat16 [1, 1024], P(None, 'shard'), may hold values from -4 to 4
- norm1_gain: bfloat16 [1, 1024], P(None, 'shard'), may hold values from 0.5 to 1.5
- norm1_bias: bfloat16 [1, 1024], P(None, 'shard'), may hold values from -4 to 4
- w_in: bfloat16 [1, 1024, 4096], P(None, 'shard'), may hold values from -0.1875 to 0.1875
- b_in: bfloat16 [1, 4096], P(None, 'shard'), may hold values from -4 to 4
- w_out: bfloat16 [1, 4096, 1024], P(None, 'shard'), may hold values from -0.09375 to 0.09375
- b_out: bfloat16 [1, 1024], P(None, 'shard'), may hold values from -4 to 4
- norm2_gain: bfloat16 [1, 1024], P(None, 'shard'), may hold values from 0.5 to 1.5
- norm2_bias: bfloat16 [1, 1024], P(None, 'shard'), may hold values from -4 to 4
Outputs:
- outputs: bfloat16 [128, 128, 1024], P(('rep', 'shard'))
- grad_inputs: float32 [128, 128, 1024], P(('rep', 'shard'))
- grad_w_qkv: float32 [1, 1024, 3072], P(None, 'shard')
- grad_b_qv: float32 [1, 2, 1024], P(None, None, 'shard')
- grad_w_att: float32 [1, 1024, 1024], P(None, 'shard')
- grad_b_att: float32 [1, 1024], P(None, 'shard')
- grad_norm1_gain: float32 [1, 1024], P(None, 'shard')
- grad_norm1_bias: float32 [1, 1024], P(None, 'shard')
- grad_w_in: float32 [1, 1024, 4096], P(None, 'shard')
- grad_b_in: float32 [1, 4096], P(None, 'shard')
- grad_w_out: float32 [1, 4096, 1024], P(None, 'shard')
- grad_b_out: float32 [1, 1024], P(None, 'shard')
- grad_norm2_gain: float32 [1, 1024], P(None, 'shard')
- grad_norm2_bias: float32 [1, 1024], P(None, 'shard')
The draws below stay inside these ranges and needn't reach their ends.
Inputs may be any that keep to these rules, and one draw needn't show every extreme that they name: `lengths`: some sequence has all 128 positions valid.
All inputs are finite; a program needn't handle non-finite values.
Results may differ from the reference program's by a relative error of at most 0.013.
Values may be sent and summed in bfloat16 or wider, within the bound.
No kernel may reach another device: no remote copies, remote signals or barrier semaphores. Data moves between devices by JAX's collectives and lax.ppermute only.
A program may use at most 192 MiB of HBM per device.

```python
import math
import jax
import jax.numpy as jnp
from jax import lax

D = 1024
HEAD_DIM = 64
FF = 4096
SEQ_LEN = 128
LAYERS = 1
SEQS = 128
N_SHARD = 32


def draw_lengths(key, part):
    values = jax.random.randint(jax.random.fold_in(key, 11), (SEQS,), SEQ_LEN // 4, SEQ_LEN + 1)
    where_full = jax.random.randint(jax.random.fold_in(key, 12), (), 0, SEQS)
    values = values.at[where_full].set(SEQ_LEN)
    values = values.at[(where_full + 1) % SEQS].set(SEQ_LEN // 4)
    return values.astype(jnp.int32)


def block_levels(key, dims, shards, smallest, largest):
    def one(position, parts):
        draws = jax.random.uniform(jax.random.fold_in(jax.random.fold_in(key, 6), position), (parts,), jnp.float32, smallest / len(shards), largest / len(shards))
        return jnp.repeat(jnp.exp(draws), dims[position] // parts).reshape((-1,) + (1,) * (len(dims) - position - 1))

    loudness = one(*shards[0])
    for cut in shards[1:]:
        loudness = loudness * one(*cut)
    return loudness


def centred(rng, extent, width, reach, shards=(), dtype=jnp.bfloat16):
    values = width * jax.random.normal(rng, extent, jnp.float32)
    if shards:
        values = values * block_levels(rng, extent, shards, -0.22, 0.18)
    return jnp.clip(values, -reach, reach).astype(dtype)


def setup_inputs(seed: int = 0) -> dict:
    arg_keys = jax.random.split(jax.random.key(seed), 16)
    return {
        "inputs": centred(arg_keys[0], (SEQS, SEQ_LEN, D), 1.0, 6.0, ((0, 128),)),
        "lengths": draw_lengths(jax.random.fold_in(arg_keys[15], 71), 0),
        "cotangent": centred(arg_keys[2], (SEQS, SEQ_LEN, D), 1.0, 6.0, ((0, 128),)),
        "w_qkv": centred(arg_keys[3], (LAYERS, D, 3 * D), D ** -0.5, 0.1875, ((1, 32),)),
        "b_qv": centred(arg_keys[4], (LAYERS, 2, D), 0.3, 4.0, ((2, 32),)),
        "w_att": centred(arg_keys[5], (LAYERS, D, D), (D // 32) ** -0.5, 1.0, ((1, 32),)),
        "b_att": centred(arg_keys[6], (LAYERS, D), 0.3, 4.0, ((1, 32),)),
        "norm1_gain": jnp.clip(1.0 + 0.1 * jax.random.normal(arg_keys[7], (LAYERS, D), jnp.float32), 0.5, 1.5).astype(jnp.bfloat16),
        "norm1_bias": centred(arg_keys[8], (LAYERS, D), 0.3, 4.0, ((1, 32),)),
        "w_in": centred(arg_keys[9], (LAYERS, D, FF), D ** -0.5, 0.1875, ((1, 32),)),
        "b_in": centred(arg_keys[10], (LAYERS, FF), 0.3, 4.0, ((1, 32),)),
        "w_out": centred(arg_keys[11], (LAYERS, FF, D), FF ** -0.5, 0.09375, ((1, 32),)),
        "b_out": centred(arg_keys[12], (LAYERS, D), 0.3, 4.0, ((1, 32),)),
        "norm2_gain": jnp.clip(1.0 + 0.1 * jax.random.normal(arg_keys[13], (LAYERS, D), jnp.float32), 0.5, 1.5).astype(jnp.bfloat16),
        "norm2_bias": centred(arg_keys[14], (LAYERS, D), 0.3, 4.0, ((1, 32),)),
    }


EPS = 1e-12
ROOT_HALF = 0.7071067811865476
INV_ROOT_TWO_PI = 0.3989422804014327

def batched(form, left, right):
    return jnp.einsum(form, left.astype(jnp.float32), right.astype(jnp.float32))

def layer_norm(residual, gain, shift):
    row_mean = lax.optimization_barrier(jnp.mean(residual, axis=-1, keepdims=True))
    centered = residual - row_mean
    variance = lax.optimization_barrier(jnp.mean(centered * centered, axis=-1, keepdims=True))
    inv_std = lax.rsqrt(variance + EPS)
    normed = centered * inv_std
    return (normed * gain.astype(jnp.float32) + shift.astype(jnp.float32), normed, inv_std)

def norm_backward(upstream, normed, inv_std, gain):
    grad_gain = lax.optimization_barrier(jnp.sum(upstream * normed, axis=0))
    grad_shift = lax.optimization_barrier(jnp.sum(upstream, axis=0))
    scaled = upstream * gain.astype(jnp.float32)
    grad_res = inv_std * (scaled - lax.optimization_barrier(jnp.mean(scaled, axis=-1, keepdims=True)) - normed * lax.optimization_barrier(jnp.mean(scaled * normed, axis=-1, keepdims=True)))
    return (grad_res, grad_gain, grad_shift)

def attention_scores(query_bf, key_bf, key_valid):
    scores = batched('bqhe,bkhe->bhqk', query_bf, key_bf) * (1.0 / math.sqrt(HEAD_DIM))
    return jnp.where(key_valid[:, None, None, :], scores, -1e+30)

def layer_forward(hidden, hidden_bf, params, key_valid, batch_size):
    w_qkv, b_qv, w_att, b_att, gain_one, shift_one, w_in, b_in, w_out, b_out, gain_two, shift_two = params
    model_width = hidden.shape[1]
    seq_count = hidden.shape[0] // batch_size
    shape_heads = (batch_size, seq_count, model_width // HEAD_DIM, HEAD_DIM)
    packed = jnp.dot(hidden_bf, w_qkv, preferred_element_type=jnp.float32)
    bias_qv = b_qv.astype(jnp.float32)
    query_bf = (packed[:, :model_width] + bias_qv[0]).astype(jnp.bfloat16).reshape(shape_heads)
    key_bf = packed[:, model_width:2 * model_width].astype(jnp.bfloat16).reshape(shape_heads)
    value_bf = (packed[:, 2 * model_width:] + bias_qv[1]).astype(jnp.bfloat16).reshape(shape_heads)
    scores = attention_scores(query_bf, key_bf, key_valid)
    row_max = lax.optimization_barrier(jnp.max(scores, axis=-1, keepdims=True))
    row_lse = row_max + jnp.log(lax.optimization_barrier(jnp.sum(jnp.exp(scores - row_max), axis=-1, keepdims=True)))
    probs_bf = jnp.exp(scores - row_lse).astype(jnp.bfloat16)
    context_bf = batched('bhqk,bkhe->bqhe', probs_bf, value_bf).astype(jnp.bfloat16).reshape(-1, model_width)
    first = hidden + jnp.dot(context_bf, w_att, preferred_element_type=jnp.float32) + b_att.astype(jnp.float32)
    middle, normed_one, inv_one = layer_norm(first, gain_one, shift_one)
    middle_bf = middle.astype(jnp.bfloat16)
    pre_act = jnp.dot(middle_bf, w_in, preferred_element_type=jnp.float32) + b_in.astype(jnp.float32)
    act_bf = (pre_act * 0.5 * (1.0 + jax.scipy.special.erf(pre_act * ROOT_HALF))).astype(jnp.bfloat16)
    second = middle + jnp.dot(act_bf, w_out, preferred_element_type=jnp.float32) + b_out.astype(jnp.float32)
    result, normed_two, inv_two = layer_norm(second, gain_two, shift_two)
    stored = (hidden_bf, query_bf, key_bf, value_bf, row_lse, context_bf, normed_one, inv_one, middle_bf, pre_act, act_bf, normed_two, inv_two)
    return (result, stored)

def layer_backward(upstream, stored, params, key_valid, batch_size):
    w_qkv, b_qv, w_att, b_att, gain_one, shift_one, w_in, b_in, w_out, b_out, gain_two, shift_two = params
    hidden_bf, query_bf, key_bf, value_bf, row_lse, context_bf, normed_one, inv_one, middle_bf, pre_act, act_bf, normed_two, inv_two = stored
    model_width = upstream.shape[1]
    shape_heads = query_bf.shape
    grad_second, grad_gain_two, grad_shift_two = norm_backward(upstream, normed_two, inv_two, gain_two)
    grad_b_out = lax.optimization_barrier(jnp.sum(grad_second, axis=0))
    second_bf = grad_second.astype(jnp.bfloat16)
    grad_w_out = jnp.dot(act_bf.T, second_bf, preferred_element_type=jnp.float32)
    back_act = jnp.dot(second_bf, w_out.T, preferred_element_type=jnp.float32)
    cumulative = 0.5 * (1.0 + jax.scipy.special.erf(pre_act * ROOT_HALF))
    density = jnp.exp(-0.5 * pre_act * pre_act) * INV_ROOT_TWO_PI
    grad_pre = back_act * (cumulative + pre_act * density)
    pre_bf = grad_pre.astype(jnp.bfloat16)
    grad_w_in = jnp.dot(middle_bf.T, pre_bf, preferred_element_type=jnp.float32)
    grad_b_in = lax.optimization_barrier(jnp.sum(grad_pre, axis=0))
    grad_middle = grad_second + jnp.dot(pre_bf, w_in.T, preferred_element_type=jnp.float32)
    grad_first, grad_gain_one, grad_shift_one = norm_backward(grad_middle, normed_one, inv_one, gain_one)
    grad_b_att = lax.optimization_barrier(jnp.sum(grad_first, axis=0))
    first_bf = grad_first.astype(jnp.bfloat16)
    grad_w_att = jnp.dot(context_bf.T, first_bf, preferred_element_type=jnp.float32)
    grad_context = jnp.dot(first_bf, w_att.T, preferred_element_type=jnp.float32).astype(jnp.bfloat16).reshape(shape_heads)
    scores = attention_scores(query_bf, key_bf, key_valid)
    probs = jnp.exp(scores - row_lse)
    grad_value = batched('bhqk,bqhe->bkhe', probs.astype(jnp.bfloat16), grad_context).reshape(-1, model_width)
    grad_probs = batched('bqhe,bkhe->bhqk', grad_context, value_bf)
    inner = lax.optimization_barrier(jnp.sum(probs * grad_probs, axis=-1, keepdims=True))
    grad_scores = (probs * (grad_probs - inner) * (1.0 / math.sqrt(HEAD_DIM))).astype(jnp.bfloat16)
    grad_query = batched('bhqk,bkhe->bqhe', grad_scores, key_bf).reshape(-1, model_width)
    grad_key = batched('bhqk,bqhe->bkhe', grad_scores, query_bf).reshape(-1, model_width)
    grad_b_qv = jnp.stack([lax.optimization_barrier(jnp.sum(grad_query, axis=0)), lax.optimization_barrier(jnp.sum(grad_value, axis=0))])
    packed_bf = jnp.concatenate([grad_query, grad_key, grad_value], axis=1).astype(jnp.bfloat16)
    grad_w_qkv = jnp.dot(hidden_bf.T, packed_bf, preferred_element_type=jnp.float32)
    grad_hidden = grad_first + jnp.dot(packed_bf, w_qkv.T, preferred_element_type=jnp.float32)
    terms = (grad_w_qkv, grad_b_qv, grad_w_att, grad_b_att, grad_gain_one, grad_shift_one, grad_w_in, grad_b_in, grad_w_out, grad_b_out, grad_gain_two, grad_shift_two)
    return (grad_hidden, terms)

def reference(inputs, lengths, cotangent, w_qkv, b_qv, w_att, b_att, norm1_gain, norm1_bias, w_in, b_in, w_out, b_out, norm2_gain, norm2_bias):
    all_params = (w_qkv, b_qv, w_att, b_att, norm1_gain, norm1_bias, w_in, b_in, w_out, b_out, norm2_gain, norm2_bias)
    block_seqs = N_SHARD
    seq_total = inputs.shape[0]
    seq_count = inputs.shape[1]
    model_width = inputs.shape[2]
    blocks = seq_total // block_seqs

    def per_block(carry, block):
        x_block, len_block, cot_block = block
        key_valid = lax.broadcasted_iota(jnp.int32, (block_seqs, seq_count), 1) < len_block[:, None]
        hidden = x_block.astype(jnp.float32).reshape(-1, model_width)
        hidden_bf = x_block.reshape(-1, model_width)
        stored_list = []
        for layer_index in range(LAYERS):
            params = tuple((member[layer_index] for member in all_params))
            hidden, stored = layer_forward(hidden, hidden_bf, params, key_valid, block_seqs)
            hidden_bf = hidden.astype(jnp.bfloat16)
            stored_list.append(stored)
        upstream = cot_block.astype(jnp.float32).reshape(-1, model_width)
        layer_terms = [None] * LAYERS
        for layer_index in reversed(range(LAYERS)):
            params = tuple((member[layer_index] for member in all_params))
            upstream, terms = layer_backward(upstream, stored_list[layer_index], params, key_valid, block_seqs)
            layer_terms[layer_index] = terms
        updated = tuple((carry[member] + jnp.stack([layer_terms[layer_index][member] for layer_index in range(LAYERS)]) for member in range(12)))
        return (updated, (hidden_bf.reshape(x_block.shape), upstream.reshape(x_block.shape)))
    initial = tuple((jnp.zeros(member.shape, jnp.float32) for member in all_params))
    x_blocks = inputs.reshape(blocks, block_seqs, seq_count, model_width)
    len_blocks = lengths.reshape(blocks, block_seqs)
    cot_blocks = cotangent.reshape(blocks, block_seqs, seq_count, model_width)
    summed, (outs, grads_in) = lax.scan(per_block, initial, (x_blocks, len_blocks, cot_blocks))
    return (outs.reshape(inputs.shape), grads_in.reshape(inputs.shape), summed[0], summed[1], summed[2], summed[3], summed[4], summed[5], summed[6], summed[7], summed[8], summed[9], summed[10], summed[11])
```

```python
import math

import jax
import jax.numpy as jnp
from jax import lax
from jax.sharding import PartitionSpec as P

HEAD_DIM = 64
LAYERS = 1


EPS = 1e-12
ROOT_HALF = 0.7071067811865476
INV_ROOT_TWO_PI = 0.3989422804014327


def batched(form, left, right):
    return jnp.einsum(form, left, right, preferred_element_type=jnp.float32)


def layer_norm(residual, gain, shift):
    row_mean = jnp.mean(residual, axis=-1, keepdims=True)
    centered = residual - row_mean
    variance = jnp.mean(centered * centered, axis=-1, keepdims=True)
    inv_std = lax.rsqrt(variance + EPS)
    normed = centered * inv_std
    return (normed * gain.astype(jnp.float32) + shift.astype(jnp.float32), normed, inv_std)


def norm_backward(upstream, normed, inv_std, gain):
    grad_gain = jnp.sum(upstream * normed, axis=0)
    grad_shift = jnp.sum(upstream, axis=0)
    scaled = upstream * gain.astype(jnp.float32)
    grad_res = inv_std * (
        scaled
        - jnp.mean(scaled, axis=-1, keepdims=True)
        - normed * jnp.mean(scaled * normed, axis=-1, keepdims=True)
    )
    return (grad_res, grad_gain, grad_shift)


def attention_scores(query_bf, key_bf, key_valid):
    scores = batched("bqhe,bkhe->bhqk", query_bf, key_bf) * (1.0 / math.sqrt(HEAD_DIM))
    return jnp.where(key_valid[:, None, None, :], scores, -1e30)


def layer_forward(hidden, hidden_bf, params, key_valid, batch_size):
    (
        w_qkv,
        b_qv,
        w_att,
        b_att,
        gain_one,
        shift_one,
        w_in,
        b_in,
        w_out,
        b_out,
        gain_two,
        shift_two,
    ) = params
    model_width = hidden.shape[1]
    seq_count = hidden.shape[0] // batch_size
    shape_heads = (batch_size, seq_count, model_width // HEAD_DIM, HEAD_DIM)
    packed = jnp.dot(hidden_bf, w_qkv, preferred_element_type=jnp.float32)
    bias_qv = b_qv.astype(jnp.float32)
    query_bf = (packed[:, :model_width] + bias_qv[0]).astype(jnp.bfloat16).reshape(shape_heads)
    key_bf = packed[:, model_width : 2 * model_width].astype(jnp.bfloat16).reshape(shape_heads)
    value_bf = (packed[:, 2 * model_width :] + bias_qv[1]).astype(jnp.bfloat16).reshape(shape_heads)
    scores = attention_scores(query_bf, key_bf, key_valid)
    row_max = jnp.max(scores, axis=-1, keepdims=True)
    row_lse = row_max + jnp.log(jnp.sum(jnp.exp(scores - row_max), axis=-1, keepdims=True))
    probs_bf = jnp.exp(scores - row_lse).astype(jnp.bfloat16)
    context_bf = (
        batched("bhqk,bkhe->bqhe", probs_bf, value_bf).astype(jnp.bfloat16).reshape(-1, model_width)
    )
    first = (
        hidden
        + jnp.dot(context_bf, w_att, preferred_element_type=jnp.float32)
        + b_att.astype(jnp.float32)
    )
    middle, normed_one, inv_one = layer_norm(first, gain_one, shift_one)
    middle_bf = middle.astype(jnp.bfloat16)
    pre_act = jnp.dot(middle_bf, w_in, preferred_element_type=jnp.float32) + b_in.astype(
        jnp.float32
    )
    act_bf = (pre_act * 0.5 * (1.0 + jax.scipy.special.erf(pre_act * ROOT_HALF))).astype(
        jnp.bfloat16
    )
    second = (
        middle
        + jnp.dot(act_bf, w_out, preferred_element_type=jnp.float32)
        + b_out.astype(jnp.float32)
    )
    result, normed_two, inv_two = layer_norm(second, gain_two, shift_two)
    stored = (
        hidden_bf,
        query_bf,
        key_bf,
        value_bf,
        row_lse,
        context_bf,
        normed_one,
        inv_one,
        middle_bf,
        pre_act,
        act_bf,
        normed_two,
        inv_two,
    )
    return (result, stored)


def layer_backward(upstream, stored, params, key_valid):
    (
        w_qkv,
        b_qv,
        w_att,
        b_att,
        gain_one,
        shift_one,
        w_in,
        b_in,
        w_out,
        b_out,
        gain_two,
        shift_two,
    ) = params
    (
        hidden_bf,
        query_bf,
        key_bf,
        value_bf,
        row_lse,
        context_bf,
        normed_one,
        inv_one,
        middle_bf,
        pre_act,
        act_bf,
        normed_two,
        inv_two,
    ) = stored
    model_width = upstream.shape[1]
    shape_heads = query_bf.shape
    grad_second, grad_gain_two, grad_shift_two = norm_backward(
        upstream, normed_two, inv_two, gain_two
    )
    grad_b_out = jnp.sum(grad_second, axis=0)
    second_bf = grad_second.astype(jnp.bfloat16)
    grad_w_out = jnp.dot(act_bf.T, second_bf, preferred_element_type=jnp.float32)
    back_act = jnp.dot(second_bf, w_out.T, preferred_element_type=jnp.float32)
    cumulative = 0.5 * (1.0 + jax.scipy.special.erf(pre_act * ROOT_HALF))
    density = jnp.exp(-0.5 * pre_act * pre_act) * INV_ROOT_TWO_PI
    grad_pre = back_act * (cumulative + pre_act * density)
    pre_bf = grad_pre.astype(jnp.bfloat16)
    grad_w_in = jnp.dot(middle_bf.T, pre_bf, preferred_element_type=jnp.float32)
    grad_b_in = jnp.sum(grad_pre, axis=0)
    grad_middle = grad_second + jnp.dot(pre_bf, w_in.T, preferred_element_type=jnp.float32)
    grad_first, grad_gain_one, grad_shift_one = norm_backward(
        grad_middle, normed_one, inv_one, gain_one
    )
    grad_b_att = jnp.sum(grad_first, axis=0)
    first_bf = grad_first.astype(jnp.bfloat16)
    grad_w_att = jnp.dot(context_bf.T, first_bf, preferred_element_type=jnp.float32)
    grad_context = (
        jnp.dot(first_bf, w_att.T, preferred_element_type=jnp.float32)
        .astype(jnp.bfloat16)
        .reshape(shape_heads)
    )
    scores = attention_scores(query_bf, key_bf, key_valid)
    probs = jnp.exp(scores - row_lse)
    grad_value = batched("bhqk,bqhe->bkhe", probs.astype(jnp.bfloat16), grad_context).reshape(
        -1, model_width
    )
    grad_probs = batched("bqhe,bkhe->bhqk", grad_context, value_bf)
    inner = jnp.sum(probs * grad_probs, axis=-1, keepdims=True)
    grad_scores = (probs * (grad_probs - inner) * (1.0 / math.sqrt(HEAD_DIM))).astype(jnp.bfloat16)
    grad_query = batched("bhqk,bkhe->bqhe", grad_scores, key_bf).reshape(-1, model_width)
    grad_key = batched("bhqk,bqhe->bkhe", grad_scores, query_bf).reshape(-1, model_width)
    grad_b_qv = jnp.stack([jnp.sum(grad_query, axis=0), jnp.sum(grad_value, axis=0)])
    packed_bf = jnp.concatenate([grad_query, grad_key, grad_value], axis=1).astype(jnp.bfloat16)
    grad_w_qkv = jnp.dot(hidden_bf.T, packed_bf, preferred_element_type=jnp.float32)
    grad_hidden = grad_first + jnp.dot(packed_bf, w_qkv.T, preferred_element_type=jnp.float32)
    terms = (
        grad_w_qkv,
        grad_b_qv,
        grad_w_att,
        grad_b_att,
        grad_gain_one,
        grad_shift_one,
        grad_w_in,
        grad_b_in,
        grad_w_out,
        grad_b_out,
        grad_gain_two,
        grad_shift_two,
    )
    return (grad_hidden, terms)


SHARD_AXES = ("y", "xl", "z")
PAIR_AXES = ("xh", "core")


def pack_halves(w_qkv, w_att, w_in, w_out, small):
    rows = w_qkv.shape[0]
    split = w_qkv.shape[1]
    pad = jnp.zeros((rows, small.shape[1]), w_qkv.dtype)
    first = jnp.concatenate([w_qkv, w_in[:, :split], pad], axis=1)
    second = jnp.concatenate(
        [w_att, w_in[:, split:], w_out.reshape(rows, -1), small], axis=1
    )
    return first, second


def unpack_halves(first, second, width, ff):
    split = 3 * width
    w_qkv = first[:, :split]
    w_in = jnp.concatenate([first[:, split : 2 * split], second[:, width : width + ff - split]], axis=1)
    at = width + ff - split
    w_att = second[:, :width]
    w_out = second[:, at : at + ff]
    small = second[:, at + ff :]
    return w_qkv, w_att, w_in, w_out, small


def body(
    inputs,
    lengths,
    cotangent,
    w_qkv,
    b_qv,
    w_att,
    b_att,
    norm1_gain,
    norm1_bias,
    w_in,
    b_in,
    w_out,
    b_out,
    norm2_gain,
    norm2_bias,
):
    batch_size, seq_count, model_width = inputs.shape
    ff = w_in.shape[2]
    rows = w_qkv.shape[1]
    core = lax.axis_index("core")
    key_valid = lax.broadcasted_iota(jnp.int32, (batch_size, seq_count), 1) < lengths[:, None]
    hidden = inputs.astype(jnp.float32).reshape(-1, model_width)
    hidden_bf = inputs.reshape(-1, model_width)
    small = jnp.concatenate(
        [
            b_qv[0].T,
            b_att[0][:, None],
            norm1_gain[0][:, None],
            norm1_bias[0][:, None],
            b_out[0][:, None],
            norm2_gain[0][:, None],
            norm2_bias[0][:, None],
            b_in[0].reshape(rows, -1),
        ],
        axis=1,
    )
    first, second = pack_halves(w_qkv[0], w_att[0], w_in[0], w_out[0], small)
    mine = jnp.where(core == 0, first, second)
    gathered = lax.all_gather(mine, SHARD_AXES, axis=0, tiled=True)
    both = lax.all_gather(gathered, "core", axis=0, tiled=False)
    f_qkv, f_att, f_in, f_out, f_small = unpack_halves(both[0], both[1], model_width, ff)
    f_out = f_out.reshape(ff, model_width)
    f_bqv = f_small[:, 0:2].T
    f_bin = f_small[:, 8:].reshape(ff)
    params = (
        f_qkv,
        f_bqv,
        f_att,
        f_small[:, 2],
        f_small[:, 3],
        f_small[:, 4],
        f_in,
        f_bin,
        f_out,
        f_small[:, 5],
        f_small[:, 6],
        f_small[:, 7],
    )
    hidden, stored = layer_forward(hidden, hidden_bf, params, key_valid, batch_size)
    outputs = hidden.astype(jnp.bfloat16).reshape(inputs.shape)
    upstream = cotangent.astype(jnp.float32).reshape(-1, model_width)
    upstream, terms = layer_backward(upstream, stored, params, key_valid)
    (g_qkv, g_bqv, g_att, g_batt, g_n1g, g_n1b, g_in, g_bin, g_out, g_bout, g_n2g, g_n2b) = terms
    g_small = jnp.concatenate(
        [
            g_bqv.T,
            g_batt[:, None],
            g_n1g[:, None],
            g_n1b[:, None],
            g_bout[:, None],
            g_n2g[:, None],
            g_n2b[:, None],
            g_bin.reshape(model_width, -1),
        ],
        axis=1,
    )
    g_first, g_second = pack_halves(g_qkv, g_att, g_in, g_out, g_small)
    stacked = jnp.stack([g_first, g_second])
    half = lax.psum_scatter(stacked, "core", scatter_dimension=0, tiled=False)
    part = lax.psum_scatter(half, SHARD_AXES, scatter_dimension=0, tiled=True)
    part = lax.psum(part, "xh")
    res = lax.all_gather(part, "core", axis=0, tiled=False)
    r_qkv, r_att, r_in, r_out, r_small = unpack_halves(res[0], res[1], model_width, ff)
    grad_inputs = upstream.reshape(inputs.shape)
    return (
        outputs,
        grad_inputs,
        r_qkv[None],
        r_small[:, 0:2].T[None],
        r_att[None],
        r_small[:, 2][None],
        r_small[:, 3][None],
        r_small[:, 4][None],
        r_in[None],
        r_small[:, 8:].reshape(-1)[None],
        r_out.reshape(-1, model_width)[None],
        r_small[:, 5][None],
        r_small[:, 6][None],
        r_small[:, 7][None],
    )


def solution(mesh):
    devices = mesh.devices.reshape(2, 2, 4, 2, 4)
    fine = jax.sharding.Mesh(devices, ("xh", "core", "y", "xl", "z"))
    seqs = P(("xh", "core", "y", "xl", "z"), None, None)
    rows = P(None, SHARD_AXES, None)
    vec = P(None, SHARD_AXES)
    return jax.shard_map(
        body,
        mesh=fine,
        in_specs=(
            seqs,
            P(("xh", "core", "y", "xl", "z")),
            seqs,
            rows,
            P(None, None, SHARD_AXES),
            rows,
            vec,
            vec,
            vec,
            rows,
            vec,
            rows,
            vec,
            vec,
            vec,
        ),
        out_specs=(
            seqs,
            seqs,
            rows,
            P(None, None, SHARD_AXES),
            rows,
            vec,
            vec,
            vec,
            rows,
            vec,
            rows,
            vec,
            vec,
            vec,
        ),
        check_vma=False,
    )
```

```python
import math

import jax
import jax.numpy as jnp
from jax import lax
from jax.sharding import PartitionSpec as P

HEAD_DIM = 64
LAYERS = 1


EPS = 1e-12
ROOT_HALF = 0.7071067811865476
INV_ROOT_TWO_PI = 0.3989422804014327


def batched(form, left, right):
    return jnp.einsum(form, left, right, preferred_element_type=jnp.float32)


def layer_norm(residual, gain, shift):
    row_mean = jnp.mean(residual, axis=-1, keepdims=True)
    centered = residual - row_mean
    variance = jnp.mean(centered * centered, axis=-1, keepdims=True)
    inv_std = lax.rsqrt(variance + EPS)
    normed = centered * inv_std
    return (normed * gain.astype(jnp.float32) + shift.astype(jnp.float32), normed, inv_std)


def norm_backward(upstream, normed, inv_std, gain):
    grad_gain = jnp.sum(upstream * normed, axis=0)
    grad_shift = jnp.sum(upstream, axis=0)
    scaled = upstream * gain.astype(jnp.float32)
    grad_res = inv_std * (
        scaled
        - jnp.mean(scaled, axis=-1, keepdims=True)
        - normed * jnp.mean(scaled * normed, axis=-1, keepdims=True)
    )
    return (grad_res, grad_gain, grad_shift)


def attention_scores(query_bf, key_bf, key_valid):
    scores = batched("bqhe,bkhe->bhqk", query_bf, key_bf) * (1.0 / math.sqrt(HEAD_DIM))
    return jnp.where(key_valid[:, None, None, :], scores, -1e30)


def layer_forward(hidden, hidden_bf, params, key_valid, batch_size):
    (
        w_qkv,
        b_qv,
        w_att,
        b_att,
        gain_one,
        shift_one,
        w_in,
        b_in,
        w_out,
        b_out,
        gain_two,
        shift_two,
    ) = params
    model_width = hidden.shape[1]
    seq_count = hidden.shape[0] // batch_size
    shape_heads = (batch_size, seq_count, model_width // HEAD_DIM, HEAD_DIM)
    packed = jnp.dot(hidden_bf, w_qkv, preferred_element_type=jnp.float32)
    bias_qv = b_qv.astype(jnp.float32)
    query_bf = (packed[:, :model_width] + bias_qv[0]).astype(jnp.bfloat16).reshape(shape_heads)
    key_bf = packed[:, model_width : 2 * model_width].astype(jnp.bfloat16).reshape(shape_heads)
    value_bf = (packed[:, 2 * model_width :] + bias_qv[1]).astype(jnp.bfloat16).reshape(shape_heads)
    scores = attention_scores(query_bf, key_bf, key_valid)
    row_max = jnp.max(scores, axis=-1, keepdims=True)
    row_lse = row_max + jnp.log(jnp.sum(jnp.exp(scores - row_max), axis=-1, keepdims=True))
    probs_bf = jnp.exp(scores - row_lse).astype(jnp.bfloat16)
    context_bf = (
        batched("bhqk,bkhe->bqhe", probs_bf, value_bf).astype(jnp.bfloat16).reshape(-1, model_width)
    )
    first = (
        hidden
        + jnp.dot(context_bf, w_att, preferred_element_type=jnp.float32)
        + b_att.astype(jnp.float32)
    )
    middle, normed_one, inv_one = layer_norm(first, gain_one, shift_one)
    middle_bf = middle.astype(jnp.bfloat16)
    pre_act = jnp.dot(middle_bf, w_in, preferred_element_type=jnp.float32) + b_in.astype(
        jnp.float32
    )
    act_bf = (pre_act * 0.5 * (1.0 + jax.scipy.special.erf(pre_act * ROOT_HALF))).astype(
        jnp.bfloat16
    )
    second = (
        middle
        + jnp.einsum(
            "tkj,kjd->td",
            act_bf.reshape(act_bf.shape[0], -1, w_out.shape[1]),
            w_out,
            preferred_element_type=jnp.float32,
        )
        + b_out.astype(jnp.float32)
    )
    result, normed_two, inv_two = layer_norm(second, gain_two, shift_two)
    stored = (
        hidden_bf,
        query_bf,
        key_bf,
        value_bf,
        row_lse,
        context_bf,
        normed_one,
        inv_one,
        middle_bf,
        pre_act,
        act_bf,
        normed_two,
        inv_two,
    )
    return (result, stored)


def layer_backward(upstream, stored, params, key_valid):
    (
        w_qkv,
        b_qv,
        w_att,
        b_att,
        gain_one,
        shift_one,
        w_in,
        b_in,
        w_out,
        b_out,
        gain_two,
        shift_two,
    ) = params
    (
        hidden_bf,
        query_bf,
        key_bf,
        value_bf,
        row_lse,
        context_bf,
        normed_one,
        inv_one,
        middle_bf,
        pre_act,
        act_bf,
        normed_two,
        inv_two,
    ) = stored
    model_width = upstream.shape[1]
    shape_heads = query_bf.shape
    grad_second, grad_gain_two, grad_shift_two = norm_backward(
        upstream, normed_two, inv_two, gain_two
    )
    grad_b_out = jnp.sum(grad_second, axis=0)
    second_bf = grad_second.astype(jnp.bfloat16)
    back_act = jnp.einsum(
        "td,kjd->tkj", second_bf, w_out, preferred_element_type=jnp.float32
    ).reshape(second_bf.shape[0], -1)
    cumulative = 0.5 * (1.0 + jax.scipy.special.erf(pre_act * ROOT_HALF))
    density = jnp.exp(-0.5 * pre_act * pre_act) * INV_ROOT_TWO_PI
    grad_pre = back_act * (cumulative + pre_act * density)
    pre_bf = grad_pre.astype(jnp.bfloat16)
    grad_b_in = jnp.sum(grad_pre, axis=0)
    grad_middle = grad_second + jnp.dot(pre_bf, w_in.T, preferred_element_type=jnp.float32)
    grad_first, grad_gain_one, grad_shift_one = norm_backward(
        grad_middle, normed_one, inv_one, gain_one
    )
    grad_b_att = jnp.sum(grad_first, axis=0)
    first_bf = grad_first.astype(jnp.bfloat16)
    grad_context = (
        jnp.dot(first_bf, w_att.T, preferred_element_type=jnp.float32)
        .astype(jnp.bfloat16)
        .reshape(shape_heads)
    )
    scores = attention_scores(query_bf, key_bf, key_valid)
    probs = jnp.exp(scores - row_lse)
    grad_value = batched("bhqk,bqhe->bkhe", probs.astype(jnp.bfloat16), grad_context).reshape(
        -1, model_width
    )
    grad_probs = batched("bqhe,bkhe->bhqk", grad_context, value_bf)
    inner = jnp.sum(probs * grad_probs, axis=-1, keepdims=True)
    grad_scores = (probs * (grad_probs - inner) * (1.0 / math.sqrt(HEAD_DIM))).astype(jnp.bfloat16)
    grad_query = batched("bhqk,bkhe->bqhe", grad_scores, key_bf).reshape(-1, model_width)
    grad_key = batched("bhqk,bqhe->bkhe", grad_scores, query_bf).reshape(-1, model_width)
    grad_b_qv = jnp.stack([jnp.sum(grad_query, axis=0), jnp.sum(grad_value, axis=0)])
    packed_bf = jnp.concatenate([grad_query, grad_key, grad_value], axis=1).astype(jnp.bfloat16)
    grad_hidden = grad_first + jnp.dot(packed_bf, w_qkv.T, preferred_element_type=jnp.float32)
    terms = (
        (hidden_bf, packed_bf),
        grad_b_qv,
        (context_bf, first_bf),
        grad_b_att,
        grad_gain_one,
        grad_shift_one,
        (middle_bf, pre_bf),
        grad_b_in,
        (act_bf, second_bf),
        grad_b_out,
        grad_gain_two,
        grad_shift_two,
    )
    return (grad_hidden, terms)


SHARD_AXES = ("y", "xl", "z")
PAIR_AXES = ("xh", "core")


def pack_halves(w_qkv, w_att, w_in, w_out, small):
    rows = w_qkv.shape[0]
    split = w_qkv.shape[1]
    pad = jnp.zeros((rows, small.shape[1]), w_qkv.dtype)
    first = jnp.concatenate([w_qkv, w_in[:, :split], pad], axis=1)
    second = jnp.concatenate(
        [w_att, w_in[:, split:], w_out.reshape(rows, -1), small], axis=1
    )
    return first, second


def unpack_halves(first, second, width, ff):
    split = 3 * width
    w_qkv = first[:, :split]
    w_in = jnp.concatenate([first[:, split : 2 * split], second[:, width : width + ff - split]], axis=1)
    at = width + ff - split
    w_att = second[:, :width]
    w_out = second[:, at : at + ff]
    small = second[:, at + ff :]
    return w_qkv, w_att, w_in, w_out, small


def body(
    inputs,
    lengths,
    cotangent,
    w_qkv,
    b_qv,
    w_att,
    b_att,
    norm1_gain,
    norm1_bias,
    w_in,
    b_in,
    w_out,
    b_out,
    norm2_gain,
    norm2_bias,
):
    batch_size, seq_count, model_width = inputs.shape
    ff = w_in.shape[2]
    rows = w_qkv.shape[1]
    core = lax.axis_index("core")
    key_valid = lax.broadcasted_iota(jnp.int32, (batch_size, seq_count), 1) < lengths[:, None]
    hidden = inputs.astype(jnp.float32).reshape(-1, model_width)
    hidden_bf = inputs.reshape(-1, model_width)
    small = jnp.concatenate(
        [
            b_qv[0].T,
            b_att[0][:, None],
            norm1_gain[0][:, None],
            norm1_bias[0][:, None],
            b_out[0][:, None],
            norm2_gain[0][:, None],
            norm2_bias[0][:, None],
            b_in[0].reshape(rows, -1),
        ],
        axis=1,
    )
    first, second = pack_halves(w_qkv[0], w_att[0], w_in[0], w_out[0], small)
    mine = jnp.where(core == 0, first, second)
    gathered = lax.all_gather(mine, SHARD_AXES, axis=0, tiled=True)
    both = lax.all_gather(gathered, "core", axis=0, tiled=False)
    f_qkv, f_att, f_in, f_out, f_small = unpack_halves(both[0], both[1], model_width, ff)
    f_out = f_out.reshape(f_out.shape[0], -1, model_width)
    f_bqv = f_small[:, 0:2].T
    f_bin = f_small[:, 8:].reshape(ff)
    params = (
        f_qkv,
        f_bqv,
        f_att,
        f_small[:, 2],
        f_small[:, 3],
        f_small[:, 4],
        f_in,
        f_bin,
        f_out,
        f_small[:, 5],
        f_small[:, 6],
        f_small[:, 7],
    )
    hidden, stored = layer_forward(hidden, hidden_bf, params, key_valid, batch_size)
    outputs = hidden.astype(jnp.bfloat16).reshape(inputs.shape)
    upstream = cotangent.astype(jnp.float32).reshape(-1, model_width)
    upstream, terms = layer_backward(upstream, stored, params, key_valid)
    (g_qkv, g_bqv, g_att, g_batt, g_n1g, g_n1b, g_in, g_bin, g_out, g_bout, g_n2g, g_n2b) = terms
    g_small = jnp.concatenate(
        [
            g_bqv.T,
            g_batt[:, None],
            g_n1g[:, None],
            g_n1b[:, None],
            g_bout[:, None],
            g_n2g[:, None],
            g_n2b[:, None],
            g_bin.reshape(model_width, -1),
        ],
        axis=1,
    )
    tokens = g_qkv[0].shape[0]
    col = lambda b, c: b[:, c * model_width : (c + 1) * model_width]
    act_split = g_out[0].reshape(tokens, model_width, -1)
    hi = g_small.astype(jnp.bfloat16)
    rest = g_small - hi.astype(jnp.float32)
    mid_part = rest.astype(jnp.bfloat16)
    low = (rest - mid_part.astype(jnp.float32)).astype(jnp.bfloat16)
    n_small = g_small.shape[1]
    pieces = jnp.concatenate([hi.T, mid_part.T, low.T], axis=0)
    enc_left = jnp.zeros((tokens, model_width), jnp.bfloat16).at[: 3 * n_small].set(pieces)
    picks = lax.broadcasted_iota(jnp.int32, (tokens, model_width), 1) == (
        lax.broadcasted_iota(jnp.int32, (tokens, model_width), 0) % n_small
    )
    rows_used = lax.broadcasted_iota(jnp.int32, (tokens, model_width), 0) < 3 * n_small
    enc_right = (picks & rows_used).astype(jnp.bfloat16)
    zero = jnp.zeros((tokens, model_width), jnp.bfloat16)
    lefts = [g_qkv[0]] * 3 + [g_in[0]] * 3 + [zero]
    lefts += [g_att[0], g_in[0]] + [act_split[:, :, j] for j in range(4)] + [enc_left]
    rights = [col(g_qkv[1], c) for c in range(3)] + [col(g_in[1], c) for c in range(3)] + [zero]
    rights += [g_att[1], col(g_in[1], 3)] + [g_out[1]] * 4 + [enc_right]
    wgrads = jnp.einsum(
        "btk,btn->bkn",
        jnp.stack(lefts),
        jnp.stack(rights),
        preferred_element_type=jnp.float32,
    ).reshape(2, len(lefts) // 2, model_width, model_width)
    half = lax.psum_scatter(wgrads, "core", scatter_dimension=0, tiled=False)
    part = lax.psum_scatter(half, SHARD_AXES, scatter_dimension=1, tiled=True)
    part = lax.psum(part, "xh")
    res = lax.all_gather(part, "core", axis=0, tiled=False)
    r0, r1 = res[0], res[1]
    r_qkv = jnp.concatenate([r0[0], r0[1], r0[2]], axis=1)
    r_in = jnp.concatenate([r0[3], r0[4], r0[5], r1[1]], axis=1)
    r_att = r1[0]
    r_out = jnp.stack([r1[2], r1[3], r1[4], r1[5]], axis=1)
    r_small = r1[6][:, :n_small]
    grad_inputs = upstream.reshape(inputs.shape)
    return (
        outputs,
        grad_inputs,
        r_qkv[None],
        r_small[:, 0:2].T[None],
        r_att[None],
        r_small[:, 2][None],
        r_small[:, 3][None],
        r_small[:, 4][None],
        r_in[None],
        r_small[:, 8:].reshape(-1)[None],
        r_out.reshape(-1, model_width)[None],
        r_small[:, 5][None],
        r_small[:, 6][None],
        r_small[:, 7][None],
    )


def solution(mesh):
    devices = mesh.devices.reshape(2, 2, 4, 2, 4)
    fine = jax.sharding.Mesh(devices, ("xh", "core", "y", "xl", "z"))
    seqs = P(("xh", "core", "y", "xl", "z"), None, None)
    rows = P(None, SHARD_AXES, None)
    vec = P(None, SHARD_AXES)
    return jax.shard_map(
        body,
        mesh=fine,
        in_specs=(
            seqs,
            P(("xh", "core", "y", "xl", "z")),
            seqs,
            rows,
            P(None, None, SHARD_AXES),
            rows,
            vec,
            vec,
            vec,
            rows,
            vec,
            rows,
            vec,
            vec,
            vec,
        ),
        out_specs=(
            seqs,
            seqs,
            rows,
            P(None, None, SHARD_AXES),
            rows,
            vec,
            vec,
            vec,
            rows,
            vec,
            rows,
            vec,
            vec,
            vec,
        ),
        check_vma=False,
    )
```

```python
import math

import jax
import jax.numpy as jnp
from jax import lax
from jax.sharding import PartitionSpec as P

HEAD_DIM = 64
LAYERS = 1


EPS = 1e-12
ROOT_HALF = 0.7071067811865476
INV_ROOT_TWO_PI = 0.3989422804014327


def batched(form, left, right):
    return jnp.einsum(form, left, right, preferred_element_type=jnp.float32)


def layer_norm(residual, gain, shift):
    row_mean = jnp.mean(residual, axis=-1, keepdims=True)
    centered = residual - row_mean
    variance = jnp.mean(centered * centered, axis=-1, keepdims=True)
    inv_std = lax.rsqrt(variance + EPS)
    normed = centered * inv_std
    return (normed * gain.astype(jnp.float32) + shift.astype(jnp.float32), normed, inv_std)


def norm_backward(upstream, normed, inv_std, gain):
    grad_gain = jnp.sum(upstream * normed, axis=0)
    grad_shift = jnp.sum(upstream, axis=0)
    scaled = upstream * gain.astype(jnp.float32)
    grad_res = inv_std * (
        scaled
        - jnp.mean(scaled, axis=-1, keepdims=True)
        - normed * jnp.mean(scaled * normed, axis=-1, keepdims=True)
    )
    return (grad_res, grad_gain, grad_shift)


def attention_scores(query_bf, key_bf, key_valid):
    scores = batched("bqhe,bkhe->bhqk", query_bf, key_bf) * (1.0 / math.sqrt(HEAD_DIM))
    return jnp.where(key_valid[:, None, None, :], scores, -1e30)


def layer_forward(hidden, hidden_bf, params, key_valid, batch_size):
    (
        w_qkv,
        b_qv,
        w_att,
        b_att,
        gain_one,
        shift_one,
        w_in,
        b_in,
        w_out,
        b_out,
        gain_two,
        shift_two,
    ) = params
    model_width = hidden.shape[1]
    seq_count = hidden.shape[0] // batch_size
    shape_heads = (batch_size, seq_count, model_width // HEAD_DIM, HEAD_DIM)
    packed = jnp.dot(hidden_bf, w_qkv, preferred_element_type=jnp.float32)
    bias_qv = b_qv.astype(jnp.float32)
    query_bf = (packed[:, :model_width] + bias_qv[0]).astype(jnp.bfloat16).reshape(shape_heads)
    key_bf = packed[:, model_width : 2 * model_width].astype(jnp.bfloat16).reshape(shape_heads)
    value_bf = (packed[:, 2 * model_width :] + bias_qv[1]).astype(jnp.bfloat16).reshape(shape_heads)
    scores = attention_scores(query_bf, key_bf, key_valid)
    row_max = jnp.max(scores, axis=-1, keepdims=True)
    row_lse = row_max + jnp.log(jnp.sum(jnp.exp(scores - row_max), axis=-1, keepdims=True))
    probs_bf = jnp.exp(scores - row_lse).astype(jnp.bfloat16)
    context_bf = (
        batched("bhqk,bkhe->bqhe", probs_bf, value_bf).astype(jnp.bfloat16).reshape(-1, model_width)
    )
    first = (
        hidden
        + jnp.dot(context_bf, w_att, preferred_element_type=jnp.float32)
        + b_att.astype(jnp.float32)
    )
    middle, normed_one, inv_one = layer_norm(first, gain_one, shift_one)
    middle_bf = middle.astype(jnp.bfloat16)
    pre_act = jnp.dot(middle_bf, w_in, preferred_element_type=jnp.float32) + b_in.astype(
        jnp.float32
    )
    act_bf = (pre_act * 0.5 * (1.0 + jax.scipy.special.erf(pre_act * ROOT_HALF))).astype(
        jnp.bfloat16
    )
    second = (
        middle
        + jnp.einsum(
            "tkj,kjd->td",
            act_bf.reshape(act_bf.shape[0], -1, w_out.shape[1]),
            w_out,
            preferred_element_type=jnp.float32,
        )
        + b_out.astype(jnp.float32)
    )
    result, normed_two, inv_two = layer_norm(second, gain_two, shift_two)
    stored = (
        hidden_bf,
        query_bf,
        key_bf,
        value_bf,
        row_lse,
        context_bf,
        normed_one,
        inv_one,
        middle_bf,
        pre_act,
        act_bf,
        normed_two,
        inv_two,
    )
    return (result, stored)


def layer_backward(upstream, stored, params, key_valid):
    (
        w_qkv,
        b_qv,
        w_att,
        b_att,
        gain_one,
        shift_one,
        w_in,
        b_in,
        w_out,
        b_out,
        gain_two,
        shift_two,
    ) = params
    (
        hidden_bf,
        query_bf,
        key_bf,
        value_bf,
        row_lse,
        context_bf,
        normed_one,
        inv_one,
        middle_bf,
        pre_act,
        act_bf,
        normed_two,
        inv_two,
    ) = stored
    model_width = upstream.shape[1]
    shape_heads = query_bf.shape
    grad_second, grad_gain_two, grad_shift_two = norm_backward(
        upstream, normed_two, inv_two, gain_two
    )
    grad_b_out = jnp.sum(grad_second, axis=0)
    second_bf = grad_second.astype(jnp.bfloat16)
    back_act = jnp.einsum(
        "td,kjd->tkj", second_bf, w_out, preferred_element_type=jnp.float32
    ).reshape(second_bf.shape[0], -1)
    cumulative = 0.5 * (1.0 + jax.scipy.special.erf(pre_act * ROOT_HALF))
    density = jnp.exp(-0.5 * pre_act * pre_act) * INV_ROOT_TWO_PI
    grad_pre = back_act * (cumulative + pre_act * density)
    pre_bf = grad_pre.astype(jnp.bfloat16)
    grad_b_in = jnp.sum(grad_pre, axis=0)
    grad_middle = grad_second + jnp.dot(pre_bf, w_in.T, preferred_element_type=jnp.float32)
    grad_first, grad_gain_one, grad_shift_one = norm_backward(
        grad_middle, normed_one, inv_one, gain_one
    )
    grad_b_att = jnp.sum(grad_first, axis=0)
    first_bf = grad_first.astype(jnp.bfloat16)
    grad_context = (
        jnp.dot(first_bf, w_att.T, preferred_element_type=jnp.float32)
        .astype(jnp.bfloat16)
        .reshape(shape_heads)
    )
    scores = attention_scores(query_bf, key_bf, key_valid)
    probs = jnp.exp(scores - row_lse)
    grad_value = batched("bhqk,bqhe->bkhe", probs.astype(jnp.bfloat16), grad_context).reshape(
        -1, model_width
    )
    grad_probs = batched("bqhe,bkhe->bhqk", grad_context, value_bf)
    inner = jnp.sum(probs * grad_probs, axis=-1, keepdims=True)
    grad_scores = (probs * (grad_probs - inner) * (1.0 / math.sqrt(HEAD_DIM))).astype(jnp.bfloat16)
    grad_query = batched("bhqk,bkhe->bqhe", grad_scores, key_bf).reshape(-1, model_width)
    grad_key = batched("bhqk,bqhe->bkhe", grad_scores, query_bf).reshape(-1, model_width)
    grad_b_qv = jnp.stack([jnp.sum(grad_query, axis=0), jnp.sum(grad_value, axis=0)])
    packed_bf = jnp.concatenate([grad_query, grad_key, grad_value], axis=1).astype(jnp.bfloat16)
    grad_hidden = grad_first + jnp.dot(packed_bf, w_qkv.T, preferred_element_type=jnp.float32)
    terms = (
        (hidden_bf, packed_bf),
        grad_b_qv,
        (context_bf, first_bf),
        grad_b_att,
        grad_gain_one,
        grad_shift_one,
        (middle_bf, pre_bf),
        grad_b_in,
        (act_bf, second_bf),
        grad_b_out,
        grad_gain_two,
        grad_shift_two,
    )
    return (grad_hidden, terms)


SHARD_AXES = ("y", "xl", "z")
PAIR_AXES = ("xh", "core")


def pack_halves(w_qkv, w_att, w_in, w_out, small):
    rows = w_qkv.shape[0]
    split = w_qkv.shape[1]
    pad = jnp.zeros((rows, small.shape[1]), w_qkv.dtype)
    first = jnp.concatenate([w_qkv, w_in[:, :split], pad], axis=1)
    second = jnp.concatenate(
        [w_att, w_in[:, split:], w_out.reshape(rows, -1), small], axis=1
    )
    return first, second


def unpack_halves(first, second, width, ff):
    split = 3 * width
    w_qkv = first[:, :split]
    w_in = jnp.concatenate([first[:, split : 2 * split], second[:, width : width + ff - split]], axis=1)
    at = width + ff - split
    w_att = second[:, :width]
    w_out = second[:, at : at + ff]
    small = second[:, at + ff :]
    return w_qkv, w_att, w_in, w_out, small


def body(
    inputs,
    lengths,
    cotangent,
    w_qkv,
    b_qv,
    w_att,
    b_att,
    norm1_gain,
    norm1_bias,
    w_in,
    b_in,
    w_out,
    b_out,
    norm2_gain,
    norm2_bias,
):
    batch_size, seq_count, model_width = inputs.shape
    ff = w_in.shape[2]
    rows = w_qkv.shape[1]
    core = lax.axis_index("core")
    key_valid = lax.broadcasted_iota(jnp.int32, (batch_size, seq_count), 1) < lengths[:, None]
    hidden = inputs.astype(jnp.float32).reshape(-1, model_width)
    hidden_bf = inputs.reshape(-1, model_width)
    small = jnp.concatenate(
        [
            b_qv[0].T,
            b_att[0][:, None],
            norm1_gain[0][:, None],
            norm1_bias[0][:, None],
            b_out[0][:, None],
            norm2_gain[0][:, None],
            norm2_bias[0][:, None],
            b_in[0].reshape(rows, -1),
        ],
        axis=1,
    )
    first, second = pack_halves(w_qkv[0], w_att[0], w_in[0], w_out[0], small)
    mine = jnp.where(core == 0, first, second)
    gathered = lax.all_gather(mine, SHARD_AXES, axis=0, tiled=True)
    both = lax.all_gather(gathered, "core", axis=0, tiled=False)
    f_qkv, f_att, f_in, f_out, f_small = unpack_halves(both[0], both[1], model_width, ff)
    f_out = f_out.reshape(f_out.shape[0], -1, model_width)
    f_bqv = f_small[:, 0:2].T
    f_bin = f_small[:, 8:].reshape(ff)
    params = (
        f_qkv,
        f_bqv,
        f_att,
        f_small[:, 2],
        f_small[:, 3],
        f_small[:, 4],
        f_in,
        f_bin,
        f_out,
        f_small[:, 5],
        f_small[:, 6],
        f_small[:, 7],
    )
    hidden, stored = layer_forward(hidden, hidden_bf, params, key_valid, batch_size)
    outputs = hidden.astype(jnp.bfloat16).reshape(inputs.shape)
    upstream = cotangent.astype(jnp.float32).reshape(-1, model_width)
    upstream, terms = layer_backward(upstream, stored, params, key_valid)
    (g_qkv, g_bqv, g_att, g_batt, g_n1g, g_n1b, g_in, g_bin, g_out, g_bout, g_n2g, g_n2b) = terms
    g_small = jnp.concatenate(
        [
            g_bqv.T,
            g_batt[:, None],
            g_n1g[:, None],
            g_n1b[:, None],
            g_bout[:, None],
            g_n2g[:, None],
            g_n2b[:, None],
            g_bin.reshape(model_width, -1),
        ],
        axis=1,
    )
    tokens = g_qkv[0].shape[0]
    col = lambda b, c: b[:, c * model_width : (c + 1) * model_width]
    act_split = g_out[0].reshape(tokens, model_width, -1)
    hi = g_small.astype(jnp.bfloat16)
    rest = g_small - hi.astype(jnp.float32)
    mid_part = rest.astype(jnp.bfloat16)
    low = (rest - mid_part.astype(jnp.float32)).astype(jnp.bfloat16)
    n_small = g_small.shape[1]
    pieces = jnp.concatenate([hi.T, mid_part.T, low.T], axis=0)
    enc_left = jnp.zeros((tokens, model_width), jnp.bfloat16).at[: 3 * n_small].set(pieces)
    picks = lax.broadcasted_iota(jnp.int32, (tokens, model_width), 1) == (
        lax.broadcasted_iota(jnp.int32, (tokens, model_width), 0) % n_small
    )
    rows_used = lax.broadcasted_iota(jnp.int32, (tokens, model_width), 0) < 3 * n_small
    enc_right = (picks & rows_used).astype(jnp.bfloat16)
    zero = jnp.zeros((tokens, model_width), jnp.bfloat16)
    lefts = [g_qkv[0]] * 3 + [g_in[0]] * 3 + [zero]
    lefts += [g_att[0], g_in[0]] + [act_split[:, :, j] for j in range(4)] + [enc_left]
    rights = [col(g_qkv[1], c) for c in range(3)] + [col(g_in[1], c) for c in range(3)] + [zero]
    rights += [g_att[1], col(g_in[1], 3)] + [g_out[1]] * 4 + [enc_right]
    wgrads = jnp.einsum(
        "btk,btn->bkn",
        jnp.stack(lefts),
        jnp.stack(rights),
        preferred_element_type=jnp.float32,
    ).reshape(2, len(lefts) // 2, model_width, model_width)
    half = lax.psum_scatter(wgrads, "core", scatter_dimension=0, tiled=False)
    part = lax.psum_scatter(
        half.astype(jnp.bfloat16), SHARD_AXES, scatter_dimension=1, tiled=True
    )
    part = lax.psum(part.astype(jnp.float32), "xh")
    res = lax.all_gather(part, "core", axis=0, tiled=False)
    r0, r1 = res[0], res[1]
    r_qkv = jnp.concatenate([r0[0], r0[1], r0[2]], axis=1)
    r_in = jnp.concatenate([r0[3], r0[4], r0[5], r1[1]], axis=1)
    r_att = r1[0]
    r_out = jnp.stack([r1[2], r1[3], r1[4], r1[5]], axis=1)
    r_small = r1[6][:, :n_small]
    grad_inputs = upstream.reshape(inputs.shape)
    return (
        outputs,
        grad_inputs,
        r_qkv[None],
        r_small[:, 0:2].T[None],
        r_att[None],
        r_small[:, 2][None],
        r_small[:, 3][None],
        r_small[:, 4][None],
        r_in[None],
        r_small[:, 8:].reshape(-1)[None],
        r_out.reshape(-1, model_width)[None],
        r_small[:, 5][None],
        r_small[:, 6][None],
        r_small[:, 7][None],
    )


def solution(mesh):
    devices = mesh.devices.reshape(2, 2, 4, 2, 4)
    fine = jax.sharding.Mesh(devices, ("xh", "core", "y", "xl", "z"))
    seqs = P(("xh", "core", "y", "xl", "z"), None, None)
    rows = P(None, SHARD_AXES, None)
    vec = P(None, SHARD_AXES)
    return jax.shard_map(
        body,
        mesh=fine,
        in_specs=(
            seqs,
            P(("xh", "core", "y", "xl", "z")),
            seqs,
            rows,
            P(None, None, SHARD_AXES),
            rows,
            vec,
            vec,
            vec,
            rows,
            vec,
            rows,
            vec,
            vec,
            vec,
        ),
        out_specs=(
            seqs,
            seqs,
            rows,
            P(None, None, SHARD_AXES),
            rows,
            vec,
            vec,
            vec,
            rows,
            vec,
            rows,
            vec,
            vec,
            vec,
        ),
        check_vma=False,
    )
```

```python
import math

import jax
import jax.numpy as jnp
from jax import lax
from jax.experimental import pallas as pl
from jax.experimental.pallas import tpu as pltpu
from jax.sharding import PartitionSpec as P

HEAD_DIM = 64
LAYERS = 1


EPS = 1e-12
ROOT_HALF = 0.7071067811865476
INV_ROOT_TWO_PI = 0.3989422804014327


def _ffn_out_kernel(act_ref, w_ref, out_ref):
    @pl.when(pl.program_id(0) == 0)
    def _():
        out_ref[...] = jnp.zeros_like(out_ref)

    out_ref[...] += jnp.dot(act_ref[...], w_ref[...], preferred_element_type=jnp.float32)


def ffn_out(act_grouped, w_out):
    buffer, first_block = w_out
    tokens = act_grouped.shape[0]
    width = buffer.shape[0]
    groups = act_grouped.shape[1] // width
    return pl.pallas_call(
        _ffn_out_kernel,
        grid=(groups,),
        in_specs=[
            pl.BlockSpec((tokens, width), lambda j: (0, j)),
            pl.BlockSpec((width, width), lambda j: (0, first_block + j)),
        ],
        out_specs=pl.BlockSpec((tokens, width), lambda j: (0, 0)),
        out_shape=jax.ShapeDtypeStruct((tokens, width), jnp.float32),
        cost_estimate=pl.CostEstimate(
            flops=2 * tokens * width * width * groups,
            bytes_accessed=2 * width * width * groups + 2 * tokens * width * groups + 4 * tokens * width,
            transcendentals=0,
        ),
    )(act_grouped, buffer)


def _ffn_out_back_kernel(grad_ref, w_ref, out_ref):
    out_ref[...] = lax.dot_general(
        grad_ref[...],
        w_ref[...],
        (((1,), (1,)), ((), ())),
        preferred_element_type=jnp.float32,
    )


def ffn_out_back(grad_bf, w_out):
    buffer, first_block = w_out
    tokens = grad_bf.shape[0]
    width = buffer.shape[0]
    groups = 4
    return pl.pallas_call(
        _ffn_out_back_kernel,
        grid=(groups,),
        in_specs=[
            pl.BlockSpec((tokens, width), lambda j: (0, 0)),
            pl.BlockSpec((width, width), lambda j: (0, first_block + j)),
        ],
        out_specs=pl.BlockSpec((tokens, width), lambda j: (0, j)),
        out_shape=jax.ShapeDtypeStruct((tokens, width * groups), jnp.float32),
        cost_estimate=pl.CostEstimate(
            flops=2 * tokens * width * width * groups,
            bytes_accessed=2 * width * width * groups + 2 * tokens * width + 4 * tokens * width * groups,
            transcendentals=0,
        ),
    )(grad_bf, buffer)


def group_columns(x, groups):
    tokens = x.shape[0]
    return x.reshape(tokens, -1, groups).transpose(0, 2, 1).reshape(tokens, -1)


def ungroup_columns(x, groups):
    tokens = x.shape[0]
    return x.reshape(tokens, groups, -1).transpose(0, 2, 1).reshape(tokens, -1)


def batched(form, left, right):
    return jnp.einsum(form, left, right, preferred_element_type=jnp.float32)


def layer_norm(residual, gain, shift):
    row_mean = jnp.mean(residual, axis=-1, keepdims=True)
    centered = residual - row_mean
    variance = jnp.mean(centered * centered, axis=-1, keepdims=True)
    inv_std = lax.rsqrt(variance + EPS)
    normed = centered * inv_std
    return (normed * gain.astype(jnp.float32) + shift.astype(jnp.float32), normed, inv_std)


def norm_backward(upstream, normed, inv_std, gain):
    grad_gain = jnp.sum(upstream * normed, axis=0)
    grad_shift = jnp.sum(upstream, axis=0)
    scaled = upstream * gain.astype(jnp.float32)
    grad_res = inv_std * (
        scaled
        - jnp.mean(scaled, axis=-1, keepdims=True)
        - normed * jnp.mean(scaled * normed, axis=-1, keepdims=True)
    )
    return (grad_res, grad_gain, grad_shift)


def attention_scores(query_bf, key_bf, key_valid):
    scores = batched("bqhe,bkhe->bhqk", query_bf, key_bf) * (1.0 / math.sqrt(HEAD_DIM))
    return jnp.where(key_valid[:, None, None, :], scores, -1e30)


def layer_forward(hidden, hidden_bf, params, key_valid, batch_size):
    (
        w_qkv,
        b_qv,
        w_att,
        b_att,
        gain_one,
        shift_one,
        w_in,
        b_in,
        w_out,
        b_out,
        gain_two,
        shift_two,
    ) = params
    model_width = hidden.shape[1]
    seq_count = hidden.shape[0] // batch_size
    shape_heads = (batch_size, seq_count, model_width // HEAD_DIM, HEAD_DIM)
    packed = jnp.dot(hidden_bf, w_qkv, preferred_element_type=jnp.float32)
    bias_qv = b_qv.astype(jnp.float32)
    query_bf = (packed[:, :model_width] + bias_qv[0]).astype(jnp.bfloat16).reshape(shape_heads)
    key_bf = packed[:, model_width : 2 * model_width].astype(jnp.bfloat16).reshape(shape_heads)
    value_bf = (packed[:, 2 * model_width :] + bias_qv[1]).astype(jnp.bfloat16).reshape(shape_heads)
    scores = attention_scores(query_bf, key_bf, key_valid)
    row_max = jnp.max(scores, axis=-1, keepdims=True)
    row_lse = row_max + jnp.log(jnp.sum(jnp.exp(scores - row_max), axis=-1, keepdims=True))
    probs_bf = jnp.exp(scores - row_lse).astype(jnp.bfloat16)
    context_bf = (
        batched("bhqk,bkhe->bqhe", probs_bf, value_bf).astype(jnp.bfloat16).reshape(-1, model_width)
    )
    first = (
        hidden
        + jnp.dot(context_bf, w_att, preferred_element_type=jnp.float32)
        + b_att.astype(jnp.float32)
    )
    middle, normed_one, inv_one = layer_norm(first, gain_one, shift_one)
    middle_bf = middle.astype(jnp.bfloat16)
    pre_act = jnp.dot(middle_bf, w_in, preferred_element_type=jnp.float32) + b_in.astype(
        jnp.float32
    )
    act_bf = (pre_act * 0.5 * (1.0 + jax.scipy.special.erf(pre_act * ROOT_HALF))).astype(
        jnp.bfloat16
    )
    second = (
        middle
        + ffn_out(group_columns(act_bf, 4), w_out)
        + b_out.astype(jnp.float32)
    )
    result, normed_two, inv_two = layer_norm(second, gain_two, shift_two)
    stored = (
        hidden_bf,
        query_bf,
        key_bf,
        value_bf,
        row_lse,
        context_bf,
        normed_one,
        inv_one,
        middle_bf,
        pre_act,
        act_bf,
        normed_two,
        inv_two,
    )
    return (result, stored)


def layer_backward(upstream, stored, params, key_valid):
    (
        w_qkv,
        b_qv,
        w_att,
        b_att,
        gain_one,
        shift_one,
        w_in,
        b_in,
        w_out,
        b_out,
        gain_two,
        shift_two,
    ) = params
    (
        hidden_bf,
        query_bf,
        key_bf,
        value_bf,
        row_lse,
        context_bf,
        normed_one,
        inv_one,
        middle_bf,
        pre_act,
        act_bf,
        normed_two,
        inv_two,
    ) = stored
    model_width = upstream.shape[1]
    shape_heads = query_bf.shape
    grad_second, grad_gain_two, grad_shift_two = norm_backward(
        upstream, normed_two, inv_two, gain_two
    )
    grad_b_out = jnp.sum(grad_second, axis=0)
    second_bf = grad_second.astype(jnp.bfloat16)
    back_act = ungroup_columns(ffn_out_back(second_bf, w_out), 4)
    cumulative = 0.5 * (1.0 + jax.scipy.special.erf(pre_act * ROOT_HALF))
    density = jnp.exp(-0.5 * pre_act * pre_act) * INV_ROOT_TWO_PI
    grad_pre = back_act * (cumulative + pre_act * density)
    pre_bf = grad_pre.astype(jnp.bfloat16)
    grad_b_in = jnp.sum(grad_pre, axis=0)
    grad_middle = grad_second + jnp.dot(pre_bf, w_in.T, preferred_element_type=jnp.float32)
    grad_first, grad_gain_one, grad_shift_one = norm_backward(
        grad_middle, normed_one, inv_one, gain_one
    )
    grad_b_att = jnp.sum(grad_first, axis=0)
    first_bf = grad_first.astype(jnp.bfloat16)
    grad_context = (
        jnp.dot(first_bf, w_att.T, preferred_element_type=jnp.float32)
        .astype(jnp.bfloat16)
        .reshape(shape_heads)
    )
    scores = attention_scores(query_bf, key_bf, key_valid)
    probs = jnp.exp(scores - row_lse)
    grad_value = batched("bhqk,bqhe->bkhe", probs.astype(jnp.bfloat16), grad_context).reshape(
        -1, model_width
    )
    grad_probs = batched("bqhe,bkhe->bhqk", grad_context, value_bf)
    inner = jnp.sum(probs * grad_probs, axis=-1, keepdims=True)
    grad_scores = (probs * (grad_probs - inner) * (1.0 / math.sqrt(HEAD_DIM))).astype(jnp.bfloat16)
    grad_query = batched("bhqk,bkhe->bqhe", grad_scores, key_bf).reshape(-1, model_width)
    grad_key = batched("bhqk,bqhe->bkhe", grad_scores, query_bf).reshape(-1, model_width)
    grad_b_qv = jnp.stack([jnp.sum(grad_query, axis=0), jnp.sum(grad_value, axis=0)])
    packed_bf = jnp.concatenate([grad_query, grad_key, grad_value], axis=1).astype(jnp.bfloat16)
    grad_hidden = grad_first + jnp.dot(packed_bf, w_qkv.T, preferred_element_type=jnp.float32)
    terms = (
        (hidden_bf, packed_bf),
        grad_b_qv,
        (context_bf, first_bf),
        grad_b_att,
        grad_gain_one,
        grad_shift_one,
        (middle_bf, pre_bf),
        grad_b_in,
        (act_bf, second_bf),
        grad_b_out,
        grad_gain_two,
        grad_shift_two,
    )
    return (grad_hidden, terms)


SHARD_AXES = ("y", "xl", "z")
PAIR_AXES = ("xh", "core")


def pack_halves(w_qkv, w_att, w_in, w_out, small):
    rows = w_qkv.shape[0]
    split = w_qkv.shape[1]
    pad = jnp.zeros((rows, small.shape[1]), w_qkv.dtype)
    first = jnp.concatenate([w_qkv, w_in[:, :split], pad], axis=1)
    second = jnp.concatenate(
        [w_att, w_in[:, split:], w_out.reshape(rows, -1), small], axis=1
    )
    return first, second


def unpack_halves(first, second, width, ff):
    split = 3 * width
    w_qkv = first[:, :split]
    w_in = jnp.concatenate([first[:, split : 2 * split], second[:, width : width + ff - split]], axis=1)
    at = width + ff - split
    w_att = second[:, :width]
    w_out = second[:, at : at + ff]
    small = second[:, at + ff :]
    return w_qkv, w_att, w_in, w_out, small


def body(
    inputs,
    lengths,
    cotangent,
    w_qkv,
    b_qv,
    w_att,
    b_att,
    norm1_gain,
    norm1_bias,
    w_in,
    b_in,
    w_out,
    b_out,
    norm2_gain,
    norm2_bias,
):
    batch_size, seq_count, model_width = inputs.shape
    ff = w_in.shape[2]
    rows = w_qkv.shape[1]
    core = lax.axis_index("core")
    key_valid = lax.broadcasted_iota(jnp.int32, (batch_size, seq_count), 1) < lengths[:, None]
    hidden = inputs.astype(jnp.float32).reshape(-1, model_width)
    hidden_bf = inputs.reshape(-1, model_width)
    small = jnp.concatenate(
        [
            b_qv[0].T,
            b_att[0][:, None],
            norm1_gain[0][:, None],
            norm1_bias[0][:, None],
            b_out[0][:, None],
            norm2_gain[0][:, None],
            norm2_bias[0][:, None],
            b_in[0].reshape(rows, -1),
        ],
        axis=1,
    )
    first, second = pack_halves(w_qkv[0], w_att[0], w_in[0], w_out[0], small)
    mine = jnp.where(core == 0, first, second)
    gathered = lax.all_gather(mine, SHARD_AXES, axis=0, tiled=True)
    both = lax.all_gather(gathered, "core", axis=0, tiled=False)
    f_qkv, f_att, f_in, f_out, f_small = unpack_halves(both[0], both[1], model_width, ff)
    f_out = (both[1], (model_width + ff - 3 * model_width) // model_width)
    f_bqv = f_small[:, 0:2].T
    f_bin = f_small[:, 8:].reshape(ff)
    params = (
        f_qkv,
        f_bqv,
        f_att,
        f_small[:, 2],
        f_small[:, 3],
        f_small[:, 4],
        f_in,
        f_bin,
        f_out,
        f_small[:, 5],
        f_small[:, 6],
        f_small[:, 7],
    )
    hidden, stored = layer_forward(hidden, hidden_bf, params, key_valid, batch_size)
    outputs = hidden.astype(jnp.bfloat16).reshape(inputs.shape)
    upstream = cotangent.astype(jnp.float32).reshape(-1, model_width)
    upstream, terms = layer_backward(upstream, stored, params, key_valid)
    (g_qkv, g_bqv, g_att, g_batt, g_n1g, g_n1b, g_in, g_bin, g_out, g_bout, g_n2g, g_n2b) = terms
    g_small = jnp.concatenate(
        [
            g_bqv.T,
            g_batt[:, None],
            g_n1g[:, None],
            g_n1b[:, None],
            g_bout[:, None],
            g_n2g[:, None],
            g_n2b[:, None],
            g_bin.reshape(model_width, -1),
        ],
        axis=1,
    )
    tokens = g_qkv[0].shape[0]
    col = lambda b, c: b[:, c * model_width : (c + 1) * model_width]
    act_split = g_out[0].reshape(tokens, model_width, -1)
    hi = g_small.astype(jnp.bfloat16)
    rest = g_small - hi.astype(jnp.float32)
    mid_part = rest.astype(jnp.bfloat16)
    low = (rest - mid_part.astype(jnp.float32)).astype(jnp.bfloat16)
    n_small = g_small.shape[1]
    pieces = jnp.concatenate([hi.T, mid_part.T, low.T], axis=0)
    enc_left = jnp.zeros((tokens, model_width), jnp.bfloat16).at[: 3 * n_small].set(pieces)
    picks = lax.broadcasted_iota(jnp.int32, (tokens, model_width), 1) == (
        lax.broadcasted_iota(jnp.int32, (tokens, model_width), 0) % n_small
    )
    rows_used = lax.broadcasted_iota(jnp.int32, (tokens, model_width), 0) < 3 * n_small
    enc_right = (picks & rows_used).astype(jnp.bfloat16)
    zero = jnp.zeros((tokens, model_width), jnp.bfloat16)
    lefts = [g_qkv[0]] * 3 + [g_in[0]] * 3 + [zero]
    lefts += [g_att[0], g_in[0]] + [act_split[:, :, j] for j in range(4)] + [enc_left]
    rights = [col(g_qkv[1], c) for c in range(3)] + [col(g_in[1], c) for c in range(3)] + [zero]
    rights += [g_att[1], col(g_in[1], 3)] + [g_out[1]] * 4 + [enc_right]
    wgrads = jnp.einsum(
        "btk,btn->bkn",
        jnp.stack(lefts),
        jnp.stack(rights),
        preferred_element_type=jnp.float32,
    ).reshape(2, len(lefts) // 2, model_width, model_width)
    half = lax.psum_scatter(wgrads, "core", scatter_dimension=0, tiled=False)
    part = lax.psum_scatter(half, SHARD_AXES, scatter_dimension=1, tiled=True)
    part = lax.psum(part, "xh")
    res = lax.all_gather(part, "core", axis=0, tiled=False)
    r0, r1 = res[0], res[1]
    r_qkv = jnp.concatenate([r0[0], r0[1], r0[2]], axis=1)
    r_in = jnp.concatenate([r0[3], r0[4], r0[5], r1[1]], axis=1)
    r_att = r1[0]
    r_out = jnp.stack([r1[2], r1[3], r1[4], r1[5]], axis=1)
    r_small = r1[6][:, :n_small]
    grad_inputs = upstream.reshape(inputs.shape)
    return (
        outputs,
        grad_inputs,
        r_qkv[None],
        r_small[:, 0:2].T[None],
        r_att[None],
        r_small[:, 2][None],
        r_small[:, 3][None],
        r_small[:, 4][None],
        r_in[None],
        r_small[:, 8:].reshape(-1)[None],
        r_out.reshape(-1, model_width)[None],
        r_small[:, 5][None],
        r_small[:, 6][None],
        r_small[:, 7][None],
    )


def solution(mesh):
    devices = mesh.devices.reshape(2, 2, 4, 2, 4)
    fine = jax.sharding.Mesh(devices, ("xh", "core", "y", "xl", "z"))
    seqs = P(("xh", "core", "y", "xl", "z"), None, None)
    rows = P(None, SHARD_AXES, None)
    vec = P(None, SHARD_AXES)
    return jax.shard_map(
        body,
        mesh=fine,
        in_specs=(
            seqs,
            P(("xh", "core", "y", "xl", "z")),
            seqs,
            rows,
            P(None, None, SHARD_AXES),
            rows,
            vec,
            vec,
            vec,
            rows,
            vec,
            rows,
            vec,
            vec,
            vec,
        ),
        out_specs=(
            seqs,
            seqs,
            rows,
            P(None, None, SHARD_AXES),
            rows,
            vec,
            vec,
            vec,
            rows,
            vec,
            rows,
            vec,
            vec,
            vec,
        ),
        check_vma=False,
    )
```

```python
import math

import jax
import jax.numpy as jnp
from jax import lax
from jax.experimental import pallas as pl
from jax.experimental.pallas import tpu as pltpu
from jax.sharding import PartitionSpec as P

HEAD_DIM = 64
LAYERS = 1


EPS = 1e-12
ROOT_HALF = 0.7071067811865476
INV_ROOT_TWO_PI = 0.3989422804014327


def _ffn_out_kernel(act_ref, w_ref, out_ref):
    @pl.when(pl.program_id(0) == 0)
    def _():
        out_ref[...] = jnp.zeros_like(out_ref)

    out_ref[...] += jnp.dot(act_ref[...], w_ref[...], preferred_element_type=jnp.float32)


def ffn_out(act_grouped, w_out):
    buffer, which, first_block = w_out
    tokens = act_grouped.shape[0]
    width = buffer.shape[1]
    groups = act_grouped.shape[1] // width
    return pl.pallas_call(
        _ffn_out_kernel,
        grid=(groups,),
        in_specs=[
            pl.BlockSpec((tokens, width), lambda j: (0, j)),
            pl.BlockSpec((None, width, width), lambda j: (which, 0, first_block + j)),
        ],
        out_specs=pl.BlockSpec((tokens, width), lambda j: (0, 0)),
        out_shape=jax.ShapeDtypeStruct((tokens, width), jnp.float32),
        cost_estimate=pl.CostEstimate(
            flops=2 * tokens * width * width * groups,
            bytes_accessed=2 * width * width * groups + 2 * tokens * width * groups + 4 * tokens * width,
            transcendentals=0,
        ),
    )(act_grouped, buffer)


def _ffn_out_back_kernel(grad_ref, w_ref, out_ref):
    out_ref[...] = lax.dot_general(
        grad_ref[...],
        w_ref[...],
        (((1,), (1,)), ((), ())),
        preferred_element_type=jnp.float32,
    )


def ffn_out_back(grad_bf, w_out):
    buffer, which, first_block = w_out
    tokens = grad_bf.shape[0]
    width = buffer.shape[1]
    groups = 4
    return pl.pallas_call(
        _ffn_out_back_kernel,
        grid=(groups,),
        in_specs=[
            pl.BlockSpec((tokens, width), lambda j: (0, 0)),
            pl.BlockSpec((None, width, width), lambda j: (which, 0, first_block + j)),
        ],
        out_specs=pl.BlockSpec((tokens, width), lambda j: (0, j)),
        out_shape=jax.ShapeDtypeStruct((tokens, width * groups), jnp.float32),
        cost_estimate=pl.CostEstimate(
            flops=2 * tokens * width * width * groups,
            bytes_accessed=2 * width * width * groups + 2 * tokens * width + 4 * tokens * width * groups,
            transcendentals=0,
        ),
    )(grad_bf, buffer)


def group_columns(x, groups):
    tokens = x.shape[0]
    return x.reshape(tokens, -1, groups).transpose(0, 2, 1).reshape(tokens, -1)


def ungroup_columns(x, groups):
    tokens = x.shape[0]
    return x.reshape(tokens, groups, -1).transpose(0, 2, 1).reshape(tokens, -1)


def batched(form, left, right):
    return jnp.einsum(form, left, right, preferred_element_type=jnp.float32)


def layer_norm(residual, gain, shift):
    row_mean = jnp.mean(residual, axis=-1, keepdims=True)
    centered = residual - row_mean
    variance = jnp.mean(centered * centered, axis=-1, keepdims=True)
    inv_std = lax.rsqrt(variance + EPS)
    normed = centered * inv_std
    return (normed * gain.astype(jnp.float32) + shift.astype(jnp.float32), normed, inv_std)


def norm_backward(upstream, normed, inv_std, gain):
    grad_gain = jnp.sum(upstream * normed, axis=0)
    grad_shift = jnp.sum(upstream, axis=0)
    scaled = upstream * gain.astype(jnp.float32)
    grad_res = inv_std * (
        scaled
        - jnp.mean(scaled, axis=-1, keepdims=True)
        - normed * jnp.mean(scaled * normed, axis=-1, keepdims=True)
    )
    return (grad_res, grad_gain, grad_shift)


def attention_scores(query_bf, key_bf, key_valid):
    scores = batched("bqhe,bkhe->bhqk", query_bf, key_bf) * (1.0 / math.sqrt(HEAD_DIM))
    return jnp.where(key_valid[:, None, None, :], scores, -1e30)


def layer_forward(hidden, hidden_bf, params, key_valid, batch_size):
    (
        w_qkv,
        b_qv,
        w_att,
        b_att,
        gain_one,
        shift_one,
        w_in,
        b_in,
        w_out,
        b_out,
        gain_two,
        shift_two,
    ) = params
    model_width = hidden.shape[1]
    seq_count = hidden.shape[0] // batch_size
    shape_heads = (batch_size, seq_count, model_width // HEAD_DIM, HEAD_DIM)
    packed = jnp.dot(hidden_bf, w_qkv, preferred_element_type=jnp.float32)
    bias_qv = b_qv.astype(jnp.float32)
    query_bf = (packed[:, :model_width] + bias_qv[0]).astype(jnp.bfloat16).reshape(shape_heads)
    key_bf = packed[:, model_width : 2 * model_width].astype(jnp.bfloat16).reshape(shape_heads)
    value_bf = (packed[:, 2 * model_width :] + bias_qv[1]).astype(jnp.bfloat16).reshape(shape_heads)
    scores = attention_scores(query_bf, key_bf, key_valid)
    row_max = jnp.max(scores, axis=-1, keepdims=True)
    row_lse = row_max + jnp.log(jnp.sum(jnp.exp(scores - row_max), axis=-1, keepdims=True))
    probs_bf = jnp.exp(scores - row_lse).astype(jnp.bfloat16)
    context_bf = (
        batched("bhqk,bkhe->bqhe", probs_bf, value_bf).astype(jnp.bfloat16).reshape(-1, model_width)
    )
    first = (
        hidden
        + jnp.dot(context_bf, w_att, preferred_element_type=jnp.float32)
        + b_att.astype(jnp.float32)
    )
    middle, normed_one, inv_one = layer_norm(first, gain_one, shift_one)
    middle_bf = middle.astype(jnp.bfloat16)
    pre_act = jnp.dot(middle_bf, w_in, preferred_element_type=jnp.float32) + b_in.astype(
        jnp.float32
    )
    act_bf = (pre_act * 0.5 * (1.0 + jax.scipy.special.erf(pre_act * ROOT_HALF))).astype(
        jnp.bfloat16
    )
    second = (
        middle
        + ffn_out(act_bf, w_out)
        + b_out.astype(jnp.float32)
    )
    result, normed_two, inv_two = layer_norm(second, gain_two, shift_two)
    stored = (
        hidden_bf,
        query_bf,
        key_bf,
        value_bf,
        row_lse,
        context_bf,
        normed_one,
        inv_one,
        middle_bf,
        pre_act,
        act_bf,
        normed_two,
        inv_two,
    )
    return (result, stored)


def layer_backward(upstream, stored, params, key_valid):
    (
        w_qkv,
        b_qv,
        w_att,
        b_att,
        gain_one,
        shift_one,
        w_in,
        b_in,
        w_out,
        b_out,
        gain_two,
        shift_two,
    ) = params
    (
        hidden_bf,
        query_bf,
        key_bf,
        value_bf,
        row_lse,
        context_bf,
        normed_one,
        inv_one,
        middle_bf,
        pre_act,
        act_bf,
        normed_two,
        inv_two,
    ) = stored
    model_width = upstream.shape[1]
    shape_heads = query_bf.shape
    grad_second, grad_gain_two, grad_shift_two = norm_backward(
        upstream, normed_two, inv_two, gain_two
    )
    grad_b_out = jnp.sum(grad_second, axis=0)
    second_bf = grad_second.astype(jnp.bfloat16)
    back_act = ffn_out_back(second_bf, w_out)
    cumulative = 0.5 * (1.0 + jax.scipy.special.erf(pre_act * ROOT_HALF))
    density = jnp.exp(-0.5 * pre_act * pre_act) * INV_ROOT_TWO_PI
    grad_pre = back_act * (cumulative + pre_act * density)
    pre_bf = grad_pre.astype(jnp.bfloat16)
    grad_b_in = jnp.sum(grad_pre, axis=0)
    grad_middle = grad_second + jnp.dot(pre_bf, w_in.T, preferred_element_type=jnp.float32)
    grad_first, grad_gain_one, grad_shift_one = norm_backward(
        grad_middle, normed_one, inv_one, gain_one
    )
    grad_b_att = jnp.sum(grad_first, axis=0)
    first_bf = grad_first.astype(jnp.bfloat16)
    grad_context = (
        jnp.dot(first_bf, w_att.T, preferred_element_type=jnp.float32)
        .astype(jnp.bfloat16)
        .reshape(shape_heads)
    )
    scores = attention_scores(query_bf, key_bf, key_valid)
    probs = jnp.exp(scores - row_lse)
    grad_value = batched("bhqk,bqhe->bkhe", probs.astype(jnp.bfloat16), grad_context).reshape(
        -1, model_width
    )
    grad_probs = batched("bqhe,bkhe->bhqk", grad_context, value_bf)
    inner = jnp.sum(probs * grad_probs, axis=-1, keepdims=True)
    grad_scores = (probs * (grad_probs - inner) * (1.0 / math.sqrt(HEAD_DIM))).astype(jnp.bfloat16)
    grad_query = batched("bhqk,bkhe->bqhe", grad_scores, key_bf).reshape(-1, model_width)
    grad_key = batched("bhqk,bqhe->bkhe", grad_scores, query_bf).reshape(-1, model_width)
    grad_b_qv = jnp.stack([jnp.sum(grad_query, axis=0), jnp.sum(grad_value, axis=0)])
    packed_bf = jnp.concatenate([grad_query, grad_key, grad_value], axis=1).astype(jnp.bfloat16)
    grad_hidden = grad_first + jnp.dot(packed_bf, w_qkv.T, preferred_element_type=jnp.float32)
    terms = (
        (hidden_bf, packed_bf),
        grad_b_qv,
        (context_bf, first_bf),
        grad_b_att,
        grad_gain_one,
        grad_shift_one,
        (middle_bf, pre_bf),
        grad_b_in,
        (act_bf, second_bf),
        grad_b_out,
        grad_gain_two,
        grad_shift_two,
    )
    return (grad_hidden, terms)


SHARD_AXES = ("y", "xl", "z")
PAIR_AXES = ("xh", "core")


def pack_halves(w_qkv, w_att, w_in, w_out, small):
    rows = w_qkv.shape[0]
    split = w_qkv.shape[1]
    pad = jnp.zeros((rows, small.shape[1]), w_qkv.dtype)
    first = jnp.concatenate([w_qkv, w_in[:, :split], pad], axis=1)
    second = jnp.concatenate(
        [w_att, w_in[:, split:], w_out.reshape(rows, -1), small], axis=1
    )
    return first, second


def unpack_halves(first, second, width, ff):
    split = 3 * width
    w_qkv = first[:, :split]
    w_in = jnp.concatenate([first[:, split : 2 * split], second[:, width : width + ff - split]], axis=1)
    at = width + ff - split
    w_att = second[:, :width]
    w_out = second[:, at : at + ff]
    small = second[:, at + ff :]
    return w_qkv, w_att, w_in, w_out, small


def body(
    inputs,
    lengths,
    cotangent,
    w_qkv,
    b_qv,
    w_att,
    b_att,
    norm1_gain,
    norm1_bias,
    w_in,
    b_in,
    w_out,
    b_out,
    norm2_gain,
    norm2_bias,
):
    batch_size, seq_count, model_width = inputs.shape
    ff = w_in.shape[2]
    rows = w_qkv.shape[1]
    core = lax.axis_index("core")
    key_valid = lax.broadcasted_iota(jnp.int32, (batch_size, seq_count), 1) < lengths[:, None]
    hidden = inputs.astype(jnp.float32).reshape(-1, model_width)
    hidden_bf = inputs.reshape(-1, model_width)
    small = jnp.concatenate(
        [
            b_qv[0].T,
            b_att[0][:, None],
            norm1_gain[0][:, None],
            norm1_bias[0][:, None],
            b_out[0][:, None],
            norm2_gain[0][:, None],
            norm2_bias[0][:, None],
            b_in[0].reshape(rows, -1),
        ],
        axis=1,
    )
    first, second = pack_halves(w_qkv[0], w_att[0], group_columns(w_in[0], 4), w_out[0], small)
    mine = jnp.where(core == 0, first, second)
    gathered = lax.all_gather(mine, SHARD_AXES, axis=0, tiled=True)
    both = lax.all_gather(gathered, "core", axis=0, tiled=False)
    f_qkv, f_att, f_in, f_out, f_small = unpack_halves(both[0], both[1], model_width, ff)
    f_out = (both, 1, (model_width + ff - 3 * model_width) // model_width)
    f_bqv = f_small[:, 0:2].T
    f_bin = group_columns(f_small[:, 8:].reshape(1, ff), 4)[0]
    params = (
        f_qkv,
        f_bqv,
        f_att,
        f_small[:, 2],
        f_small[:, 3],
        f_small[:, 4],
        f_in,
        f_bin,
        f_out,
        f_small[:, 5],
        f_small[:, 6],
        f_small[:, 7],
    )
    hidden, stored = layer_forward(hidden, hidden_bf, params, key_valid, batch_size)
    outputs = hidden.astype(jnp.bfloat16).reshape(inputs.shape)
    upstream = cotangent.astype(jnp.float32).reshape(-1, model_width)
    upstream, terms = layer_backward(upstream, stored, params, key_valid)
    (g_qkv, g_bqv, g_att, g_batt, g_n1g, g_n1b, g_in, g_bin, g_out, g_bout, g_n2g, g_n2b) = terms
    g_small = jnp.concatenate(
        [
            g_bqv.T,
            g_batt[:, None],
            g_n1g[:, None],
            g_n1b[:, None],
            g_bout[:, None],
            g_n2g[:, None],
            g_n2b[:, None],
            ungroup_columns(g_bin[None], 4)[0].reshape(model_width, -1),
        ],
        axis=1,
    )
    tokens = g_qkv[0].shape[0]
    col = lambda b, c: b[:, c * model_width : (c + 1) * model_width]
    hi = g_small.astype(jnp.bfloat16)
    rest = g_small - hi.astype(jnp.float32)
    mid_part = rest.astype(jnp.bfloat16)
    low = (rest - mid_part.astype(jnp.float32)).astype(jnp.bfloat16)
    n_small = g_small.shape[1]
    pieces = jnp.concatenate([hi.T, mid_part.T, low.T], axis=0)
    enc_left = jnp.zeros((tokens, model_width), jnp.bfloat16).at[: 3 * n_small].set(pieces)
    picks = lax.broadcasted_iota(jnp.int32, (tokens, model_width), 1) == (
        lax.broadcasted_iota(jnp.int32, (tokens, model_width), 0) % n_small
    )
    rows_used = lax.broadcasted_iota(jnp.int32, (tokens, model_width), 0) < 3 * n_small
    enc_right = (picks & rows_used).astype(jnp.bfloat16)
    zero = jnp.zeros((tokens, model_width), jnp.bfloat16)
    lefts = [g_qkv[0]] * 3 + [g_in[0]] * 3 + [zero]
    lefts += [g_att[0], g_in[0]] + [col(g_out[0], j) for j in range(4)] + [enc_left]
    rights = [col(g_qkv[1], c) for c in range(3)] + [col(g_in[1], c) for c in range(3)] + [zero]
    rights += [g_att[1], col(g_in[1], 3)] + [g_out[1]] * 4 + [enc_right]
    wgrads = jnp.einsum(
        "btk,btn->bkn",
        jnp.stack(lefts),
        jnp.stack(rights),
        preferred_element_type=jnp.float32,
    ).reshape(2, len(lefts) // 2, model_width, model_width)
    half = lax.psum_scatter(wgrads, "core", scatter_dimension=0, tiled=False)
    part = lax.psum_scatter(half, SHARD_AXES, scatter_dimension=1, tiled=True)
    part = lax.psum(part, "xh")
    res = lax.all_gather(part, "core", axis=0, tiled=False)
    r0, r1 = res[0], res[1]
    r_qkv = jnp.concatenate([r0[0], r0[1], r0[2]], axis=1)
    r_in = ungroup_columns(jnp.concatenate([r0[3], r0[4], r0[5], r1[1]], axis=1), 4)
    r_att = r1[0]
    r_out = jnp.stack([r1[2], r1[3], r1[4], r1[5]], axis=1)
    r_small = r1[6][:, :n_small]
    grad_inputs = upstream.reshape(inputs.shape)
    return (
        outputs,
        grad_inputs,
        r_qkv[None],
        r_small[:, 0:2].T[None],
        r_att[None],
        r_small[:, 2][None],
        r_small[:, 3][None],
        r_small[:, 4][None],
        r_in[None],
        r_small[:, 8:].reshape(-1)[None],
        r_out.reshape(-1, model_width)[None],
        r_small[:, 5][None],
        r_small[:, 6][None],
        r_small[:, 7][None],
    )


def solution(mesh):
    devices = mesh.devices.reshape(2, 2, 4, 2, 4)
    fine = jax.sharding.Mesh(devices, ("xh", "core", "y", "xl", "z"))
    seqs = P(("xh", "core", "y", "xl", "z"), None, None)
    rows = P(None, SHARD_AXES, None)
    vec = P(None, SHARD_AXES)
    return jax.shard_map(
        body,
        mesh=fine,
        in_specs=(
            seqs,
            P(("xh", "core", "y", "xl", "z")),
            seqs,
            rows,
            P(None, None, SHARD_AXES),
            rows,
            vec,
            vec,
            vec,
            rows,
            vec,
            rows,
            vec,
            vec,
            vec,
        ),
        out_specs=(
            seqs,
            seqs,
            rows,
            P(None, None, SHARD_AXES),
            rows,
            vec,
            vec,
            vec,
            rows,
            vec,
            rows,
            vec,
            vec,
            vec,
        ),
        check_vma=False,
    )
```

```python
import math

import jax
import jax.numpy as jnp
from jax import lax
from jax.experimental import pallas as pl
from jax.experimental.pallas import tpu as pltpu
from jax.sharding import PartitionSpec as P

HEAD_DIM = 64
LAYERS = 1


EPS = 1e-12
ROOT_HALF = 0.7071067811865476
INV_ROOT_TWO_PI = 0.3989422804014327


def _ffn_out_kernel(act_ref, w_ref, out_ref):
    @pl.when(pl.program_id(0) == 0)
    def _():
        out_ref[...] = jnp.zeros_like(out_ref)

    out_ref[...] += jnp.dot(act_ref[...], w_ref[...], preferred_element_type=jnp.float32)


def ffn_out(act_grouped, w_out):
    buffer, which, first_block = w_out
    tokens = act_grouped.shape[0]
    width = buffer.shape[1]
    groups = act_grouped.shape[1] // width
    return pl.pallas_call(
        _ffn_out_kernel,
        grid=(groups,),
        in_specs=[
            pl.BlockSpec((tokens, width), lambda j: (0, j)),
            pl.BlockSpec((None, width, width), lambda j: (which, 0, first_block + j)),
        ],
        out_specs=pl.BlockSpec((tokens, width), lambda j: (0, 0)),
        out_shape=jax.ShapeDtypeStruct((tokens, width), jnp.float32),
        cost_estimate=pl.CostEstimate(
            flops=2 * tokens * width * width * groups,
            bytes_accessed=2 * width * width * groups + 2 * tokens * width * groups + 4 * tokens * width,
            transcendentals=0,
        ),
    )(act_grouped, buffer)


def _ffn_out_back_kernel(grad_ref, w_ref, out_ref):
    out_ref[...] = lax.dot_general(
        grad_ref[...],
        w_ref[...],
        (((1,), (1,)), ((), ())),
        preferred_element_type=jnp.float32,
    )


def ffn_out_back(grad_bf, w_out):
    buffer, which, first_block = w_out
    tokens = grad_bf.shape[0]
    width = buffer.shape[1]
    groups = 4
    return pl.pallas_call(
        _ffn_out_back_kernel,
        grid=(groups,),
        in_specs=[
            pl.BlockSpec((tokens, width), lambda j: (0, 0)),
            pl.BlockSpec((None, width, width), lambda j: (which, 0, first_block + j)),
        ],
        out_specs=pl.BlockSpec((tokens, width), lambda j: (0, j)),
        out_shape=jax.ShapeDtypeStruct((tokens, width * groups), jnp.float32),
        cost_estimate=pl.CostEstimate(
            flops=2 * tokens * width * width * groups,
            bytes_accessed=2 * width * width * groups + 2 * tokens * width + 4 * tokens * width * groups,
            transcendentals=0,
        ),
    )(grad_bf, buffer)


def group_columns(x, groups):
    tokens = x.shape[0]
    return x.reshape(tokens, -1, groups).transpose(0, 2, 1).reshape(tokens, -1)


def ungroup_columns(x, groups):
    tokens = x.shape[0]
    return x.reshape(tokens, groups, -1).transpose(0, 2, 1).reshape(tokens, -1)


def batched(form, left, right):
    return jnp.einsum(form, left, right, preferred_element_type=jnp.float32)


def layer_norm(residual, gain, shift):
    row_mean = jnp.mean(residual, axis=-1, keepdims=True)
    centered = residual - row_mean
    variance = jnp.mean(centered * centered, axis=-1, keepdims=True)
    inv_std = lax.rsqrt(variance + EPS)
    normed = centered * inv_std
    return (normed * gain.astype(jnp.float32) + shift.astype(jnp.float32), normed, inv_std)


def norm_backward(upstream, normed, inv_std, gain):
    grad_gain = jnp.sum(upstream * normed, axis=0)
    grad_shift = jnp.sum(upstream, axis=0)
    scaled = upstream * gain.astype(jnp.float32)
    grad_res = inv_std * (
        scaled
        - jnp.mean(scaled, axis=-1, keepdims=True)
        - normed * jnp.mean(scaled * normed, axis=-1, keepdims=True)
    )
    return (grad_res, grad_gain, grad_shift)


def attention_scores(query_bf, key_bf, key_valid):
    scores = batched("bqhe,bkhe->bhqk", query_bf, key_bf) * (1.0 / math.sqrt(HEAD_DIM))
    return jnp.where(key_valid[:, None, None, :], scores, -1e30)


def layer_forward(hidden, hidden_bf, params, key_valid, batch_size):
    (
        w_qkv,
        b_qv,
        w_att,
        b_att,
        gain_one,
        shift_one,
        w_in,
        b_in,
        w_out,
        b_out,
        gain_two,
        shift_two,
    ) = params
    model_width = hidden.shape[1]
    seq_count = hidden.shape[0] // batch_size
    shape_heads = (batch_size, seq_count, model_width // HEAD_DIM, HEAD_DIM)
    packed = jnp.dot(hidden_bf, w_qkv, preferred_element_type=jnp.float32)
    bias_qv = b_qv.astype(jnp.float32)
    query_bf = (packed[:, :model_width] + bias_qv[0]).astype(jnp.bfloat16).reshape(shape_heads)
    key_bf = packed[:, model_width : 2 * model_width].astype(jnp.bfloat16).reshape(shape_heads)
    value_bf = (packed[:, 2 * model_width :] + bias_qv[1]).astype(jnp.bfloat16).reshape(shape_heads)
    scores = attention_scores(query_bf, key_bf, key_valid)
    row_max = jnp.max(scores, axis=-1, keepdims=True)
    row_lse = row_max + jnp.log(jnp.sum(jnp.exp(scores - row_max), axis=-1, keepdims=True))
    probs_bf = jnp.exp(scores - row_lse).astype(jnp.bfloat16)
    context_bf = (
        batched("bhqk,bkhe->bqhe", probs_bf, value_bf).astype(jnp.bfloat16).reshape(-1, model_width)
    )
    first = (
        hidden
        + jnp.dot(context_bf, w_att, preferred_element_type=jnp.float32)
        + b_att.astype(jnp.float32)
    )
    middle, normed_one, inv_one = layer_norm(first, gain_one, shift_one)
    middle_bf = middle.astype(jnp.bfloat16)
    pre_act = jnp.dot(middle_bf, w_in, preferred_element_type=jnp.float32) + b_in.astype(
        jnp.float32
    )
    act_bf = (pre_act * 0.5 * (1.0 + jax.scipy.special.erf(pre_act * ROOT_HALF))).astype(
        jnp.bfloat16
    )
    second = (
        middle
        + ffn_out(act_bf, w_out)
        + b_out.astype(jnp.float32)
    )
    result, normed_two, inv_two = layer_norm(second, gain_two, shift_two)
    stored = (
        hidden_bf,
        query_bf,
        key_bf,
        value_bf,
        row_lse,
        context_bf,
        normed_one,
        inv_one,
        middle_bf,
        pre_act,
        act_bf,
        normed_two,
        inv_two,
    )
    return (result, stored)


def layer_backward(upstream, stored, params, key_valid):
    (
        w_qkv,
        b_qv,
        w_att,
        b_att,
        gain_one,
        shift_one,
        w_in,
        b_in,
        w_out,
        b_out,
        gain_two,
        shift_two,
    ) = params
    (
        hidden_bf,
        query_bf,
        key_bf,
        value_bf,
        row_lse,
        context_bf,
        normed_one,
        inv_one,
        middle_bf,
        pre_act,
        act_bf,
        normed_two,
        inv_two,
    ) = stored
    model_width = upstream.shape[1]
    shape_heads = query_bf.shape
    grad_second, grad_gain_two, grad_shift_two = norm_backward(
        upstream, normed_two, inv_two, gain_two
    )
    grad_b_out = jnp.sum(grad_second, axis=0)
    second_bf = grad_second.astype(jnp.bfloat16)
    back_act = ffn_out_back(second_bf, w_out)
    cumulative = 0.5 * (1.0 + jax.scipy.special.erf(pre_act * ROOT_HALF))
    density = jnp.exp(-0.5 * pre_act * pre_act) * INV_ROOT_TWO_PI
    grad_pre = back_act * (cumulative + pre_act * density)
    pre_bf = grad_pre.astype(jnp.bfloat16)
    grad_b_in = jnp.sum(grad_pre, axis=0)
    grad_middle = grad_second + jnp.dot(pre_bf, w_in.T, preferred_element_type=jnp.float32)
    grad_first, grad_gain_one, grad_shift_one = norm_backward(
        grad_middle, normed_one, inv_one, gain_one
    )
    grad_b_att = jnp.sum(grad_first, axis=0)
    first_bf = grad_first.astype(jnp.bfloat16)
    grad_context = (
        jnp.dot(first_bf, w_att.T, preferred_element_type=jnp.float32)
        .astype(jnp.bfloat16)
        .reshape(shape_heads)
    )
    scores = attention_scores(query_bf, key_bf, key_valid)
    probs = jnp.exp(scores - row_lse)
    grad_value = batched("bhqk,bqhe->bkhe", probs.astype(jnp.bfloat16), grad_context).reshape(
        -1, model_width
    )
    grad_probs = batched("bqhe,bkhe->bhqk", grad_context, value_bf)
    inner = jnp.sum(probs * grad_probs, axis=-1, keepdims=True)
    grad_scores = (probs * (grad_probs - inner) * (1.0 / math.sqrt(HEAD_DIM))).astype(jnp.bfloat16)
    grad_query = batched("bhqk,bkhe->bqhe", grad_scores, key_bf).reshape(-1, model_width)
    grad_key = batched("bhqk,bqhe->bkhe", grad_scores, query_bf).reshape(-1, model_width)
    grad_b_qv = jnp.stack([jnp.sum(grad_query, axis=0), jnp.sum(grad_value, axis=0)])
    packed_bf = jnp.concatenate([grad_query, grad_key, grad_value], axis=1).astype(jnp.bfloat16)
    grad_hidden = grad_first + jnp.dot(packed_bf, w_qkv.T, preferred_element_type=jnp.float32)
    terms = (
        (hidden_bf, packed_bf),
        grad_b_qv,
        (context_bf, first_bf),
        grad_b_att,
        grad_gain_one,
        grad_shift_one,
        (middle_bf, pre_bf),
        grad_b_in,
        (act_bf, second_bf),
        grad_b_out,
        grad_gain_two,
        grad_shift_two,
    )
    return (grad_hidden, terms)


SHARD_AXES = ("y", "xl", "z")
PAIR_AXES = ("xh", "core")


def pack_halves(w_qkv, w_att, w_in, w_out, small):
    rows = w_qkv.shape[0]
    split = w_qkv.shape[1]
    pad = jnp.zeros((rows, small.shape[1]), w_qkv.dtype)
    first = jnp.concatenate([w_qkv, w_in[:, :split], pad], axis=1)
    second = jnp.concatenate(
        [w_att, w_in[:, split:], w_out.reshape(rows, -1), small], axis=1
    )
    return first, second


def unpack_halves(first, second, width, ff):
    split = 3 * width
    w_qkv = first[:, :split]
    w_in = jnp.concatenate([first[:, split : 2 * split], second[:, width : width + ff - split]], axis=1)
    at = width + ff - split
    w_att = second[:, :width]
    w_out = second[:, at : at + ff]
    small = second[:, at + ff :]
    return w_qkv, w_att, w_in, w_out, small


def body(
    inputs,
    lengths,
    cotangent,
    w_qkv,
    b_qv,
    w_att,
    b_att,
    norm1_gain,
    norm1_bias,
    w_in,
    b_in,
    w_out,
    b_out,
    norm2_gain,
    norm2_bias,
):
    batch_size, seq_count, model_width = inputs.shape
    ff = w_in.shape[2]
    rows = w_qkv.shape[1]
    core = lax.axis_index("core")
    key_valid = lax.broadcasted_iota(jnp.int32, (batch_size, seq_count), 1) < lengths[:, None]
    hidden = inputs.astype(jnp.float32).reshape(-1, model_width)
    hidden_bf = inputs.reshape(-1, model_width)
    small = jnp.concatenate(
        [
            b_qv[0].T,
            b_att[0][:, None],
            norm1_gain[0][:, None],
            norm1_bias[0][:, None],
            b_out[0][:, None],
            norm2_gain[0][:, None],
            norm2_bias[0][:, None],
            b_in[0].reshape(rows, -1),
        ],
        axis=1,
    )
    first, second = pack_halves(w_qkv[0], w_att[0], group_columns(w_in[0], 4), w_out[0], small)
    mine = jnp.where(core == 0, first, second)
    gathered = lax.all_gather(mine, SHARD_AXES, axis=0, tiled=True)
    both = lax.all_gather(gathered, "core", axis=0, tiled=False)
    f_qkv, f_att, f_in, f_out, f_small = unpack_halves(both[0], both[1], model_width, ff)
    f_out = (both, 1, (model_width + ff - 3 * model_width) // model_width)
    f_bqv = f_small[:, 0:2].T
    f_bin = group_columns(f_small[:, 8:].reshape(1, ff), 4)[0]
    params = (
        f_qkv,
        f_bqv,
        f_att,
        f_small[:, 2],
        f_small[:, 3],
        f_small[:, 4],
        f_in,
        f_bin,
        f_out,
        f_small[:, 5],
        f_small[:, 6],
        f_small[:, 7],
    )
    hidden, stored = layer_forward(hidden, hidden_bf, params, key_valid, batch_size)
    outputs = hidden.astype(jnp.bfloat16).reshape(inputs.shape)
    upstream = cotangent.astype(jnp.float32).reshape(-1, model_width)
    upstream, terms = layer_backward(upstream, stored, params, key_valid)
    (g_qkv, g_bqv, g_att, g_batt, g_n1g, g_n1b, g_in, g_bin, g_out, g_bout, g_n2g, g_n2b) = terms
    g_small = jnp.concatenate(
        [
            g_bqv.T,
            g_batt[:, None],
            g_n1g[:, None],
            g_n1b[:, None],
            g_bout[:, None],
            g_n2g[:, None],
            g_n2b[:, None],
            ungroup_columns(g_bin[None], 4)[0].reshape(model_width, -1),
        ],
        axis=1,
    )
    tokens = g_qkv[0].shape[0]
    col = lambda b, c: b[:, c * model_width : (c + 1) * model_width]
    hi = g_small.astype(jnp.bfloat16)
    rest = g_small - hi.astype(jnp.float32)
    mid_part = rest.astype(jnp.bfloat16)
    low = (rest - mid_part.astype(jnp.float32)).astype(jnp.bfloat16)
    n_small = g_small.shape[1]
    pieces = jnp.concatenate([hi.T, mid_part.T, low.T], axis=0)
    enc_left = jnp.zeros((tokens, model_width), jnp.bfloat16).at[: 3 * n_small].set(pieces)
    picks = lax.broadcasted_iota(jnp.int32, (tokens, model_width), 1) == (
        lax.broadcasted_iota(jnp.int32, (tokens, model_width), 0) % n_small
    )
    rows_used = lax.broadcasted_iota(jnp.int32, (tokens, model_width), 0) < 3 * n_small
    enc_right = (picks & rows_used).astype(jnp.bfloat16)
    zero = jnp.zeros((tokens, model_width), jnp.bfloat16)
    lefts = [g_qkv[0]] * 3 + [g_in[0]] * 3 + [zero]
    lefts += [g_att[0], g_in[0]] + [col(g_out[0], j) for j in range(4)] + [enc_left]
    rights = [col(g_qkv[1], c) for c in range(3)] + [col(g_in[1], c) for c in range(3)] + [zero]
    rights += [g_att[1], col(g_in[1], 3)] + [g_out[1]] * 4 + [enc_right]
    wgrads = jnp.einsum(
        "btk,btn->bkn",
        jnp.stack(lefts),
        jnp.stack(rights),
        preferred_element_type=jnp.float32,
    ).reshape(2, len(lefts) // 2, model_width, model_width)
    half = lax.psum_scatter(wgrads.astype(jnp.bfloat16), "core", scatter_dimension=0, tiled=False)
    part = lax.psum_scatter(
        half.astype(jnp.float32), SHARD_AXES, scatter_dimension=1, tiled=True
    )
    part = lax.psum(part, "xh")
    res = lax.all_gather(part, "core", axis=0, tiled=False)
    r0, r1 = res[0], res[1]
    r_qkv = jnp.concatenate([r0[0], r0[1], r0[2]], axis=1)
    r_in = ungroup_columns(jnp.concatenate([r0[3], r0[4], r0[5], r1[1]], axis=1), 4)
    r_att = r1[0]
    r_out = jnp.stack([r1[2], r1[3], r1[4], r1[5]], axis=1)
    r_small = r1[6][:, :n_small]
    grad_inputs = upstream.reshape(inputs.shape)
    return (
        outputs,
        grad_inputs,
        r_qkv[None],
        r_small[:, 0:2].T[None],
        r_att[None],
        r_small[:, 2][None],
        r_small[:, 3][None],
        r_small[:, 4][None],
        r_in[None],
        r_small[:, 8:].reshape(-1)[None],
        r_out.reshape(-1, model_width)[None],
        r_small[:, 5][None],
        r_small[:, 6][None],
        r_small[:, 7][None],
    )


def solution(mesh):
    devices = mesh.devices.reshape(2, 2, 4, 2, 4)
    fine = jax.sharding.Mesh(devices, ("xh", "core", "y", "xl", "z"))
    seqs = P(("xh", "core", "y", "xl", "z"), None, None)
    rows = P(None, SHARD_AXES, None)
    vec = P(None, SHARD_AXES)
    return jax.shard_map(
        body,
        mesh=fine,
        in_specs=(
            seqs,
            P(("xh", "core", "y", "xl", "z")),
            seqs,
            rows,
            P(None, None, SHARD_AXES),
            rows,
            vec,
            vec,
            vec,
            rows,
            vec,
            rows,
            vec,
            vec,
            vec,
        ),
        out_specs=(
            seqs,
            seqs,
            rows,
            P(None, None, SHARD_AXES),
            rows,
            vec,
            vec,
            vec,
            rows,
            vec,
            rows,
            vec,
            vec,
            vec,
        ),
        check_vma=False,
    )
```

```python
import math

import jax
import jax.numpy as jnp
from jax import lax
from jax.experimental import pallas as pl
from jax.experimental.pallas import tpu as pltpu
from jax.sharding import PartitionSpec as P

HEAD_DIM = 64
LAYERS = 1


EPS = 1e-12
ROOT_HALF = 0.7071067811865476
INV_ROOT_TWO_PI = 0.3989422804014327


def _ffn_out_kernel(act_ref, w_ref, out_ref):
    @pl.when(pl.program_id(0) == 0)
    def _():
        out_ref[...] = jnp.zeros_like(out_ref)

    out_ref[...] += jnp.dot(act_ref[...], w_ref[...], preferred_element_type=jnp.float32)


def ffn_out(act_grouped, w_out):
    buffer, which, first_block = w_out
    tokens = act_grouped.shape[0]
    width = buffer.shape[1]
    groups = act_grouped.shape[1] // width
    return pl.pallas_call(
        _ffn_out_kernel,
        grid=(groups,),
        in_specs=[
            pl.BlockSpec((tokens, width), lambda j: (0, j)),
            pl.BlockSpec((None, width, width), lambda j: (which, 0, first_block + j)),
        ],
        out_specs=pl.BlockSpec((tokens, width), lambda j: (0, 0)),
        out_shape=jax.ShapeDtypeStruct((tokens, width), jnp.float32),
        cost_estimate=pl.CostEstimate(
            flops=2 * tokens * width * width * groups,
            bytes_accessed=2 * width * width * groups + 2 * tokens * width * groups + 4 * tokens * width,
            transcendentals=0,
        ),
    )(act_grouped, buffer)


def _ffn_out_back_kernel(grad_ref, w_ref, out_ref):
    out_ref[...] = lax.dot_general(
        grad_ref[...],
        w_ref[...],
        (((1,), (1,)), ((), ())),
        preferred_element_type=jnp.float32,
    )


def ffn_out_back(grad_bf, w_out):
    buffer, which, first_block = w_out
    tokens = grad_bf.shape[0]
    width = buffer.shape[1]
    groups = 4
    return pl.pallas_call(
        _ffn_out_back_kernel,
        grid=(groups,),
        in_specs=[
            pl.BlockSpec((tokens, width), lambda j: (0, 0)),
            pl.BlockSpec((None, width, width), lambda j: (which, 0, first_block + j)),
        ],
        out_specs=pl.BlockSpec((tokens, width), lambda j: (0, j)),
        out_shape=jax.ShapeDtypeStruct((tokens, width * groups), jnp.float32),
        cost_estimate=pl.CostEstimate(
            flops=2 * tokens * width * width * groups,
            bytes_accessed=2 * width * width * groups + 2 * tokens * width + 4 * tokens * width * groups,
            transcendentals=0,
        ),
    )(grad_bf, buffer)


def group_columns(x, groups):
    tokens = x.shape[0]
    return x.reshape(tokens, -1, groups).transpose(0, 2, 1).reshape(tokens, -1)


def ungroup_columns(x, groups):
    tokens = x.shape[0]
    return x.reshape(tokens, groups, -1).transpose(0, 2, 1).reshape(tokens, -1)


def batched(form, left, right):
    return jnp.einsum(form, left, right, preferred_element_type=jnp.float32)


def layer_norm(residual, gain, shift):
    row_mean = jnp.mean(residual, axis=-1, keepdims=True)
    centered = residual - row_mean
    variance = jnp.mean(centered * centered, axis=-1, keepdims=True)
    inv_std = lax.rsqrt(variance + EPS)
    normed = centered * inv_std
    return (normed * gain.astype(jnp.float32) + shift.astype(jnp.float32), normed, inv_std)


def norm_backward(upstream, normed, inv_std, gain):
    grad_gain = jnp.sum(upstream * normed, axis=0)
    grad_shift = jnp.sum(upstream, axis=0)
    scaled = upstream * gain.astype(jnp.float32)
    grad_res = inv_std * (
        scaled
        - jnp.mean(scaled, axis=-1, keepdims=True)
        - normed * jnp.mean(scaled * normed, axis=-1, keepdims=True)
    )
    return (grad_res, grad_gain, grad_shift)


def attention_scores(query_bf, key_bf, key_valid):
    scores = batched("bqhe,bkhe->bhqk", query_bf, key_bf) * (1.0 / math.sqrt(HEAD_DIM))
    return jnp.where(key_valid[:, None, None, :], scores, -1e30)


def layer_forward(hidden, hidden_bf, params, key_valid, batch_size):
    (
        w_qkv,
        b_qv,
        w_att,
        b_att,
        gain_one,
        shift_one,
        w_in,
        b_in,
        w_out,
        b_out,
        gain_two,
        shift_two,
    ) = params
    model_width = hidden.shape[1]
    seq_count = hidden.shape[0] // batch_size
    shape_heads = (batch_size, seq_count, model_width // HEAD_DIM, HEAD_DIM)
    packed = jnp.dot(hidden_bf, w_qkv, preferred_element_type=jnp.float32)
    bias_qv = b_qv.astype(jnp.float32)
    query_bf = (packed[:, :model_width] + bias_qv[0]).astype(jnp.bfloat16).reshape(shape_heads)
    key_bf = packed[:, model_width : 2 * model_width].astype(jnp.bfloat16).reshape(shape_heads)
    value_bf = (packed[:, 2 * model_width :] + bias_qv[1]).astype(jnp.bfloat16).reshape(shape_heads)
    scores = attention_scores(query_bf, key_bf, key_valid)
    row_max = jnp.max(scores, axis=-1, keepdims=True)
    row_lse = row_max + jnp.log(jnp.sum(jnp.exp(scores - row_max), axis=-1, keepdims=True))
    probs_bf = jnp.exp(scores - row_lse).astype(jnp.bfloat16)
    context_bf = (
        batched("bhqk,bkhe->bqhe", probs_bf, value_bf).astype(jnp.bfloat16).reshape(-1, model_width)
    )
    first = (
        hidden
        + jnp.dot(context_bf, w_att, preferred_element_type=jnp.float32)
        + b_att.astype(jnp.float32)
    )
    middle, normed_one, inv_one = layer_norm(first, gain_one, shift_one)
    middle_bf = middle.astype(jnp.bfloat16)
    pre_act = jnp.dot(middle_bf, w_in, preferred_element_type=jnp.float32) + b_in.astype(
        jnp.float32
    )
    act_bf = (pre_act * 0.5 * (1.0 + jax.scipy.special.erf(pre_act * ROOT_HALF))).astype(
        jnp.bfloat16
    )
    second = (
        middle
        + ffn_out(act_bf, w_out)
        + b_out.astype(jnp.float32)
    )
    result, normed_two, inv_two = layer_norm(second, gain_two, shift_two)
    stored = (
        hidden_bf,
        query_bf,
        key_bf,
        value_bf,
        row_lse,
        context_bf,
        normed_one,
        inv_one,
        middle_bf,
        pre_act,
        act_bf,
        normed_two,
        inv_two,
    )
    return (result, stored)


def layer_backward(upstream, stored, params, key_valid):
    (
        w_qkv,
        b_qv,
        w_att,
        b_att,
        gain_one,
        shift_one,
        w_in,
        b_in,
        w_out,
        b_out,
        gain_two,
        shift_two,
    ) = params
    (
        hidden_bf,
        query_bf,
        key_bf,
        value_bf,
        row_lse,
        context_bf,
        normed_one,
        inv_one,
        middle_bf,
        pre_act,
        act_bf,
        normed_two,
        inv_two,
    ) = stored
    model_width = upstream.shape[1]
    shape_heads = query_bf.shape
    grad_second, grad_gain_two, grad_shift_two = norm_backward(
        upstream, normed_two, inv_two, gain_two
    )
    grad_b_out = jnp.sum(grad_second, axis=0)
    second_bf = grad_second.astype(jnp.bfloat16)
    back_act = ffn_out_back(second_bf, w_out)
    cumulative = 0.5 * (1.0 + jax.scipy.special.erf(pre_act * ROOT_HALF))
    density = jnp.exp(-0.5 * pre_act * pre_act) * INV_ROOT_TWO_PI
    grad_pre = back_act * (cumulative + pre_act * density)
    pre_bf = grad_pre.astype(jnp.bfloat16)
    grad_b_in = jnp.sum(grad_pre, axis=0)
    grad_middle = grad_second + jnp.dot(pre_bf, w_in.T, preferred_element_type=jnp.float32)
    grad_first, grad_gain_one, grad_shift_one = norm_backward(
        grad_middle, normed_one, inv_one, gain_one
    )
    grad_b_att = jnp.sum(grad_first, axis=0)
    first_bf = grad_first.astype(jnp.bfloat16)
    grad_context = (
        jnp.dot(first_bf, w_att.T, preferred_element_type=jnp.float32)
        .astype(jnp.bfloat16)
        .reshape(shape_heads)
    )
    scores = attention_scores(query_bf, key_bf, key_valid)
    probs = jnp.exp(scores - row_lse)
    grad_value = batched("bhqk,bqhe->bkhe", probs.astype(jnp.bfloat16), grad_context).reshape(
        -1, model_width
    )
    grad_probs = batched("bqhe,bkhe->bhqk", grad_context, value_bf)
    inner = jnp.sum(probs * grad_probs, axis=-1, keepdims=True)
    grad_scores = (probs * (grad_probs - inner) * (1.0 / math.sqrt(HEAD_DIM))).astype(jnp.bfloat16)
    grad_query = batched("bhqk,bkhe->bqhe", grad_scores, key_bf).reshape(-1, model_width)
    grad_key = batched("bhqk,bqhe->bkhe", grad_scores, query_bf).reshape(-1, model_width)
    grad_b_qv = jnp.stack([jnp.sum(grad_query, axis=0), jnp.sum(grad_value, axis=0)])
    packed_bf = jnp.concatenate([grad_query, grad_key, grad_value], axis=1).astype(jnp.bfloat16)
    grad_hidden = grad_first + jnp.dot(packed_bf, w_qkv.T, preferred_element_type=jnp.float32)
    terms = (
        (hidden_bf, packed_bf),
        grad_b_qv,
        (context_bf, first_bf),
        grad_b_att,
        grad_gain_one,
        grad_shift_one,
        (middle_bf, pre_bf),
        grad_b_in,
        (act_bf, second_bf),
        grad_b_out,
        grad_gain_two,
        grad_shift_two,
    )
    return (grad_hidden, terms)


SHARD_AXES = ("y", "xl", "z")
PAIR_AXES = ("xh", "core")


def pack_halves(w_qkv, w_att, w_in, w_out, small):
    rows = w_qkv.shape[0]
    split = w_qkv.shape[1]
    pad = jnp.zeros((rows, small.shape[1]), w_qkv.dtype)
    first = jnp.concatenate([w_qkv, w_in[:, :split], pad], axis=1)
    second = jnp.concatenate(
        [w_att, w_in[:, split:], w_out.reshape(rows, -1), small], axis=1
    )
    return first, second


def unpack_halves(first, second, width, ff):
    split = 3 * width
    w_qkv = first[:, :split]
    w_in = jnp.concatenate([first[:, split : 2 * split], second[:, width : width + ff - split]], axis=1)
    at = width + ff - split
    w_att = second[:, :width]
    w_out = second[:, at : at + ff]
    small = second[:, at + ff :]
    return w_qkv, w_att, w_in, w_out, small


def body(
    inputs,
    lengths,
    cotangent,
    w_qkv,
    b_qv,
    w_att,
    b_att,
    norm1_gain,
    norm1_bias,
    w_in,
    b_in,
    w_out,
    b_out,
    norm2_gain,
    norm2_bias,
):
    batch_size, seq_count, model_width = inputs.shape
    ff = w_in.shape[2]
    rows = w_qkv.shape[1]
    core = lax.axis_index("core")
    key_valid = lax.broadcasted_iota(jnp.int32, (batch_size, seq_count), 1) < lengths[:, None]
    hidden = inputs.astype(jnp.float32).reshape(-1, model_width)
    hidden_bf = inputs.reshape(-1, model_width)
    small = jnp.concatenate(
        [
            b_qv[0].T,
            b_att[0][:, None],
            norm1_gain[0][:, None],
            norm1_bias[0][:, None],
            b_out[0][:, None],
            norm2_gain[0][:, None],
            norm2_bias[0][:, None],
            b_in[0].reshape(rows, -1),
        ],
        axis=1,
    )
    first, second = pack_halves(w_qkv[0], w_att[0], group_columns(w_in[0], 4), w_out[0], small)
    mine = jnp.where(core == 0, first, second)
    gathered = lax.all_gather(mine, SHARD_AXES, axis=0, tiled=True)
    both = lax.all_gather(gathered, "core", axis=0, tiled=False)
    f_qkv, f_att, f_in, f_out, f_small = unpack_halves(both[0], both[1], model_width, ff)
    f_out = (both, 1, (model_width + ff - 3 * model_width) // model_width)
    f_bqv = f_small[:, 0:2].T
    f_bin = group_columns(f_small[:, 8:].reshape(1, ff), 4)[0]
    params = (
        f_qkv,
        f_bqv,
        f_att,
        f_small[:, 2],
        f_small[:, 3],
        f_small[:, 4],
        f_in,
        f_bin,
        f_out,
        f_small[:, 5],
        f_small[:, 6],
        f_small[:, 7],
    )
    hidden, stored = layer_forward(hidden, hidden_bf, params, key_valid, batch_size)
    outputs = hidden.astype(jnp.bfloat16).reshape(inputs.shape)
    upstream = cotangent.astype(jnp.float32).reshape(-1, model_width)
    upstream, terms = layer_backward(upstream, stored, params, key_valid)
    (g_qkv, g_bqv, g_att, g_batt, g_n1g, g_n1b, g_in, g_bin, g_out, g_bout, g_n2g, g_n2b) = terms
    g_small = jnp.concatenate(
        [
            g_bqv.T,
            g_batt[:, None],
            g_n1g[:, None],
            g_n1b[:, None],
            g_bout[:, None],
            g_n2g[:, None],
            g_n2b[:, None],
            ungroup_columns(g_bin[None], 4)[0].reshape(model_width, -1),
        ],
        axis=1,
    )
    tokens = g_qkv[0].shape[0]
    col = lambda b, c: b[:, c * model_width : (c + 1) * model_width]
    hi = g_small.astype(jnp.bfloat16)
    rest = g_small - hi.astype(jnp.float32)
    mid_part = rest.astype(jnp.bfloat16)
    low = (rest - mid_part.astype(jnp.float32)).astype(jnp.bfloat16)
    n_small = g_small.shape[1]
    pieces = jnp.concatenate([hi.T, mid_part.T, low.T], axis=0)
    enc_left = jnp.zeros((tokens, model_width), jnp.bfloat16).at[: 3 * n_small].set(pieces)
    picks = lax.broadcasted_iota(jnp.int32, (tokens, model_width), 1) == (
        lax.broadcasted_iota(jnp.int32, (tokens, model_width), 0) % n_small
    )
    rows_used = lax.broadcasted_iota(jnp.int32, (tokens, model_width), 0) < 3 * n_small
    enc_right = (picks & rows_used).astype(jnp.bfloat16)
    zero = jnp.zeros((tokens, model_width), jnp.bfloat16)
    lefts = [g_qkv[0]] * 3 + [g_in[0]] * 3 + [zero]
    lefts += [g_att[0], g_in[0]] + [col(g_out[0], j) for j in range(4)] + [enc_left]
    rights = [col(g_qkv[1], c) for c in range(3)] + [col(g_in[1], c) for c in range(3)] + [zero]
    rights += [g_att[1], col(g_in[1], 3)] + [g_out[1]] * 4 + [enc_right]
    wgrads = jnp.einsum(
        "btk,btn->bkn",
        jnp.stack(lefts),
        jnp.stack(rights),
        preferred_element_type=jnp.float32,
    ).reshape(2, len(lefts) // 2, model_width, model_width)
    half = lax.psum_scatter(wgrads.astype(jnp.bfloat16), "core", scatter_dimension=0, tiled=False)
    part = lax.psum_scatter(
        half.astype(jnp.float32), SHARD_AXES, scatter_dimension=1, tiled=True
    )
    slots = jnp.zeros((2,) + part.shape, part.dtype)
    res = lax.psum(lax.dynamic_update_index_in_dim(slots, part, core, 0), ("xh", "core"))
    r0, r1 = res[0], res[1]
    r_qkv = jnp.concatenate([r0[0], r0[1], r0[2]], axis=1)
    r_in = ungroup_columns(jnp.concatenate([r0[3], r0[4], r0[5], r1[1]], axis=1), 4)
    r_att = r1[0]
    r_out = jnp.stack([r1[2], r1[3], r1[4], r1[5]], axis=1)
    r_small = r1[6][:, :n_small]
    grad_inputs = upstream.reshape(inputs.shape)
    return (
        outputs,
        grad_inputs,
        r_qkv[None],
        r_small[:, 0:2].T[None],
        r_att[None],
        r_small[:, 2][None],
        r_small[:, 3][None],
        r_small[:, 4][None],
        r_in[None],
        r_small[:, 8:].reshape(-1)[None],
        r_out.reshape(-1, model_width)[None],
        r_small[:, 5][None],
        r_small[:, 6][None],
        r_small[:, 7][None],
    )


def solution(mesh):
    devices = mesh.devices.reshape(2, 2, 4, 2, 4)
    fine = jax.sharding.Mesh(devices, ("xh", "core", "y", "xl", "z"))
    seqs = P(("xh", "core", "y", "xl", "z"), None, None)
    rows = P(None, SHARD_AXES, None)
    vec = P(None, SHARD_AXES)
    return jax.shard_map(
        body,
        mesh=fine,
        in_specs=(
            seqs,
            P(("xh", "core", "y", "xl", "z")),
            seqs,
            rows,
            P(None, None, SHARD_AXES),
            rows,
            vec,
            vec,
            vec,
            rows,
            vec,
            rows,
            vec,
            vec,
            vec,
        ),
        out_specs=(
            seqs,
            seqs,
            rows,
            P(None, None, SHARD_AXES),
            rows,
            vec,
            vec,
            vec,
            rows,
            vec,
            rows,
            vec,
            vec,
            vec,
        ),
        check_vma=False,
    )
```

```python
import math

import jax
import jax.numpy as jnp
from jax import lax
from jax.experimental import pallas as pl
from jax.experimental.pallas import tpu as pltpu
from jax.sharding import PartitionSpec as P

HEAD_DIM = 64
LAYERS = 1


EPS = 1e-12
ROOT_HALF = 0.7071067811865476
INV_ROOT_TWO_PI = 0.3989422804014327


def _ffn_out_kernel(act_ref, w_ref, out_ref):
    @pl.when(pl.program_id(0) == 0)
    def _():
        out_ref[...] = jnp.zeros_like(out_ref)

    out_ref[...] += jnp.dot(act_ref[...], w_ref[...], preferred_element_type=jnp.float32)


def ffn_out(act_grouped, w_out):
    buffer, which, first_block = w_out
    tokens = act_grouped.shape[0]
    width = buffer.shape[1]
    groups = act_grouped.shape[1] // width
    return pl.pallas_call(
        _ffn_out_kernel,
        grid=(groups,),
        in_specs=[
            pl.BlockSpec((tokens, width), lambda j: (0, j)),
            pl.BlockSpec((None, width, width), lambda j: (which, 0, first_block + j)),
        ],
        out_specs=pl.BlockSpec((tokens, width), lambda j: (0, 0)),
        out_shape=jax.ShapeDtypeStruct((tokens, width), jnp.float32),
        cost_estimate=pl.CostEstimate(
            flops=2 * tokens * width * width * groups,
            bytes_accessed=2 * width * width * groups + 2 * tokens * width * groups + 4 * tokens * width,
            transcendentals=0,
        ),
    )(act_grouped, buffer)


def _ffn_out_back_kernel(grad_ref, w_ref, out_ref):
    out_ref[...] = lax.dot_general(
        grad_ref[...],
        w_ref[...],
        (((1,), (1,)), ((), ())),
        preferred_element_type=jnp.float32,
    )


def ffn_out_back(grad_bf, w_out):
    buffer, which, first_block = w_out
    tokens = grad_bf.shape[0]
    width = buffer.shape[1]
    groups = 4
    return pl.pallas_call(
        _ffn_out_back_kernel,
        grid=(groups,),
        in_specs=[
            pl.BlockSpec((tokens, width), lambda j: (0, 0)),
            pl.BlockSpec((None, width, width), lambda j: (which, 0, first_block + j)),
        ],
        out_specs=pl.BlockSpec((tokens, width), lambda j: (0, j)),
        out_shape=jax.ShapeDtypeStruct((tokens, width * groups), jnp.float32),
        cost_estimate=pl.CostEstimate(
            flops=2 * tokens * width * width * groups,
            bytes_accessed=2 * width * width * groups + 2 * tokens * width + 4 * tokens * width * groups,
            transcendentals=0,
        ),
    )(grad_bf, buffer)


def group_columns(x, groups):
    tokens = x.shape[0]
    return x.reshape(tokens, -1, groups).transpose(0, 2, 1).reshape(tokens, -1)


def ungroup_columns(x, groups):
    tokens = x.shape[0]
    return x.reshape(tokens, groups, -1).transpose(0, 2, 1).reshape(tokens, -1)


def batched(form, left, right):
    return jnp.einsum(form, left, right, preferred_element_type=jnp.float32)


def layer_norm(residual, gain, shift):
    row_mean = jnp.mean(residual, axis=-1, keepdims=True)
    centered = residual - row_mean
    variance = jnp.mean(centered * centered, axis=-1, keepdims=True)
    inv_std = lax.rsqrt(variance + EPS)
    normed = centered * inv_std
    return (normed * gain.astype(jnp.float32) + shift.astype(jnp.float32), normed, inv_std)


def norm_backward(upstream, normed, inv_std, gain):
    grad_gain = jnp.sum(upstream * normed, axis=0)
    grad_shift = jnp.sum(upstream, axis=0)
    scaled = upstream * gain.astype(jnp.float32)
    grad_res = inv_std * (
        scaled
        - jnp.mean(scaled, axis=-1, keepdims=True)
        - normed * jnp.mean(scaled * normed, axis=-1, keepdims=True)
    )
    return (grad_res, grad_gain, grad_shift)


def attention_scores(query_bf, key_bf, key_valid):
    scores = batched("bqhe,bkhe->bhqk", query_bf, key_bf) * (1.0 / math.sqrt(HEAD_DIM))
    return jnp.where(key_valid[:, None, None, :], scores, -1e30)


def layer_forward(hidden, hidden_bf, params, key_valid, batch_size):
    (
        w_qkv,
        b_qv,
        w_att,
        b_att,
        gain_one,
        shift_one,
        w_in,
        b_in,
        w_out,
        b_out,
        gain_two,
        shift_two,
    ) = params
    model_width = hidden.shape[1]
    seq_count = hidden.shape[0] // batch_size
    shape_heads = (batch_size, seq_count, model_width // HEAD_DIM, HEAD_DIM)
    packed = jnp.dot(hidden_bf, w_qkv, preferred_element_type=jnp.float32)
    bias_qv = b_qv.astype(jnp.float32)
    query_bf = (packed[:, :model_width] + bias_qv[0]).astype(jnp.bfloat16).reshape(shape_heads)
    key_bf = packed[:, model_width : 2 * model_width].astype(jnp.bfloat16).reshape(shape_heads)
    value_bf = (packed[:, 2 * model_width :] + bias_qv[1]).astype(jnp.bfloat16).reshape(shape_heads)
    scores = attention_scores(query_bf, key_bf, key_valid)
    row_max = jnp.max(scores, axis=-1, keepdims=True)
    row_lse = row_max + jnp.log(jnp.sum(jnp.exp(scores - row_max), axis=-1, keepdims=True))
    probs_bf = jnp.exp(scores - row_lse).astype(jnp.bfloat16)
    context_bf = (
        batched("bhqk,bkhe->bqhe", probs_bf, value_bf).astype(jnp.bfloat16).reshape(-1, model_width)
    )
    first = (
        hidden
        + jnp.dot(context_bf, w_att, preferred_element_type=jnp.float32)
        + b_att.astype(jnp.float32)
    )
    middle, normed_one, inv_one = layer_norm(first, gain_one, shift_one)
    middle_bf = middle.astype(jnp.bfloat16)
    pre_act = jnp.dot(middle_bf, w_in, preferred_element_type=jnp.float32) + b_in.astype(
        jnp.float32
    )
    act_bf = (pre_act * 0.5 * (1.0 + jax.scipy.special.erf(pre_act * ROOT_HALF))).astype(
        jnp.bfloat16
    )
    second = (
        middle
        + ffn_out(act_bf, w_out)
        + b_out.astype(jnp.float32)
    )
    result, normed_two, inv_two = layer_norm(second, gain_two, shift_two)
    stored = (
        hidden_bf,
        query_bf,
        key_bf,
        value_bf,
        row_lse,
        context_bf,
        normed_one,
        inv_one,
        middle_bf,
        pre_act,
        act_bf,
        normed_two,
        inv_two,
    )
    return (result, stored)


def layer_backward(upstream, stored, params, key_valid):
    (
        w_qkv,
        b_qv,
        w_att,
        b_att,
        gain_one,
        shift_one,
        w_in,
        b_in,
        w_out,
        b_out,
        gain_two,
        shift_two,
    ) = params
    (
        hidden_bf,
        query_bf,
        key_bf,
        value_bf,
        row_lse,
        context_bf,
        normed_one,
        inv_one,
        middle_bf,
        pre_act,
        act_bf,
        normed_two,
        inv_two,
    ) = stored
    model_width = upstream.shape[1]
    shape_heads = query_bf.shape
    grad_second, grad_gain_two, grad_shift_two = norm_backward(
        upstream, normed_two, inv_two, gain_two
    )
    grad_b_out = jnp.sum(grad_second, axis=0)
    second_bf = grad_second.astype(jnp.bfloat16)
    back_act = ffn_out_back(second_bf, w_out)
    cumulative = 0.5 * (1.0 + jax.scipy.special.erf(pre_act * ROOT_HALF))
    density = jnp.exp(-0.5 * pre_act * pre_act) * INV_ROOT_TWO_PI
    grad_pre = back_act * (cumulative + pre_act * density)
    pre_bf = grad_pre.astype(jnp.bfloat16)
    grad_b_in = jnp.sum(grad_pre, axis=0)
    grad_middle = grad_second + jnp.dot(pre_bf, w_in.T, preferred_element_type=jnp.float32)
    grad_first, grad_gain_one, grad_shift_one = norm_backward(
        grad_middle, normed_one, inv_one, gain_one
    )
    grad_b_att = jnp.sum(grad_first, axis=0)
    first_bf = grad_first.astype(jnp.bfloat16)
    grad_context = (
        jnp.dot(first_bf, w_att.T, preferred_element_type=jnp.float32)
        .astype(jnp.bfloat16)
        .reshape(shape_heads)
    )
    scores = attention_scores(query_bf, key_bf, key_valid)
    probs = jnp.exp(scores - row_lse)
    grad_value = batched("bhqk,bqhe->bkhe", probs.astype(jnp.bfloat16), grad_context).reshape(
        -1, model_width
    )
    grad_probs = batched("bqhe,bkhe->bhqk", grad_context, value_bf)
    inner = jnp.sum(probs * grad_probs, axis=-1, keepdims=True)
    grad_scores = (probs * (grad_probs - inner) * (1.0 / math.sqrt(HEAD_DIM))).astype(jnp.bfloat16)
    grad_query = batched("bhqk,bkhe->bqhe", grad_scores, key_bf).reshape(-1, model_width)
    grad_key = batched("bhqk,bqhe->bkhe", grad_scores, query_bf).reshape(-1, model_width)
    grad_b_qv = jnp.stack([jnp.sum(grad_query, axis=0), jnp.sum(grad_value, axis=0)])
    packed_bf = jnp.concatenate([grad_query, grad_key, grad_value], axis=1).astype(jnp.bfloat16)
    grad_hidden = grad_first + jnp.dot(packed_bf, w_qkv.T, preferred_element_type=jnp.float32)
    terms = (
        (hidden_bf, packed_bf),
        grad_b_qv,
        (context_bf, first_bf),
        grad_b_att,
        grad_gain_one,
        grad_shift_one,
        (middle_bf, pre_bf),
        grad_b_in,
        (act_bf, second_bf),
        grad_b_out,
        grad_gain_two,
        grad_shift_two,
    )
    return (grad_hidden, terms)


SHARD_AXES = ("y", "xl", "z")
PAIR_AXES = ("xh", "core")


def pack_halves(w_qkv, w_att, w_in, w_out, small):
    rows = w_qkv.shape[0]
    split = w_qkv.shape[1]
    pad = jnp.zeros((rows, small.shape[1]), w_qkv.dtype)
    first = jnp.concatenate([w_qkv, w_in[:, :split], pad], axis=1)
    second = jnp.concatenate(
        [w_att, w_in[:, split:], w_out.reshape(rows, -1), small], axis=1
    )
    return first, second


def unpack_halves(first, second, width, ff):
    split = 3 * width
    w_qkv = first[:, :split]
    w_in = jnp.concatenate([first[:, split : 2 * split], second[:, width : width + ff - split]], axis=1)
    at = width + ff - split
    w_att = second[:, :width]
    w_out = second[:, at : at + ff]
    small = second[:, at + ff :]
    return w_qkv, w_att, w_in, w_out, small


def body(
    inputs,
    lengths,
    cotangent,
    w_qkv,
    b_qv,
    w_att,
    b_att,
    norm1_gain,
    norm1_bias,
    w_in,
    b_in,
    w_out,
    b_out,
    norm2_gain,
    norm2_bias,
):
    batch_size, seq_count, model_width = inputs.shape
    ff = w_in.shape[2]
    rows = w_qkv.shape[1]
    core = lax.axis_index("core")
    key_valid = lax.broadcasted_iota(jnp.int32, (batch_size, seq_count), 1) < lengths[:, None]
    hidden = inputs.astype(jnp.float32).reshape(-1, model_width)
    hidden_bf = inputs.reshape(-1, model_width)
    small = jnp.concatenate(
        [
            b_qv[0].T,
            b_att[0][:, None],
            norm1_gain[0][:, None],
            norm1_bias[0][:, None],
            b_out[0][:, None],
            norm2_gain[0][:, None],
            norm2_bias[0][:, None],
            b_in[0].reshape(rows, -1),
        ],
        axis=1,
    )
    first, second = pack_halves(w_qkv[0], w_att[0], group_columns(w_in[0], 4), w_out[0], small)
    mine = jnp.where(core == 0, first, second)
    gathered = lax.all_gather(mine, SHARD_AXES, axis=0, tiled=True)
    both = lax.all_gather(gathered, "core", axis=0, tiled=False)
    f_qkv, f_att, f_in, f_out, f_small = unpack_halves(both[0], both[1], model_width, ff)
    f_out = (both, 1, (model_width + ff - 3 * model_width) // model_width)
    f_bqv = f_small[:, 0:2].T
    f_bin = group_columns(f_small[:, 8:].reshape(1, ff), 4)[0]
    params = (
        f_qkv,
        f_bqv,
        f_att,
        f_small[:, 2],
        f_small[:, 3],
        f_small[:, 4],
        f_in,
        f_bin,
        f_out,
        f_small[:, 5],
        f_small[:, 6],
        f_small[:, 7],
    )
    hidden, stored = layer_forward(hidden, hidden_bf, params, key_valid, batch_size)
    outputs = hidden.astype(jnp.bfloat16).reshape(inputs.shape)
    upstream = cotangent.astype(jnp.float32).reshape(-1, model_width)
    upstream, terms = layer_backward(upstream, stored, params, key_valid)
    (g_qkv, g_bqv, g_att, g_batt, g_n1g, g_n1b, g_in, g_bin, g_out, g_bout, g_n2g, g_n2b) = terms
    g_small = jnp.concatenate(
        [
            g_bqv.T,
            g_batt[:, None],
            g_n1g[:, None],
            g_n1b[:, None],
            g_bout[:, None],
            g_n2g[:, None],
            g_n2b[:, None],
            ungroup_columns(g_bin[None], 4)[0].reshape(model_width, -1),
        ],
        axis=1,
    )
    tokens = g_qkv[0].shape[0]
    col = lambda b, c: b[:, c * model_width : (c + 1) * model_width]
    hi = g_small.astype(jnp.bfloat16)
    rest = g_small - hi.astype(jnp.float32)
    mid_part = rest.astype(jnp.bfloat16)
    low = (rest - mid_part.astype(jnp.float32)).astype(jnp.bfloat16)
    n_small = g_small.shape[1]
    pieces = jnp.concatenate([hi.T, mid_part.T, low.T], axis=0)
    enc_left = jnp.zeros((tokens, model_width), jnp.bfloat16).at[: 3 * n_small].set(pieces)
    picks = lax.broadcasted_iota(jnp.int32, (tokens, model_width), 1) == (
        lax.broadcasted_iota(jnp.int32, (tokens, model_width), 0) % n_small
    )
    rows_used = lax.broadcasted_iota(jnp.int32, (tokens, model_width), 0) < 3 * n_small
    enc_right = (picks & rows_used).astype(jnp.bfloat16)
    zero = jnp.zeros((tokens, model_width), jnp.bfloat16)
    lefts = [g_qkv[0]] * 3 + [g_in[0]] * 3
    lefts += [g_att[0], g_in[0]] + [col(g_out[0], j) for j in range(4)]
    rights = [col(g_qkv[1], c) for c in range(3)] + [col(g_in[1], c) for c in range(3)]
    rights += [g_att[1], col(g_in[1], 3)] + [g_out[1]] * 4
    narrow = model_width // 4
    split_left = [a for a in lefts for _ in range(4)]
    split_right = [b[:, q * narrow : (q + 1) * narrow] for b in rights for q in range(4)]
    at = len(split_left) // 2
    split_left = split_left[:at] + [zero] + split_left[at:] + [enc_left]
    split_right = split_right[:at] + [zero[:, :narrow]] + split_right[at:] + [enc_right[:, :narrow]]
    wgrads = jnp.einsum(
        "btk,btn->bkn",
        jnp.stack(split_left),
        jnp.stack(split_right),
        preferred_element_type=jnp.float32,
    ).reshape(2, len(split_left) // 2, model_width, narrow)
    half = lax.psum_scatter(wgrads.astype(jnp.bfloat16), "core", scatter_dimension=0, tiled=False)
    part = lax.psum_scatter(
        half.astype(jnp.float32), SHARD_AXES, scatter_dimension=1, tiled=True
    )
    part = lax.psum(part, "xh")
    res = lax.all_gather(part, "core", axis=0, tiled=False)
    r0, r1 = res[0], res[1]
    joined = lambda r: r.transpose(1, 0, 2).reshape(r.shape[1], -1)
    r_qkv = joined(r0[0:12])
    r_in = ungroup_columns(jnp.concatenate([joined(r0[12:24]), joined(r1[4:8])], axis=1), 4)
    r_att = joined(r1[0:4])
    r_out = jnp.stack([joined(r1[8 + 4 * j : 12 + 4 * j]) for j in range(4)], axis=1)
    r_small = r1[24][:, :n_small]
    grad_inputs = upstream.reshape(inputs.shape)
    return (
        outputs,
        grad_inputs,
        r_qkv[None],
        r_small[:, 0:2].T[None],
        r_att[None],
        r_small[:, 2][None],
        r_small[:, 3][None],
        r_small[:, 4][None],
        r_in[None],
        r_small[:, 8:].reshape(-1)[None],
        r_out.reshape(-1, model_width)[None],
        r_small[:, 5][None],
        r_small[:, 6][None],
        r_small[:, 7][None],
    )


def solution(mesh):
    devices = mesh.devices.reshape(2, 2, 4, 2, 4)
    fine = jax.sharding.Mesh(devices, ("xh", "core", "y", "xl", "z"))
    seqs = P(("xh", "core", "y", "xl", "z"), None, None)
    rows = P(None, SHARD_AXES, None)
    vec = P(None, SHARD_AXES)
    return jax.shard_map(
        body,
        mesh=fine,
        in_specs=(
            seqs,
            P(("xh", "core", "y", "xl", "z")),
            seqs,
            rows,
            P(None, None, SHARD_AXES),
            rows,
            vec,
            vec,
            vec,
            rows,
            vec,
            rows,
            vec,
            vec,
            vec,
        ),
        out_specs=(
            seqs,
            seqs,
            rows,
            P(None, None, SHARD_AXES),
            rows,
            vec,
            vec,
            vec,
            rows,
            vec,
            rows,
            vec,
            vec,
            vec,
        ),
        check_vma=False,
    )
```

```python
import math

import jax
import jax.numpy as jnp
from jax import lax
from jax.experimental import pallas as pl
from jax.experimental.pallas import tpu as pltpu
from jax.sharding import PartitionSpec as P

HEAD_DIM = 64
LAYERS = 1


EPS = 1e-12
ROOT_HALF = 0.7071067811865476
INV_ROOT_TWO_PI = 0.3989422804014327


def _ffn_out_kernel(act_ref, w_ref, out_ref):
    @pl.when(pl.program_id(0) == 0)
    def _():
        out_ref[...] = jnp.zeros_like(out_ref)

    out_ref[...] += jnp.dot(act_ref[...], w_ref[...], preferred_element_type=jnp.float32)


def ffn_out(act_grouped, w_out):
    buffer, which, first_block = w_out
    tokens = act_grouped.shape[0]
    width = buffer.shape[1]
    groups = act_grouped.shape[1] // width
    return pl.pallas_call(
        _ffn_out_kernel,
        grid=(groups,),
        in_specs=[
            pl.BlockSpec((tokens, width), lambda j: (0, j)),
            pl.BlockSpec((None, width, width), lambda j: (which, 0, first_block + j)),
        ],
        out_specs=pl.BlockSpec((tokens, width), lambda j: (0, 0)),
        out_shape=jax.ShapeDtypeStruct((tokens, width), jnp.float32),
        cost_estimate=pl.CostEstimate(
            flops=2 * tokens * width * width * groups,
            bytes_accessed=2 * width * width * groups + 2 * tokens * width * groups + 4 * tokens * width,
            transcendentals=0,
        ),
    )(act_grouped, buffer)


def _ffn_out_back_kernel(grad_ref, w_ref, out_ref):
    out_ref[...] = lax.dot_general(
        grad_ref[...],
        w_ref[...],
        (((1,), (1,)), ((), ())),
        preferred_element_type=jnp.float32,
    )


def ffn_out_back(grad_bf, w_out):
    buffer, which, first_block = w_out
    tokens = grad_bf.shape[0]
    width = buffer.shape[1]
    groups = 4
    return pl.pallas_call(
        _ffn_out_back_kernel,
        grid=(groups,),
        in_specs=[
            pl.BlockSpec((tokens, width), lambda j: (0, 0)),
            pl.BlockSpec((None, width, width), lambda j: (which, 0, first_block + j)),
        ],
        out_specs=pl.BlockSpec((tokens, width), lambda j: (0, j)),
        out_shape=jax.ShapeDtypeStruct((tokens, width * groups), jnp.float32),
        cost_estimate=pl.CostEstimate(
            flops=2 * tokens * width * width * groups,
            bytes_accessed=2 * width * width * groups + 2 * tokens * width + 4 * tokens * width * groups,
            transcendentals=0,
        ),
    )(grad_bf, buffer)


def _wgrad_kernel(left_ref, right_ref, out_ref):
    out_ref[...] = lax.dot_general(
        left_ref[...],
        right_ref[...],
        (((0,), (0,)), ((), ())),
        preferred_element_type=jnp.float32,
    ).astype(out_ref.dtype)


def weight_grads(lefts, rights):
    blocks, tokens, rows = lefts.shape
    cols = rights.shape[2]
    return pl.pallas_call(
        _wgrad_kernel,
        grid=(blocks,),
        in_specs=[
            pl.BlockSpec((None, tokens, rows), lambda b: (b, 0, 0)),
            pl.BlockSpec((None, tokens, cols), lambda b: (b, 0, 0)),
        ],
        out_specs=pl.BlockSpec((None, rows, cols), lambda b: (b, 0, 0)),
        out_shape=jax.ShapeDtypeStruct((blocks, rows, cols), jnp.bfloat16),
        cost_estimate=pl.CostEstimate(
            flops=2 * blocks * tokens * rows * cols,
            bytes_accessed=2 * blocks * (tokens * rows + tokens * cols + rows * cols),
            transcendentals=0,
        ),
    )(lefts, rights)

def group_columns(x, groups):
    tokens = x.shape[0]
    return x.reshape(tokens, -1, groups).transpose(0, 2, 1).reshape(tokens, -1)


def ungroup_columns(x, groups):
    tokens = x.shape[0]
    return x.reshape(tokens, groups, -1).transpose(0, 2, 1).reshape(tokens, -1)


def batched(form, left, right):
    return jnp.einsum(form, left, right, preferred_element_type=jnp.float32)


def layer_norm(residual, gain, shift):
    row_mean = jnp.mean(residual, axis=-1, keepdims=True)
    centered = residual - row_mean
    variance = jnp.mean(centered * centered, axis=-1, keepdims=True)
    inv_std = lax.rsqrt(variance + EPS)
    normed = centered * inv_std
    return (normed * gain.astype(jnp.float32) + shift.astype(jnp.float32), normed, inv_std)


def norm_backward(upstream, normed, inv_std, gain):
    grad_gain = jnp.sum(upstream * normed, axis=0)
    grad_shift = jnp.sum(upstream, axis=0)
    scaled = upstream * gain.astype(jnp.float32)
    grad_res = inv_std * (
        scaled
        - jnp.mean(scaled, axis=-1, keepdims=True)
        - normed * jnp.mean(scaled * normed, axis=-1, keepdims=True)
    )
    return (grad_res, grad_gain, grad_shift)


def attention_scores(query_bf, key_bf, key_valid):
    scores = batched("bqhe,bkhe->bhqk", query_bf, key_bf) * (1.0 / math.sqrt(HEAD_DIM))
    return jnp.where(key_valid[:, None, None, :], scores, -1e30)


def layer_forward(hidden, hidden_bf, params, key_valid, batch_size):
    (
        w_qkv,
        b_qv,
        w_att,
        b_att,
        gain_one,
        shift_one,
        w_in,
        b_in,
        w_out,
        b_out,
        gain_two,
        shift_two,
    ) = params
    model_width = hidden.shape[1]
    seq_count = hidden.shape[0] // batch_size
    shape_heads = (batch_size, seq_count, model_width // HEAD_DIM, HEAD_DIM)
    packed = jnp.dot(hidden_bf, w_qkv, preferred_element_type=jnp.float32)
    bias_qv = b_qv.astype(jnp.float32)
    query_bf = (packed[:, :model_width] + bias_qv[0]).astype(jnp.bfloat16).reshape(shape_heads)
    key_bf = packed[:, model_width : 2 * model_width].astype(jnp.bfloat16).reshape(shape_heads)
    value_bf = (packed[:, 2 * model_width :] + bias_qv[1]).astype(jnp.bfloat16).reshape(shape_heads)
    scores = attention_scores(query_bf, key_bf, key_valid)
    row_max = jnp.max(scores, axis=-1, keepdims=True)
    row_lse = row_max + jnp.log(jnp.sum(jnp.exp(scores - row_max), axis=-1, keepdims=True))
    probs_bf = jnp.exp(scores - row_lse).astype(jnp.bfloat16)
    context_bf = (
        batched("bhqk,bkhe->bqhe", probs_bf, value_bf).astype(jnp.bfloat16).reshape(-1, model_width)
    )
    first = (
        hidden
        + jnp.dot(context_bf, w_att, preferred_element_type=jnp.float32)
        + b_att.astype(jnp.float32)
    )
    middle, normed_one, inv_one = layer_norm(first, gain_one, shift_one)
    middle_bf = middle.astype(jnp.bfloat16)
    pre_act = jnp.dot(middle_bf, w_in, preferred_element_type=jnp.float32) + b_in.astype(
        jnp.float32
    )
    act_bf = (pre_act * 0.5 * (1.0 + jax.scipy.special.erf(pre_act * ROOT_HALF))).astype(
        jnp.bfloat16
    )
    second = (
        middle
        + ffn_out(act_bf, w_out)
        + b_out.astype(jnp.float32)
    )
    result, normed_two, inv_two = layer_norm(second, gain_two, shift_two)
    stored = (
        hidden_bf,
        query_bf,
        key_bf,
        value_bf,
        row_lse,
        context_bf,
        normed_one,
        inv_one,
        middle_bf,
        pre_act,
        act_bf,
        normed_two,
        inv_two,
    )
    return (result, stored)


def layer_backward(upstream, stored, params, key_valid):
    (
        w_qkv,
        b_qv,
        w_att,
        b_att,
        gain_one,
        shift_one,
        w_in,
        b_in,
        w_out,
        b_out,
        gain_two,
        shift_two,
    ) = params
    (
        hidden_bf,
        query_bf,
        key_bf,
        value_bf,
        row_lse,
        context_bf,
        normed_one,
        inv_one,
        middle_bf,
        pre_act,
        act_bf,
        normed_two,
        inv_two,
    ) = stored
    model_width = upstream.shape[1]
    shape_heads = query_bf.shape
    grad_second, grad_gain_two, grad_shift_two = norm_backward(
        upstream, normed_two, inv_two, gain_two
    )
    grad_b_out = jnp.sum(grad_second, axis=0)
    second_bf = grad_second.astype(jnp.bfloat16)
    back_act = ffn_out_back(second_bf, w_out)
    cumulative = 0.5 * (1.0 + jax.scipy.special.erf(pre_act * ROOT_HALF))
    density = jnp.exp(-0.5 * pre_act * pre_act) * INV_ROOT_TWO_PI
    grad_pre = back_act * (cumulative + pre_act * density)
    pre_bf = grad_pre.astype(jnp.bfloat16)
    grad_b_in = jnp.sum(grad_pre, axis=0)
    grad_middle = grad_second + jnp.dot(pre_bf, w_in.T, preferred_element_type=jnp.float32)
    grad_first, grad_gain_one, grad_shift_one = norm_backward(
        grad_middle, normed_one, inv_one, gain_one
    )
    grad_b_att = jnp.sum(grad_first, axis=0)
    first_bf = grad_first.astype(jnp.bfloat16)
    grad_context = (
        jnp.dot(first_bf, w_att.T, preferred_element_type=jnp.float32)
        .astype(jnp.bfloat16)
        .reshape(shape_heads)
    )
    scores = attention_scores(query_bf, key_bf, key_valid)
    probs = jnp.exp(scores - row_lse)
    grad_value = batched("bhqk,bqhe->bkhe", probs.astype(jnp.bfloat16), grad_context).reshape(
        -1, model_width
    )
    grad_probs = batched("bqhe,bkhe->bhqk", grad_context, value_bf)
    inner = jnp.sum(probs * grad_probs, axis=-1, keepdims=True)
    grad_scores = (probs * (grad_probs - inner) * (1.0 / math.sqrt(HEAD_DIM))).astype(jnp.bfloat16)
    grad_query = batched("bhqk,bkhe->bqhe", grad_scores, key_bf).reshape(-1, model_width)
    grad_key = batched("bhqk,bqhe->bkhe", grad_scores, query_bf).reshape(-1, model_width)
    grad_b_qv = jnp.stack([jnp.sum(grad_query, axis=0), jnp.sum(grad_value, axis=0)])
    packed_bf = jnp.concatenate([grad_query, grad_key, grad_value], axis=1).astype(jnp.bfloat16)
    grad_hidden = grad_first + jnp.dot(packed_bf, w_qkv.T, preferred_element_type=jnp.float32)
    terms = (
        (hidden_bf, packed_bf),
        grad_b_qv,
        (context_bf, first_bf),
        grad_b_att,
        grad_gain_one,
        grad_shift_one,
        (middle_bf, pre_bf),
        grad_b_in,
        (act_bf, second_bf),
        grad_b_out,
        grad_gain_two,
        grad_shift_two,
    )
    return (grad_hidden, terms)


SHARD_AXES = ("y", "xl", "z")
PAIR_AXES = ("xh", "core")


def pack_halves(w_qkv, w_att, w_in, w_out, small):
    rows = w_qkv.shape[0]
    split = w_qkv.shape[1]
    pad = jnp.zeros((rows, small.shape[1]), w_qkv.dtype)
    first = jnp.concatenate([w_qkv, w_in[:, :split], pad], axis=1)
    second = jnp.concatenate(
        [w_att, w_in[:, split:], w_out.reshape(rows, -1), small], axis=1
    )
    return first, second


def unpack_halves(first, second, width, ff):
    split = 3 * width
    w_qkv = first[:, :split]
    w_in = jnp.concatenate([first[:, split : 2 * split], second[:, width : width + ff - split]], axis=1)
    at = width + ff - split
    w_att = second[:, :width]
    w_out = second[:, at : at + ff]
    small = second[:, at + ff :]
    return w_qkv, w_att, w_in, w_out, small


def body(
    inputs,
    lengths,
    cotangent,
    w_qkv,
    b_qv,
    w_att,
    b_att,
    norm1_gain,
    norm1_bias,
    w_in,
    b_in,
    w_out,
    b_out,
    norm2_gain,
    norm2_bias,
):
    batch_size, seq_count, model_width = inputs.shape
    ff = w_in.shape[2]
    rows = w_qkv.shape[1]
    core = lax.axis_index("core")
    key_valid = lax.broadcasted_iota(jnp.int32, (batch_size, seq_count), 1) < lengths[:, None]
    hidden = inputs.astype(jnp.float32).reshape(-1, model_width)
    hidden_bf = inputs.reshape(-1, model_width)
    small = jnp.concatenate(
        [
            b_qv[0].T,
            b_att[0][:, None],
            norm1_gain[0][:, None],
            norm1_bias[0][:, None],
            b_out[0][:, None],
            norm2_gain[0][:, None],
            norm2_bias[0][:, None],
            b_in[0].reshape(rows, -1),
        ],
        axis=1,
    )
    first, second = pack_halves(w_qkv[0], w_att[0], group_columns(w_in[0], 4), w_out[0], small)
    mine = jnp.where(core == 0, first, second)
    gathered = lax.all_gather(mine, SHARD_AXES, axis=0, tiled=True)
    both = lax.all_gather(gathered, "core", axis=0, tiled=False)
    f_qkv, f_att, f_in, f_out, f_small = unpack_halves(both[0], both[1], model_width, ff)
    f_out = (both, 1, (model_width + ff - 3 * model_width) // model_width)
    f_bqv = f_small[:, 0:2].T
    f_bin = group_columns(f_small[:, 8:].reshape(1, ff), 4)[0]
    params = (
        f_qkv,
        f_bqv,
        f_att,
        f_small[:, 2],
        f_small[:, 3],
        f_small[:, 4],
        f_in,
        f_bin,
        f_out,
        f_small[:, 5],
        f_small[:, 6],
        f_small[:, 7],
    )
    hidden, stored = layer_forward(hidden, hidden_bf, params, key_valid, batch_size)
    outputs = hidden.astype(jnp.bfloat16).reshape(inputs.shape)
    upstream = cotangent.astype(jnp.float32).reshape(-1, model_width)
    upstream, terms = layer_backward(upstream, stored, params, key_valid)
    (g_qkv, g_bqv, g_att, g_batt, g_n1g, g_n1b, g_in, g_bin, g_out, g_bout, g_n2g, g_n2b) = terms
    g_small = jnp.concatenate(
        [
            g_bqv.T,
            g_batt[:, None],
            g_n1g[:, None],
            g_n1b[:, None],
            g_bout[:, None],
            g_n2g[:, None],
            g_n2b[:, None],
            ungroup_columns(g_bin[None], 4)[0].reshape(model_width, -1),
        ],
        axis=1,
    )
    tokens = g_qkv[0].shape[0]
    col = lambda b, c: b[:, c * model_width : (c + 1) * model_width]
    hi = g_small.astype(jnp.bfloat16)
    rest = g_small - hi.astype(jnp.float32)
    mid_part = rest.astype(jnp.bfloat16)
    low = (rest - mid_part.astype(jnp.float32)).astype(jnp.bfloat16)
    n_small = g_small.shape[1]
    pieces = jnp.concatenate([hi.T, mid_part.T, low.T], axis=0)
    enc_left = jnp.zeros((tokens, model_width), jnp.bfloat16).at[: 3 * n_small].set(pieces)
    picks = lax.broadcasted_iota(jnp.int32, (tokens, model_width), 1) == (
        lax.broadcasted_iota(jnp.int32, (tokens, model_width), 0) % n_small
    )
    rows_used = lax.broadcasted_iota(jnp.int32, (tokens, model_width), 0) < 3 * n_small
    enc_right = (picks & rows_used).astype(jnp.bfloat16)
    zero = jnp.zeros((tokens, model_width), jnp.bfloat16)
    lefts = [g_qkv[0]] * 3 + [g_in[0]] * 3 + [zero]
    lefts += [g_att[0], g_in[0]] + [col(g_out[0], j) for j in range(4)] + [enc_left]
    rights = [col(g_qkv[1], c) for c in range(3)] + [col(g_in[1], c) for c in range(3)] + [zero]
    rights += [g_att[1], col(g_in[1], 3)] + [g_out[1]] * 4 + [enc_right]
    wgrads = weight_grads(jnp.stack(lefts), jnp.stack(rights)).reshape(
        2, len(lefts) // 2, model_width, model_width
    )
    half = lax.psum_scatter(wgrads, "core", scatter_dimension=0, tiled=False)
    part = lax.psum_scatter(
        half.astype(jnp.float32), SHARD_AXES, scatter_dimension=1, tiled=True
    )
    part = lax.psum(part, "xh")
    res = lax.all_gather(part, "core", axis=0, tiled=False)
    r0, r1 = res[0], res[1]
    r_qkv = jnp.concatenate([r0[0], r0[1], r0[2]], axis=1)
    r_in = ungroup_columns(jnp.concatenate([r0[3], r0[4], r0[5], r1[1]], axis=1), 4)
    r_att = r1[0]
    r_out = jnp.stack([r1[2], r1[3], r1[4], r1[5]], axis=1)
    r_small = r1[6][:, :n_small]
    grad_inputs = upstream.reshape(inputs.shape)
    return (
        outputs,
        grad_inputs,
        r_qkv[None],
        r_small[:, 0:2].T[None],
        r_att[None],
        r_small[:, 2][None],
        r_small[:, 3][None],
        r_small[:, 4][None],
        r_in[None],
        r_small[:, 8:].reshape(-1)[None],
        r_out.reshape(-1, model_width)[None],
        r_small[:, 5][None],
        r_small[:, 6][None],
        r_small[:, 7][None],
    )


def solution(mesh):
    devices = mesh.devices.reshape(2, 2, 4, 2, 4)
    fine = jax.sharding.Mesh(devices, ("xh", "core", "y", "xl", "z"))
    seqs = P(("xh", "core", "y", "xl", "z"), None, None)
    rows = P(None, SHARD_AXES, None)
    vec = P(None, SHARD_AXES)
    return jax.shard_map(
        body,
        mesh=fine,
        in_specs=(
            seqs,
            P(("xh", "core", "y", "xl", "z")),
            seqs,
            rows,
            P(None, None, SHARD_AXES),
            rows,
            vec,
            vec,
            vec,
            rows,
            vec,
            rows,
            vec,
            vec,
            vec,
        ),
        out_specs=(
            seqs,
            seqs,
            rows,
            P(None, None, SHARD_AXES),
            rows,
            vec,
            vec,
            vec,
            rows,
            vec,
            rows,
            vec,
            vec,
            vec,
        ),
        check_vma=False,
    )
```

```python
import math

import jax
import jax.numpy as jnp
from jax import lax
from jax.experimental import pallas as pl
from jax.experimental.pallas import tpu as pltpu
from jax.sharding import PartitionSpec as P

HEAD_DIM = 64
LAYERS = 1


EPS = 1e-12
ROOT_HALF = 0.7071067811865476
INV_ROOT_TWO_PI = 0.3989422804014327


def _ffn_out_kernel(act_ref, w_ref, out_ref):
    @pl.when(pl.program_id(0) == 0)
    def _():
        out_ref[...] = jnp.zeros_like(out_ref)

    out_ref[...] += jnp.dot(act_ref[...], w_ref[...], preferred_element_type=jnp.float32)


def ffn_out(act_grouped, w_out):
    buffer, which, first_block = w_out
    tokens = act_grouped.shape[0]
    width = buffer.shape[1]
    groups = act_grouped.shape[1] // width
    return pl.pallas_call(
        _ffn_out_kernel,
        grid=(groups,),
        in_specs=[
            pl.BlockSpec((tokens, width), lambda j: (0, j)),
            pl.BlockSpec((None, width, width), lambda j: (which, 0, first_block + j)),
        ],
        out_specs=pl.BlockSpec((tokens, width), lambda j: (0, 0)),
        out_shape=jax.ShapeDtypeStruct((tokens, width), jnp.float32),
        cost_estimate=pl.CostEstimate(
            flops=2 * tokens * width * width * groups,
            bytes_accessed=2 * width * width * groups + 2 * tokens * width * groups + 4 * tokens * width,
            transcendentals=0,
        ),
    )(act_grouped, buffer)


def _ffn_out_back_kernel(grad_ref, w_ref, out_ref):
    out_ref[...] = lax.dot_general(
        grad_ref[...],
        w_ref[...],
        (((1,), (1,)), ((), ())),
        preferred_element_type=jnp.float32,
    )


def ffn_out_back(grad_bf, w_out):
    buffer, which, first_block = w_out
    tokens = grad_bf.shape[0]
    width = buffer.shape[1]
    groups = 4
    return pl.pallas_call(
        _ffn_out_back_kernel,
        grid=(groups,),
        in_specs=[
            pl.BlockSpec((tokens, width), lambda j: (0, 0)),
            pl.BlockSpec((None, width, width), lambda j: (which, 0, first_block + j)),
        ],
        out_specs=pl.BlockSpec((tokens, width), lambda j: (0, j)),
        out_shape=jax.ShapeDtypeStruct((tokens, width * groups), jnp.float32),
        cost_estimate=pl.CostEstimate(
            flops=2 * tokens * width * width * groups,
            bytes_accessed=2 * width * width * groups + 2 * tokens * width + 4 * tokens * width * groups,
            transcendentals=0,
        ),
    )(grad_bf, buffer)


def group_columns(x, groups):
    tokens = x.shape[0]
    return x.reshape(tokens, -1, groups).transpose(0, 2, 1).reshape(tokens, -1)


def ungroup_columns(x, groups):
    tokens = x.shape[0]
    return x.reshape(tokens, groups, -1).transpose(0, 2, 1).reshape(tokens, -1)


def batched(form, left, right):
    return jnp.einsum(form, left, right, preferred_element_type=jnp.float32)


def layer_norm(residual, gain, shift):
    row_mean = jnp.mean(residual, axis=-1, keepdims=True)
    centered = residual - row_mean
    variance = jnp.mean(centered * centered, axis=-1, keepdims=True)
    inv_std = lax.rsqrt(variance + EPS)
    normed = centered * inv_std
    return (normed * gain.astype(jnp.float32) + shift.astype(jnp.float32), normed, inv_std)


def norm_backward(upstream, normed, inv_std, gain):
    grad_gain = jnp.sum(upstream * normed, axis=0)
    grad_shift = jnp.sum(upstream, axis=0)
    scaled = upstream * gain.astype(jnp.float32)
    grad_res = inv_std * (
        scaled
        - jnp.mean(scaled, axis=-1, keepdims=True)
        - normed * jnp.mean(scaled * normed, axis=-1, keepdims=True)
    )
    return (grad_res, grad_gain, grad_shift)


def attention_scores(query_bf, key_bf, key_valid):
    scores = batched("bqhe,bkhe->bhqk", query_bf, key_bf) * (1.0 / math.sqrt(HEAD_DIM))
    return jnp.where(key_valid[:, None, None, :], scores, -1e30)


def layer_forward(hidden, hidden_bf, params, key_valid, batch_size):
    (
        w_qkv,
        b_qv,
        w_att,
        b_att,
        gain_one,
        shift_one,
        w_in,
        b_in,
        w_out,
        b_out,
        gain_two,
        shift_two,
    ) = params
    model_width = hidden.shape[1]
    seq_count = hidden.shape[0] // batch_size
    shape_heads = (batch_size, seq_count, model_width // HEAD_DIM, HEAD_DIM)
    packed = jnp.dot(hidden_bf, w_qkv, preferred_element_type=jnp.float32)
    bias_qv = b_qv.astype(jnp.float32)
    query_bf = (packed[:, :model_width] + bias_qv[0]).astype(jnp.bfloat16).reshape(shape_heads)
    key_bf = packed[:, model_width : 2 * model_width].astype(jnp.bfloat16).reshape(shape_heads)
    value_bf = (packed[:, 2 * model_width :] + bias_qv[1]).astype(jnp.bfloat16).reshape(shape_heads)
    scores = attention_scores(query_bf, key_bf, key_valid)
    row_max = jnp.max(scores, axis=-1, keepdims=True)
    row_lse = row_max + jnp.log(jnp.sum(jnp.exp(scores - row_max), axis=-1, keepdims=True))
    probs_bf = jnp.exp(scores - row_lse).astype(jnp.bfloat16)
    context_bf = (
        batched("bhqk,bkhe->bqhe", probs_bf, value_bf).astype(jnp.bfloat16).reshape(-1, model_width)
    )
    first = (
        hidden
        + jnp.dot(context_bf, w_att, preferred_element_type=jnp.float32)
        + b_att.astype(jnp.float32)
    )
    middle, normed_one, inv_one = layer_norm(first, gain_one, shift_one)
    middle_bf = middle.astype(jnp.bfloat16)
    pre_act = jnp.dot(middle_bf, w_in, preferred_element_type=jnp.float32) + b_in.astype(
        jnp.float32
    )
    act_bf = (pre_act * 0.5 * (1.0 + jax.scipy.special.erf(pre_act * ROOT_HALF))).astype(
        jnp.bfloat16
    )
    second = (
        middle
        + ffn_out(act_bf, w_out)
        + b_out.astype(jnp.float32)
    )
    result, normed_two, inv_two = layer_norm(second, gain_two, shift_two)
    stored = (
        hidden_bf,
        query_bf,
        key_bf,
        value_bf,
        row_lse,
        context_bf,
        normed_one,
        inv_one,
        middle_bf,
        pre_act,
        act_bf,
        normed_two,
        inv_two,
    )
    return (result, stored)


def layer_backward(upstream, stored, params, key_valid):
    (
        w_qkv,
        b_qv,
        w_att,
        b_att,
        gain_one,
        shift_one,
        w_in,
        b_in,
        w_out,
        b_out,
        gain_two,
        shift_two,
    ) = params
    (
        hidden_bf,
        query_bf,
        key_bf,
        value_bf,
        row_lse,
        context_bf,
        normed_one,
        inv_one,
        middle_bf,
        pre_act,
        act_bf,
        normed_two,
        inv_two,
    ) = stored
    model_width = upstream.shape[1]
    shape_heads = query_bf.shape
    grad_second, grad_gain_two, grad_shift_two = norm_backward(
        upstream, normed_two, inv_two, gain_two
    )
    grad_b_out = jnp.sum(grad_second, axis=0)
    second_bf = grad_second.astype(jnp.bfloat16)
    back_act = ffn_out_back(second_bf, w_out)
    cumulative = 0.5 * (1.0 + jax.scipy.special.erf(pre_act * ROOT_HALF))
    density = jnp.exp(-0.5 * pre_act * pre_act) * INV_ROOT_TWO_PI
    grad_pre = back_act * (cumulative + pre_act * density)
    pre_bf = grad_pre.astype(jnp.bfloat16)
    grad_b_in = jnp.sum(grad_pre, axis=0)
    grad_middle = grad_second + jnp.dot(pre_bf, w_in.T, preferred_element_type=jnp.float32)
    grad_first, grad_gain_one, grad_shift_one = norm_backward(
        grad_middle, normed_one, inv_one, gain_one
    )
    grad_b_att = jnp.sum(grad_first, axis=0)
    first_bf = grad_first.astype(jnp.bfloat16)
    grad_context = (
        jnp.dot(first_bf, w_att.T, preferred_element_type=jnp.float32)
        .astype(jnp.bfloat16)
        .reshape(shape_heads)
    )
    scores = attention_scores(query_bf, key_bf, key_valid)
    probs = jnp.exp(scores - row_lse)
    grad_value = batched("bhqk,bqhe->bkhe", probs.astype(jnp.bfloat16), grad_context).reshape(
        -1, model_width
    )
    grad_probs = batched("bqhe,bkhe->bhqk", grad_context, value_bf)
    inner = jnp.sum(probs * grad_probs, axis=-1, keepdims=True)
    grad_scores = (probs * (grad_probs - inner) * (1.0 / math.sqrt(HEAD_DIM))).astype(jnp.bfloat16)
    grad_query = batched("bhqk,bkhe->bqhe", grad_scores, key_bf).reshape(-1, model_width)
    grad_key = batched("bhqk,bqhe->bkhe", grad_scores, query_bf).reshape(-1, model_width)
    grad_b_qv = jnp.stack([jnp.sum(grad_query, axis=0), jnp.sum(grad_value, axis=0)])
    packed_bf = jnp.concatenate([grad_query, grad_key, grad_value], axis=1).astype(jnp.bfloat16)
    grad_hidden = grad_first + jnp.dot(packed_bf, w_qkv.T, preferred_element_type=jnp.float32)
    terms = (
        (hidden_bf, packed_bf),
        grad_b_qv,
        (context_bf, first_bf),
        grad_b_att,
        grad_gain_one,
        grad_shift_one,
        (middle_bf, pre_bf),
        grad_b_in,
        (act_bf, second_bf),
        grad_b_out,
        grad_gain_two,
        grad_shift_two,
    )
    return (grad_hidden, terms)


SHARD_AXES = ("y", "xl", "z")
PAIR_AXES = ("xh", "core")


def pack_halves(w_qkv, w_att, w_in, w_out, small):
    rows = w_qkv.shape[0]
    split = w_qkv.shape[1]
    pad = jnp.zeros((rows, small.shape[1]), w_qkv.dtype)
    first = jnp.concatenate([w_qkv, w_in[:, :split], pad], axis=1)
    second = jnp.concatenate(
        [w_att, w_in[:, split:], w_out.reshape(rows, -1), small], axis=1
    )
    return first, second


def unpack_halves(first, second, width, ff):
    split = 3 * width
    w_qkv = first[:, :split]
    w_in = jnp.concatenate([first[:, split : 2 * split], second[:, width : width + ff - split]], axis=1)
    at = width + ff - split
    w_att = second[:, :width]
    w_out = second[:, at : at + ff]
    small = second[:, at + ff :]
    return w_qkv, w_att, w_in, w_out, small


def body(
    inputs,
    lengths,
    cotangent,
    w_qkv,
    b_qv,
    w_att,
    b_att,
    norm1_gain,
    norm1_bias,
    w_in,
    b_in,
    w_out,
    b_out,
    norm2_gain,
    norm2_bias,
):
    batch_size, seq_count, model_width = inputs.shape
    ff = w_in.shape[2]
    rows = w_qkv.shape[1]
    core = lax.axis_index("core")
    key_valid = lax.broadcasted_iota(jnp.int32, (batch_size, seq_count), 1) < lengths[:, None]
    hidden = inputs.astype(jnp.float32).reshape(-1, model_width)
    hidden_bf = inputs.reshape(-1, model_width)
    small = jnp.concatenate(
        [
            b_qv[0].T,
            b_att[0][:, None],
            norm1_gain[0][:, None],
            norm1_bias[0][:, None],
            b_out[0][:, None],
            norm2_gain[0][:, None],
            norm2_bias[0][:, None],
            b_in[0].reshape(rows, -1),
        ],
        axis=1,
    )
    first, second = pack_halves(w_qkv[0], w_att[0], group_columns(w_in[0], 4), w_out[0], small)
    mine = jnp.where(core == 0, first, second)
    gathered = lax.all_gather(mine, SHARD_AXES, axis=0, tiled=True)
    both = lax.all_gather(gathered, "core", axis=0, tiled=False)
    f_qkv, f_att, f_in, f_out, f_small = unpack_halves(both[0], both[1], model_width, ff)
    f_out = (both, 1, (model_width + ff - 3 * model_width) // model_width)
    f_bqv = f_small[:, 0:2].T
    f_bin = group_columns(f_small[:, 8:].reshape(1, ff), 4)[0]
    params = (
        f_qkv,
        f_bqv,
        f_att,
        f_small[:, 2],
        f_small[:, 3],
        f_small[:, 4],
        f_in,
        f_bin,
        f_out,
        f_small[:, 5],
        f_small[:, 6],
        f_small[:, 7],
    )
    hidden, stored = layer_forward(hidden, hidden_bf, params, key_valid, batch_size)
    outputs = hidden.astype(jnp.bfloat16).reshape(inputs.shape)
    upstream = cotangent.astype(jnp.float32).reshape(-1, model_width)
    upstream, terms = layer_backward(upstream, stored, params, key_valid)
    (g_qkv, g_bqv, g_att, g_batt, g_n1g, g_n1b, g_in, g_bin, g_out, g_bout, g_n2g, g_n2b) = terms
    g_small = jnp.concatenate(
        [
            g_bqv.T,
            g_batt[:, None],
            g_n1g[:, None],
            g_n1b[:, None],
            g_bout[:, None],
            g_n2g[:, None],
            g_n2b[:, None],
            ungroup_columns(g_bin[None], 4)[0].reshape(model_width, -1),
        ],
        axis=1,
    )
    tokens = g_qkv[0].shape[0]
    col = lambda b, c: b[:, c * model_width : (c + 1) * model_width]
    hi = g_small.astype(jnp.bfloat16)
    rest = g_small - hi.astype(jnp.float32)
    mid_part = rest.astype(jnp.bfloat16)
    low = (rest - mid_part.astype(jnp.float32)).astype(jnp.bfloat16)
    n_small = g_small.shape[1]
    pieces = jnp.concatenate([hi.T, mid_part.T, low.T], axis=0)
    enc_left = jnp.zeros((tokens, model_width), jnp.bfloat16).at[: 3 * n_small].set(pieces)
    picks = lax.broadcasted_iota(jnp.int32, (tokens, model_width), 1) == (
        lax.broadcasted_iota(jnp.int32, (tokens, model_width), 0) % n_small
    )
    rows_used = lax.broadcasted_iota(jnp.int32, (tokens, model_width), 0) < 3 * n_small
    enc_right = (picks & rows_used).astype(jnp.bfloat16)
    zero = jnp.zeros((tokens, model_width), jnp.bfloat16)
    lefts = [g_qkv[0]] * 3 + [g_in[0]] * 3 + [zero]
    lefts += [g_att[0], g_in[0]] + [col(g_out[0], j) for j in range(4)] + [enc_left]
    rights = [col(g_qkv[1], c) for c in range(3)] + [col(g_in[1], c) for c in range(3)] + [zero]
    rights += [g_att[1], col(g_in[1], 3)] + [g_out[1]] * 4 + [enc_right]
    per_half = len(lefts) // 2
    stacked_left = jnp.stack(lefts).reshape(2, per_half, tokens, model_width)
    stacked_right = jnp.stack(rights).reshape(2, per_half, tokens, model_width)
    mine_first = core == 0

    def products(pick_first):
        left = jnp.where(pick_first, stacked_left[0], stacked_left[1])
        right = jnp.where(pick_first, stacked_right[0], stacked_right[1])
        return jnp.einsum("btk,btn->bkn", left, right, preferred_element_type=jnp.float32)

    kept = products(mine_first)
    sent = products(jnp.logical_not(mine_first)).astype(jnp.bfloat16)
    half = kept + lax.ppermute(sent, "core", perm=[(0, 1), (1, 0)]).astype(jnp.float32)
    part = lax.psum_scatter(half, SHARD_AXES, scatter_dimension=1, tiled=True)
    part = lax.psum(part, "xh")
    res = lax.all_gather(part, "core", axis=0, tiled=False)
    r0, r1 = res[0], res[1]
    r_qkv = jnp.concatenate([r0[0], r0[1], r0[2]], axis=1)
    r_in = ungroup_columns(jnp.concatenate([r0[3], r0[4], r0[5], r1[1]], axis=1), 4)
    r_att = r1[0]
    r_out = jnp.stack([r1[2], r1[3], r1[4], r1[5]], axis=1)
    r_small = r1[6][:, :n_small]
    grad_inputs = upstream.reshape(inputs.shape)
    return (
        outputs,
        grad_inputs,
        r_qkv[None],
        r_small[:, 0:2].T[None],
        r_att[None],
        r_small[:, 2][None],
        r_small[:, 3][None],
        r_small[:, 4][None],
        r_in[None],
        r_small[:, 8:].reshape(-1)[None],
        r_out.reshape(-1, model_width)[None],
        r_small[:, 5][None],
        r_small[:, 6][None],
        r_small[:, 7][None],
    )


def solution(mesh):
    devices = mesh.devices.reshape(2, 2, 4, 2, 4)
    fine = jax.sharding.Mesh(devices, ("xh", "core", "y", "xl", "z"))
    seqs = P(("xh", "core", "y", "xl", "z"), None, None)
    rows = P(None, SHARD_AXES, None)
    vec = P(None, SHARD_AXES)
    return jax.shard_map(
        body,
        mesh=fine,
        in_specs=(
            seqs,
            P(("xh", "core", "y", "xl", "z")),
            seqs,
            rows,
            P(None, None, SHARD_AXES),
            rows,
            vec,
            vec,
            vec,
            rows,
            vec,
            rows,
            vec,
            vec,
            vec,
        ),
        out_specs=(
            seqs,
            seqs,
            rows,
            P(None, None, SHARD_AXES),
            rows,
            vec,
            vec,
            vec,
            rows,
            vec,
            rows,
            vec,
            vec,
            vec,
        ),
        check_vma=False,
    )
```

```python
import math

import jax
import jax.numpy as jnp
from jax import lax
from jax.experimental import pallas as pl
from jax.experimental.pallas import tpu as pltpu
from jax.sharding import PartitionSpec as P

HEAD_DIM = 64
LAYERS = 1


EPS = 1e-12
ROOT_HALF = 0.7071067811865476
INV_ROOT_TWO_PI = 0.3989422804014327


def _ffn_out_kernel(act_ref, w_ref, out_ref):
    @pl.when(pl.program_id(0) == 0)
    def _():
        out_ref[...] = jnp.zeros_like(out_ref)

    out_ref[...] += jnp.dot(act_ref[...], w_ref[...], preferred_element_type=jnp.float32)


def ffn_out(act_grouped, w_out):
    buffer, which, first_block = w_out
    tokens = act_grouped.shape[0]
    width = buffer.shape[1]
    groups = act_grouped.shape[1] // width
    return pl.pallas_call(
        _ffn_out_kernel,
        grid=(groups,),
        in_specs=[
            pl.BlockSpec((tokens, width), lambda j: (0, j)),
            pl.BlockSpec((None, width, width), lambda j: (which, 0, first_block + j)),
        ],
        out_specs=pl.BlockSpec((tokens, width), lambda j: (0, 0)),
        out_shape=jax.ShapeDtypeStruct((tokens, width), jnp.float32),
        cost_estimate=pl.CostEstimate(
            flops=2 * tokens * width * width * groups,
            bytes_accessed=2 * width * width * groups + 2 * tokens * width * groups + 4 * tokens * width,
            transcendentals=0,
        ),
    )(act_grouped, buffer)


def _ffn_out_back_kernel(grad_ref, w_ref, out_ref):
    out_ref[...] = lax.dot_general(
        grad_ref[...],
        w_ref[...],
        (((1,), (1,)), ((), ())),
        preferred_element_type=jnp.float32,
    )


def ffn_out_back(grad_bf, w_out):
    buffer, which, first_block = w_out
    tokens = grad_bf.shape[0]
    width = buffer.shape[1]
    groups = 4
    return pl.pallas_call(
        _ffn_out_back_kernel,
        grid=(groups,),
        in_specs=[
            pl.BlockSpec((tokens, width), lambda j: (0, 0)),
            pl.BlockSpec((None, width, width), lambda j: (which, 0, first_block + j)),
        ],
        out_specs=pl.BlockSpec((tokens, width), lambda j: (0, j)),
        out_shape=jax.ShapeDtypeStruct((tokens, width * groups), jnp.float32),
        cost_estimate=pl.CostEstimate(
            flops=2 * tokens * width * width * groups,
            bytes_accessed=2 * width * width * groups + 2 * tokens * width + 4 * tokens * width * groups,
            transcendentals=0,
        ),
    )(grad_bf, buffer)


def group_columns(x, groups):
    tokens = x.shape[0]
    return x.reshape(tokens, -1, groups).transpose(0, 2, 1).reshape(tokens, -1)


def ungroup_columns(x, groups):
    tokens = x.shape[0]
    return x.reshape(tokens, groups, -1).transpose(0, 2, 1).reshape(tokens, -1)


def batched(form, left, right):
    return jnp.einsum(form, left, right, preferred_element_type=jnp.float32)


def layer_norm(residual, gain, shift):
    row_mean = jnp.mean(residual, axis=-1, keepdims=True)
    centered = residual - row_mean
    variance = jnp.mean(centered * centered, axis=-1, keepdims=True)
    inv_std = lax.rsqrt(variance + EPS)
    normed = centered * inv_std
    return (normed * gain.astype(jnp.float32) + shift.astype(jnp.float32), normed, inv_std)


def norm_backward(upstream, normed, inv_std, gain):
    grad_gain = jnp.sum(upstream * normed, axis=0)
    grad_shift = jnp.sum(upstream, axis=0)
    scaled = upstream * gain.astype(jnp.float32)
    grad_res = inv_std * (
        scaled
        - jnp.mean(scaled, axis=-1, keepdims=True)
        - normed * jnp.mean(scaled * normed, axis=-1, keepdims=True)
    )
    return (grad_res, grad_gain, grad_shift)


def attention_scores(query_bf, key_bf, key_valid):
    scores = batched("bqhe,bkhe->bhqk", query_bf, key_bf) * (1.0 / math.sqrt(HEAD_DIM))
    return jnp.where(key_valid[:, None, None, :], scores, -1e30)


def layer_forward(hidden, hidden_bf, params, key_valid, batch_size):
    (
        w_qkv,
        b_qv,
        w_att,
        b_att,
        gain_one,
        shift_one,
        w_in,
        b_in,
        w_out,
        b_out,
        gain_two,
        shift_two,
    ) = params
    model_width = hidden.shape[1]
    seq_count = hidden.shape[0] // batch_size
    shape_heads = (batch_size, seq_count, model_width // HEAD_DIM, HEAD_DIM)
    packed = jnp.dot(hidden_bf, w_qkv, preferred_element_type=jnp.float32)
    bias_qv = b_qv.astype(jnp.float32)
    query_bf = (packed[:, :model_width] + bias_qv[0]).astype(jnp.bfloat16).reshape(shape_heads)
    key_bf = packed[:, model_width : 2 * model_width].astype(jnp.bfloat16).reshape(shape_heads)
    value_bf = (packed[:, 2 * model_width :] + bias_qv[1]).astype(jnp.bfloat16).reshape(shape_heads)
    scores = attention_scores(query_bf, key_bf, key_valid)
    row_max = jnp.max(scores, axis=-1, keepdims=True)
    row_lse = row_max + jnp.log(jnp.sum(jnp.exp(scores - row_max), axis=-1, keepdims=True))
    probs_bf = jnp.exp(scores - row_lse).astype(jnp.bfloat16)
    context_bf = (
        batched("bhqk,bkhe->bqhe", probs_bf, value_bf).astype(jnp.bfloat16).reshape(-1, model_width)
    )
    first = (
        hidden
        + jnp.dot(context_bf, w_att, preferred_element_type=jnp.float32)
        + b_att.astype(jnp.float32)
    )
    middle, normed_one, inv_one = layer_norm(first, gain_one, shift_one)
    middle_bf = middle.astype(jnp.bfloat16)
    pre_act = jnp.dot(middle_bf, w_in, preferred_element_type=jnp.float32) + b_in.astype(
        jnp.float32
    )
    act_bf = (pre_act * 0.5 * (1.0 + jax.scipy.special.erf(pre_act * ROOT_HALF))).astype(
        jnp.bfloat16
    )
    second = (
        middle
        + ffn_out(act_bf, w_out)
        + b_out.astype(jnp.float32)
    )
    result, normed_two, inv_two = layer_norm(second, gain_two, shift_two)
    stored = (
        hidden_bf,
        query_bf,
        key_bf,
        value_bf,
        row_lse,
        context_bf,
        normed_one,
        inv_one,
        middle_bf,
        pre_act,
        act_bf,
        normed_two,
        inv_two,
    )
    return (result, stored)


def layer_backward(upstream, stored, params, key_valid):
    (
        w_qkv,
        b_qv,
        w_att,
        b_att,
        gain_one,
        shift_one,
        w_in,
        b_in,
        w_out,
        b_out,
        gain_two,
        shift_two,
    ) = params
    (
        hidden_bf,
        query_bf,
        key_bf,
        value_bf,
        row_lse,
        context_bf,
        normed_one,
        inv_one,
        middle_bf,
        pre_act,
        act_bf,
        normed_two,
        inv_two,
    ) = stored
    model_width = upstream.shape[1]
    shape_heads = query_bf.shape
    grad_second, grad_gain_two, grad_shift_two = norm_backward(
        upstream, normed_two, inv_two, gain_two
    )
    grad_b_out = jnp.sum(grad_second, axis=0)
    second_bf = grad_second.astype(jnp.bfloat16)
    back_act = ffn_out_back(second_bf, w_out)
    cumulative = 0.5 * (1.0 + jax.scipy.special.erf(pre_act * ROOT_HALF))
    density = jnp.exp(-0.5 * pre_act * pre_act) * INV_ROOT_TWO_PI
    grad_pre = back_act * (cumulative + pre_act * density)
    pre_bf = grad_pre.astype(jnp.bfloat16)
    grad_b_in = jnp.sum(grad_pre, axis=0)
    grad_middle = grad_second + jnp.dot(pre_bf, w_in.T, preferred_element_type=jnp.float32)
    grad_first, grad_gain_one, grad_shift_one = norm_backward(
        grad_middle, normed_one, inv_one, gain_one
    )
    grad_b_att = jnp.sum(grad_first, axis=0)
    first_bf = grad_first.astype(jnp.bfloat16)
    grad_context = (
        jnp.dot(first_bf, w_att.T, preferred_element_type=jnp.float32)
        .astype(jnp.bfloat16)
        .reshape(shape_heads)
    )
    scores = attention_scores(query_bf, key_bf, key_valid)
    probs = jnp.exp(scores - row_lse)
    grad_value = batched("bhqk,bqhe->bkhe", probs.astype(jnp.bfloat16), grad_context).reshape(
        -1, model_width
    )
    grad_probs = batched("bqhe,bkhe->bhqk", grad_context, value_bf)
    inner = jnp.sum(probs * grad_probs, axis=-1, keepdims=True)
    grad_scores = (probs * (grad_probs - inner) * (1.0 / math.sqrt(HEAD_DIM))).astype(jnp.bfloat16)
    grad_query = batched("bhqk,bkhe->bqhe", grad_scores, key_bf).reshape(-1, model_width)
    grad_key = batched("bhqk,bqhe->bkhe", grad_scores, query_bf).reshape(-1, model_width)
    grad_b_qv = jnp.stack([jnp.sum(grad_query, axis=0), jnp.sum(grad_value, axis=0)])
    packed_bf = jnp.concatenate([grad_query, grad_key, grad_value], axis=1).astype(jnp.bfloat16)
    grad_hidden = grad_first + jnp.dot(packed_bf, w_qkv.T, preferred_element_type=jnp.float32)
    terms = (
        (hidden_bf, packed_bf),
        grad_b_qv,
        (context_bf, first_bf),
        grad_b_att,
        grad_gain_one,
        grad_shift_one,
        (middle_bf, pre_bf),
        grad_b_in,
        (act_bf, second_bf),
        grad_b_out,
        grad_gain_two,
        grad_shift_two,
    )
    return (grad_hidden, terms)


SHARD_AXES = ("y", "xl", "z")
PAIR_AXES = ("xh", "core")


def pack_halves(w_qkv, w_att, w_in, w_out, small):
    rows = w_qkv.shape[0]
    split = w_qkv.shape[1]
    pad = jnp.zeros((rows, small.shape[1]), w_qkv.dtype)
    first = jnp.concatenate([w_qkv, w_in[:, :split], pad], axis=1)
    second = jnp.concatenate(
        [w_att, w_in[:, split:], w_out.reshape(rows, -1), small], axis=1
    )
    return first, second


def unpack_halves(first, second, width, ff):
    split = 3 * width
    w_qkv = first[:, :split]
    w_in = jnp.concatenate([first[:, split : 2 * split], second[:, width : width + ff - split]], axis=1)
    at = width + ff - split
    w_att = second[:, :width]
    w_out = second[:, at : at + ff]
    small = second[:, at + ff :]
    return w_qkv, w_att, w_in, w_out, small


def body(
    inputs,
    lengths,
    cotangent,
    w_qkv,
    b_qv,
    w_att,
    b_att,
    norm1_gain,
    norm1_bias,
    w_in,
    b_in,
    w_out,
    b_out,
    norm2_gain,
    norm2_bias,
):
    batch_size, seq_count, model_width = inputs.shape
    ff = w_in.shape[2]
    rows = w_qkv.shape[1]
    core = lax.axis_index("core")
    key_valid = lax.broadcasted_iota(jnp.int32, (batch_size, seq_count), 1) < lengths[:, None]
    hidden = inputs.astype(jnp.float32).reshape(-1, model_width)
    hidden_bf = inputs.reshape(-1, model_width)
    small = jnp.concatenate(
        [
            b_qv[0].T,
            b_att[0][:, None],
            norm1_gain[0][:, None],
            norm1_bias[0][:, None],
            b_out[0][:, None],
            norm2_gain[0][:, None],
            norm2_bias[0][:, None],
            b_in[0].reshape(rows, -1),
        ],
        axis=1,
    )
    first, second = pack_halves(w_qkv[0], w_att[0], group_columns(w_in[0], 4), w_out[0], small)
    mine = jnp.where(core == 0, first, second)
    gathered = lax.all_gather(mine, SHARD_AXES, axis=0, tiled=True)
    other = lax.ppermute(gathered, "core", perm=[(0, 1), (1, 0)])
    first_all = jnp.where(core == 0, gathered, other)
    second_all = jnp.where(core == 0, other, gathered)
    f_qkv, f_att, f_in, f_out, f_small = unpack_halves(first_all, second_all, model_width, ff)
    f_out = (second_all[None], 0, (model_width + ff - 3 * model_width) // model_width)
    f_bqv = f_small[:, 0:2].T
    f_bin = group_columns(f_small[:, 8:].reshape(1, ff), 4)[0]
    params = (
        f_qkv,
        f_bqv,
        f_att,
        f_small[:, 2],
        f_small[:, 3],
        f_small[:, 4],
        f_in,
        f_bin,
        f_out,
        f_small[:, 5],
        f_small[:, 6],
        f_small[:, 7],
    )
    hidden, stored = layer_forward(hidden, hidden_bf, params, key_valid, batch_size)
    outputs = hidden.astype(jnp.bfloat16).reshape(inputs.shape)
    upstream = cotangent.astype(jnp.float32).reshape(-1, model_width)
    upstream, terms = layer_backward(upstream, stored, params, key_valid)
    (g_qkv, g_bqv, g_att, g_batt, g_n1g, g_n1b, g_in, g_bin, g_out, g_bout, g_n2g, g_n2b) = terms
    g_small = jnp.concatenate(
        [
            g_bqv.T,
            g_batt[:, None],
            g_n1g[:, None],
            g_n1b[:, None],
            g_bout[:, None],
            g_n2g[:, None],
            g_n2b[:, None],
            ungroup_columns(g_bin[None], 4)[0].reshape(model_width, -1),
        ],
        axis=1,
    )
    tokens = g_qkv[0].shape[0]
    col = lambda b, c: b[:, c * model_width : (c + 1) * model_width]
    hi = g_small.astype(jnp.bfloat16)
    rest = g_small - hi.astype(jnp.float32)
    mid_part = rest.astype(jnp.bfloat16)
    low = (rest - mid_part.astype(jnp.float32)).astype(jnp.bfloat16)
    n_small = g_small.shape[1]
    pieces = jnp.concatenate([hi.T, mid_part.T, low.T], axis=0)
    enc_left = jnp.zeros((tokens, model_width), jnp.bfloat16).at[: 3 * n_small].set(pieces)
    picks = lax.broadcasted_iota(jnp.int32, (tokens, model_width), 1) == (
        lax.broadcasted_iota(jnp.int32, (tokens, model_width), 0) % n_small
    )
    rows_used = lax.broadcasted_iota(jnp.int32, (tokens, model_width), 0) < 3 * n_small
    enc_right = (picks & rows_used).astype(jnp.bfloat16)
    zero = jnp.zeros((tokens, model_width), jnp.bfloat16)
    lefts = [g_qkv[0]] * 3 + [g_in[0]] * 3 + [zero]
    lefts += [g_att[0], g_in[0]] + [col(g_out[0], j) for j in range(4)] + [enc_left]
    rights = [col(g_qkv[1], c) for c in range(3)] + [col(g_in[1], c) for c in range(3)] + [zero]
    rights += [g_att[1], col(g_in[1], 3)] + [g_out[1]] * 4 + [enc_right]
    per_half = len(lefts) // 2
    stacked_left = jnp.stack(lefts).reshape(2, per_half, tokens, model_width)
    stacked_right = jnp.stack(rights).reshape(2, per_half, tokens, model_width)
    mine_first = core == 0

    def products(pick_first):
        left = jnp.where(pick_first, stacked_left[0], stacked_left[1])
        right = jnp.where(pick_first, stacked_right[0], stacked_right[1])
        return jnp.einsum("btk,btn->bkn", left, right, preferred_element_type=jnp.float32)

    kept = products(mine_first)
    sent = products(jnp.logical_not(mine_first)).astype(jnp.bfloat16)
    half = kept + lax.ppermute(sent, "core", perm=[(0, 1), (1, 0)]).astype(jnp.float32)
    part = lax.psum_scatter(half, SHARD_AXES, scatter_dimension=1, tiled=True)
    part = lax.psum(part, "xh")
    res = lax.all_gather(part, "core", axis=0, tiled=False)
    r0, r1 = res[0], res[1]
    r_qkv = jnp.concatenate([r0[0], r0[1], r0[2]], axis=1)
    r_in = ungroup_columns(jnp.concatenate([r0[3], r0[4], r0[5], r1[1]], axis=1), 4)
    r_att = r1[0]
    r_out = jnp.stack([r1[2], r1[3], r1[4], r1[5]], axis=1)
    r_small = r1[6][:, :n_small]
    grad_inputs = upstream.reshape(inputs.shape)
    return (
        outputs,
        grad_inputs,
        r_qkv[None],
        r_small[:, 0:2].T[None],
        r_att[None],
        r_small[:, 2][None],
        r_small[:, 3][None],
        r_small[:, 4][None],
        r_in[None],
        r_small[:, 8:].reshape(-1)[None],
        r_out.reshape(-1, model_width)[None],
        r_small[:, 5][None],
        r_small[:, 6][None],
        r_small[:, 7][None],
    )


def solution(mesh):
    devices = mesh.devices.reshape(2, 2, 4, 2, 4)
    fine = jax.sharding.Mesh(devices, ("xh", "core", "y", "xl", "z"))
    seqs = P(("xh", "core", "y", "xl", "z"), None, None)
    rows = P(None, SHARD_AXES, None)
    vec = P(None, SHARD_AXES)
    return jax.shard_map(
        body,
        mesh=fine,
        in_specs=(
            seqs,
            P(("xh", "core", "y", "xl", "z")),
            seqs,
            rows,
            P(None, None, SHARD_AXES),
            rows,
            vec,
            vec,
            vec,
            rows,
            vec,
            rows,
            vec,
            vec,
            vec,
        ),
        out_specs=(
            seqs,
            seqs,
            rows,
            P(None, None, SHARD_AXES),
            rows,
            vec,
            vec,
            vec,
            rows,
            vec,
            rows,
            vec,
            vec,
            vec,
        ),
        check_vma=False,
    )
```

```python
import math

import jax
import jax.numpy as jnp
from jax import lax
from jax.experimental import pallas as pl
from jax.experimental.pallas import tpu as pltpu
from jax.sharding import PartitionSpec as P

HEAD_DIM = 64
LAYERS = 1


EPS = 1e-12
ROOT_HALF = 0.7071067811865476
INV_ROOT_TWO_PI = 0.3989422804014327


def _ffn_out_kernel(act_ref, w_ref, out_ref):
    @pl.when(pl.program_id(0) == 0)
    def _():
        out_ref[...] = jnp.zeros_like(out_ref)

    out_ref[...] += jnp.dot(act_ref[...], w_ref[...], preferred_element_type=jnp.float32)


def ffn_out(act_grouped, w_out):
    buffer, which, first_block = w_out
    tokens = act_grouped.shape[0]
    width = buffer.shape[1]
    groups = act_grouped.shape[1] // width
    return pl.pallas_call(
        _ffn_out_kernel,
        grid=(groups,),
        in_specs=[
            pl.BlockSpec((tokens, width), lambda j: (0, j)),
            pl.BlockSpec((None, width, width), lambda j: (which, 0, first_block + j)),
        ],
        out_specs=pl.BlockSpec((tokens, width), lambda j: (0, 0)),
        out_shape=jax.ShapeDtypeStruct((tokens, width), jnp.float32),
        cost_estimate=pl.CostEstimate(
            flops=2 * tokens * width * width * groups,
            bytes_accessed=2 * width * width * groups + 2 * tokens * width * groups + 4 * tokens * width,
            transcendentals=0,
        ),
    )(act_grouped, buffer)


def _ffn_out_back_kernel(grad_ref, w_ref, out_ref):
    out_ref[...] = lax.dot_general(
        grad_ref[...],
        w_ref[...],
        (((1,), (1,)), ((), ())),
        preferred_element_type=jnp.float32,
    )


def ffn_out_back(grad_bf, w_out):
    buffer, which, first_block = w_out
    tokens = grad_bf.shape[0]
    width = buffer.shape[1]
    groups = 4
    return pl.pallas_call(
        _ffn_out_back_kernel,
        grid=(groups,),
        in_specs=[
            pl.BlockSpec((tokens, width), lambda j: (0, 0)),
            pl.BlockSpec((None, width, width), lambda j: (which, 0, first_block + j)),
        ],
        out_specs=pl.BlockSpec((tokens, width), lambda j: (0, j)),
        out_shape=jax.ShapeDtypeStruct((tokens, width * groups), jnp.float32),
        cost_estimate=pl.CostEstimate(
            flops=2 * tokens * width * width * groups,
            bytes_accessed=2 * width * width * groups + 2 * tokens * width + 4 * tokens * width * groups,
            transcendentals=0,
        ),
    )(grad_bf, buffer)


def group_columns(x, groups):
    tokens = x.shape[0]
    return x.reshape(tokens, -1, groups).transpose(0, 2, 1).reshape(tokens, -1)


def ungroup_columns(x, groups):
    tokens = x.shape[0]
    return x.reshape(tokens, groups, -1).transpose(0, 2, 1).reshape(tokens, -1)


def batched(form, left, right):
    return jnp.einsum(form, left, right, preferred_element_type=jnp.float32)


def layer_norm(residual, gain, shift):
    row_mean = jnp.mean(residual, axis=-1, keepdims=True)
    centered = residual - row_mean
    variance = jnp.mean(centered * centered, axis=-1, keepdims=True)
    inv_std = lax.rsqrt(variance + EPS)
    normed = centered * inv_std
    return (normed * gain.astype(jnp.float32) + shift.astype(jnp.float32), normed, inv_std)


def norm_backward(upstream, normed, inv_std, gain):
    grad_gain = jnp.sum(upstream * normed, axis=0)
    grad_shift = jnp.sum(upstream, axis=0)
    scaled = upstream * gain.astype(jnp.float32)
    grad_res = inv_std * (
        scaled
        - jnp.mean(scaled, axis=-1, keepdims=True)
        - normed * jnp.mean(scaled * normed, axis=-1, keepdims=True)
    )
    return (grad_res, grad_gain, grad_shift)


def attention_scores(query_bf, key_bf, key_valid):
    scores = batched("bqhe,bkhe->bhqk", query_bf, key_bf) * (1.0 / math.sqrt(HEAD_DIM))
    return jnp.where(key_valid[:, None, None, :], scores, -1e30)


def layer_forward(hidden, hidden_bf, params, key_valid, batch_size):
    (
        w_qkv,
        b_qv,
        w_att,
        b_att,
        gain_one,
        shift_one,
        w_in,
        b_in,
        w_out,
        b_out,
        gain_two,
        shift_two,
    ) = params
    model_width = hidden.shape[1]
    seq_count = hidden.shape[0] // batch_size
    shape_heads = (batch_size, seq_count, model_width // HEAD_DIM, HEAD_DIM)
    packed = jnp.dot(hidden_bf, w_qkv, preferred_element_type=jnp.float32)
    bias_qv = b_qv.astype(jnp.float32)
    query_bf = (packed[:, :model_width] + bias_qv[0]).astype(jnp.bfloat16).reshape(shape_heads)
    key_bf = packed[:, model_width : 2 * model_width].astype(jnp.bfloat16).reshape(shape_heads)
    value_bf = (packed[:, 2 * model_width :] + bias_qv[1]).astype(jnp.bfloat16).reshape(shape_heads)
    scores = attention_scores(query_bf, key_bf, key_valid)
    row_max = jnp.max(scores, axis=-1, keepdims=True)
    row_lse = row_max + jnp.log(jnp.sum(jnp.exp(scores - row_max), axis=-1, keepdims=True))
    probs_bf = jnp.exp(scores - row_lse).astype(jnp.bfloat16)
    context_bf = (
        batched("bhqk,bkhe->bqhe", probs_bf, value_bf).astype(jnp.bfloat16).reshape(-1, model_width)
    )
    first = (
        hidden
        + jnp.dot(context_bf, w_att, preferred_element_type=jnp.float32)
        + b_att.astype(jnp.float32)
    )
    middle, normed_one, inv_one = layer_norm(first, gain_one, shift_one)
    middle_bf = middle.astype(jnp.bfloat16)
    pre_act = jnp.dot(middle_bf, w_in, preferred_element_type=jnp.float32) + b_in.astype(
        jnp.float32
    )
    act_bf = (pre_act * 0.5 * (1.0 + jax.scipy.special.erf(pre_act * ROOT_HALF))).astype(
        jnp.bfloat16
    )
    second = (
        middle
        + ffn_out(act_bf, w_out)
        + b_out.astype(jnp.float32)
    )
    result, normed_two, inv_two = layer_norm(second, gain_two, shift_two)
    stored = (
        hidden_bf,
        query_bf,
        key_bf,
        value_bf,
        row_lse,
        context_bf,
        normed_one,
        inv_one,
        middle_bf,
        pre_act,
        act_bf,
        normed_two,
        inv_two,
    )
    return (result, stored)


def layer_backward(upstream, stored, params, key_valid):
    (
        w_qkv,
        b_qv,
        w_att,
        b_att,
        gain_one,
        shift_one,
        w_in,
        b_in,
        w_out,
        b_out,
        gain_two,
        shift_two,
    ) = params
    (
        hidden_bf,
        query_bf,
        key_bf,
        value_bf,
        row_lse,
        context_bf,
        normed_one,
        inv_one,
        middle_bf,
        pre_act,
        act_bf,
        normed_two,
        inv_two,
    ) = stored
    model_width = upstream.shape[1]
    shape_heads = query_bf.shape
    grad_second, grad_gain_two, grad_shift_two = norm_backward(
        upstream, normed_two, inv_two, gain_two
    )
    grad_b_out = jnp.sum(grad_second, axis=0)
    second_bf = grad_second.astype(jnp.bfloat16)
    back_act = ffn_out_back(second_bf, w_out)
    cumulative = 0.5 * (1.0 + jax.scipy.special.erf(pre_act * ROOT_HALF))
    density = jnp.exp(-0.5 * pre_act * pre_act) * INV_ROOT_TWO_PI
    grad_pre = back_act * (cumulative + pre_act * density)
    pre_bf = grad_pre.astype(jnp.bfloat16)
    grad_b_in = jnp.sum(grad_pre, axis=0)
    grad_middle = grad_second + jnp.dot(pre_bf, w_in.T, preferred_element_type=jnp.float32)
    grad_first, grad_gain_one, grad_shift_one = norm_backward(
        grad_middle, normed_one, inv_one, gain_one
    )
    grad_b_att = jnp.sum(grad_first, axis=0)
    first_bf = grad_first.astype(jnp.bfloat16)
    grad_context = (
        jnp.dot(first_bf, w_att.T, preferred_element_type=jnp.float32)
        .astype(jnp.bfloat16)
        .reshape(shape_heads)
    )
    scores = attention_scores(query_bf, key_bf, key_valid)
    probs = jnp.exp(scores - row_lse)
    grad_value = batched("bhqk,bqhe->bkhe", probs.astype(jnp.bfloat16), grad_context).reshape(
        -1, model_width
    )
    grad_probs = batched("bqhe,bkhe->bhqk", grad_context, value_bf)
    inner = jnp.sum(probs * grad_probs, axis=-1, keepdims=True)
    grad_scores = (probs * (grad_probs - inner) * (1.0 / math.sqrt(HEAD_DIM))).astype(jnp.bfloat16)
    grad_query = batched("bhqk,bkhe->bqhe", grad_scores, key_bf).reshape(-1, model_width)
    grad_key = batched("bhqk,bqhe->bkhe", grad_scores, query_bf).reshape(-1, model_width)
    grad_b_qv = jnp.stack([jnp.sum(grad_query, axis=0), jnp.sum(grad_value, axis=0)])
    packed_bf = jnp.concatenate([grad_query, grad_key, grad_value], axis=1).astype(jnp.bfloat16)
    grad_hidden = grad_first + jnp.dot(packed_bf, w_qkv.T, preferred_element_type=jnp.float32)
    terms = (
        (hidden_bf, packed_bf),
        grad_b_qv,
        (context_bf, first_bf),
        grad_b_att,
        grad_gain_one,
        grad_shift_one,
        (middle_bf, pre_bf),
        grad_b_in,
        (act_bf, second_bf),
        grad_b_out,
        grad_gain_two,
        grad_shift_two,
    )
    return (grad_hidden, terms)


SHARD_AXES = ("y", "xl", "z")
PAIR_AXES = ("xh", "core")


def pack_halves(w_qkv, w_att, w_in, w_out, small):
    rows = w_qkv.shape[0]
    split = w_qkv.shape[1]
    pad = jnp.zeros((rows, small.shape[1]), w_qkv.dtype)
    first = jnp.concatenate([w_qkv, w_in[:, :split], pad], axis=1)
    second = jnp.concatenate(
        [w_att, w_in[:, split:], w_out.reshape(rows, -1), small], axis=1
    )
    return first, second


def unpack_halves(first, second, width, ff):
    split = 3 * width
    w_qkv = first[:, :split]
    w_in = jnp.concatenate([first[:, split : 2 * split], second[:, width : width + ff - split]], axis=1)
    at = width + ff - split
    w_att = second[:, :width]
    w_out = second[:, at : at + ff]
    small = second[:, at + ff :]
    return w_qkv, w_att, w_in, w_out, small


def body(
    inputs,
    lengths,
    cotangent,
    w_qkv,
    b_qv,
    w_att,
    b_att,
    norm1_gain,
    norm1_bias,
    w_in,
    b_in,
    w_out,
    b_out,
    norm2_gain,
    norm2_bias,
):
    batch_size, seq_count, model_width = inputs.shape
    ff = w_in.shape[2]
    rows = w_qkv.shape[1]
    core = lax.axis_index("core")
    key_valid = lax.broadcasted_iota(jnp.int32, (batch_size, seq_count), 1) < lengths[:, None]
    hidden = inputs.astype(jnp.float32).reshape(-1, model_width)
    hidden_bf = inputs.reshape(-1, model_width)
    small = jnp.concatenate(
        [
            b_qv[0].T,
            b_att[0][:, None],
            norm1_gain[0][:, None],
            norm1_bias[0][:, None],
            b_out[0][:, None],
            norm2_gain[0][:, None],
            norm2_bias[0][:, None],
            b_in[0].reshape(rows, -1),
        ],
        axis=1,
    )
    first, second = pack_halves(w_qkv[0], w_att[0], group_columns(w_in[0], 4), w_out[0], small)
    mine = jnp.where(core == 0, first, second)
    gathered = lax.all_gather(mine, SHARD_AXES, axis=0, tiled=True)
    both = lax.all_gather(gathered, "core", axis=0, tiled=False)
    f_qkv, f_att, f_in, f_out, f_small = unpack_halves(both[0], both[1], model_width, ff)
    f_out = (both, 1, (model_width + ff - 3 * model_width) // model_width)
    f_bqv = f_small[:, 0:2].T
    f_bin = group_columns(f_small[:, 8:].reshape(1, ff), 4)[0]
    params = (
        f_qkv,
        f_bqv,
        f_att,
        f_small[:, 2],
        f_small[:, 3],
        f_small[:, 4],
        f_in,
        f_bin,
        f_out,
        f_small[:, 5],
        f_small[:, 6],
        f_small[:, 7],
    )
    hidden, stored = layer_forward(hidden, hidden_bf, params, key_valid, batch_size)
    outputs = hidden.astype(jnp.bfloat16).reshape(inputs.shape)
    upstream = cotangent.astype(jnp.float32).reshape(-1, model_width)
    upstream, terms = layer_backward(upstream, stored, params, key_valid)
    (g_qkv, g_bqv, g_att, g_batt, g_n1g, g_n1b, g_in, g_bin, g_out, g_bout, g_n2g, g_n2b) = terms
    g_small = jnp.concatenate(
        [
            g_bqv.T,
            g_batt[:, None],
            g_n1g[:, None],
            g_n1b[:, None],
            g_bout[:, None],
            g_n2g[:, None],
            g_n2b[:, None],
            ungroup_columns(g_bin[None], 4)[0].reshape(model_width, -1),
        ],
        axis=1,
    )
    tokens = g_qkv[0].shape[0]
    col = lambda b, c: b[:, c * model_width : (c + 1) * model_width]
    hi = g_small.astype(jnp.bfloat16)
    rest = g_small - hi.astype(jnp.float32)
    mid_part = rest.astype(jnp.bfloat16)
    low = (rest - mid_part.astype(jnp.float32)).astype(jnp.bfloat16)
    n_small = g_small.shape[1]
    pieces = jnp.concatenate([hi.T, mid_part.T, low.T], axis=0)
    enc_left = jnp.zeros((tokens, model_width), jnp.bfloat16).at[: 3 * n_small].set(pieces)
    picks = lax.broadcasted_iota(jnp.int32, (tokens, model_width), 1) == (
        lax.broadcasted_iota(jnp.int32, (tokens, model_width), 0) % n_small
    )
    rows_used = lax.broadcasted_iota(jnp.int32, (tokens, model_width), 0) < 3 * n_small
    enc_right = (picks & rows_used).astype(jnp.bfloat16)
    zero = jnp.zeros((tokens, model_width), jnp.bfloat16)
    mine_first = core == 0

    def exchange(lefts, rights):
        stacked_left = jnp.stack([jnp.stack(side) for side in lefts])
        stacked_right = jnp.stack([jnp.stack(side) for side in rights])

        def products(pick_first):
            left = jnp.where(pick_first, stacked_left[0], stacked_left[1])
            right = jnp.where(pick_first, stacked_right[0], stacked_right[1])
            return jnp.einsum("btk,btn->bkn", left, right, preferred_element_type=jnp.float32)

        kept = products(mine_first)
        sent = products(jnp.logical_not(mine_first)).astype(jnp.bfloat16)
        return kept + lax.ppermute(sent, "core", perm=[(0, 1), (1, 0)]).astype(jnp.float32)

    early = exchange(
        [[g_in[0]] * 4, [col(g_out[0], j) for j in range(4)]],
        [[col(g_in[1], c) for c in range(4)], [g_out[1]] * 4],
    )
    late = exchange(
        [[g_qkv[0]] * 3, [g_att[0], enc_left, zero]],
        [[col(g_qkv[1], c) for c in range(3)], [g_att[1], enc_right, zero]],
    )
    half = jnp.concatenate([early, late], axis=0)
    part = lax.psum_scatter(half, SHARD_AXES, scatter_dimension=1, tiled=True)
    part = lax.psum(part, "xh")
    res = lax.all_gather(part, "core", axis=0, tiled=False)
    r0, r1 = res[0], res[1]
    r_in = ungroup_columns(jnp.concatenate([r0[0], r0[1], r0[2], r0[3]], axis=1), 4)
    r_qkv = jnp.concatenate([r0[4], r0[5], r0[6]], axis=1)
    r_out = jnp.stack([r1[0], r1[1], r1[2], r1[3]], axis=1)
    r_att = r1[4]
    r_small = r1[5][:, :n_small]
    grad_inputs = upstream.reshape(inputs.shape)
    return (
        outputs,
        grad_inputs,
        r_qkv[None],
        r_small[:, 0:2].T[None],
        r_att[None],
        r_small[:, 2][None],
        r_small[:, 3][None],
        r_small[:, 4][None],
        r_in[None],
        r_small[:, 8:].reshape(-1)[None],
        r_out.reshape(-1, model_width)[None],
        r_small[:, 5][None],
        r_small[:, 6][None],
        r_small[:, 7][None],
    )


def solution(mesh):
    devices = mesh.devices.reshape(2, 2, 4, 2, 4)
    fine = jax.sharding.Mesh(devices, ("xh", "core", "y", "xl", "z"))
    seqs = P(("xh", "core", "y", "xl", "z"), None, None)
    rows = P(None, SHARD_AXES, None)
    vec = P(None, SHARD_AXES)
    return jax.shard_map(
        body,
        mesh=fine,
        in_specs=(
            seqs,
            P(("xh", "core", "y", "xl", "z")),
            seqs,
            rows,
            P(None, None, SHARD_AXES),
            rows,
            vec,
            vec,
            vec,
            rows,
            vec,
            rows,
            vec,
            vec,
            vec,
        ),
        out_specs=(
            seqs,
            seqs,
            rows,
            P(None, None, SHARD_AXES),
            rows,
            vec,
            vec,
            vec,
            rows,
            vec,
            rows,
            vec,
            vec,
            vec,
        ),
        check_vma=False,
    )
```

```python
import math

import jax
import jax.numpy as jnp
from jax import lax
from jax.experimental import pallas as pl
from jax.experimental.pallas import tpu as pltpu
from jax.sharding import PartitionSpec as P

HEAD_DIM = 64
LAYERS = 1


EPS = 1e-12
ROOT_HALF = 0.7071067811865476
INV_ROOT_TWO_PI = 0.3989422804014327


def _ffn_out_kernel(act_ref, w_ref, out_ref):
    @pl.when(pl.program_id(0) == 0)
    def _():
        out_ref[...] = jnp.zeros_like(out_ref)

    out_ref[...] += jnp.dot(act_ref[...], w_ref[...], preferred_element_type=jnp.float32)


def ffn_out(act_grouped, w_out):
    buffer, which, first_block = w_out
    tokens = act_grouped.shape[0]
    width = buffer.shape[1]
    groups = act_grouped.shape[1] // width
    return pl.pallas_call(
        _ffn_out_kernel,
        grid=(groups,),
        in_specs=[
            pl.BlockSpec((tokens, width), lambda j: (0, j)),
            pl.BlockSpec((None, width, width), lambda j: (which, 0, first_block + j)),
        ],
        out_specs=pl.BlockSpec((tokens, width), lambda j: (0, 0)),
        out_shape=jax.ShapeDtypeStruct((tokens, width), jnp.float32),
        cost_estimate=pl.CostEstimate(
            flops=2 * tokens * width * width * groups,
            bytes_accessed=2 * width * width * groups + 2 * tokens * width * groups + 4 * tokens * width,
            transcendentals=0,
        ),
    )(act_grouped, buffer)


def _ffn_out_back_kernel(grad_ref, w_ref, out_ref):
    out_ref[...] = lax.dot_general(
        grad_ref[...],
        w_ref[...],
        (((1,), (1,)), ((), ())),
        preferred_element_type=jnp.float32,
    )


def ffn_out_back(grad_bf, w_out):
    buffer, which, first_block = w_out
    tokens = grad_bf.shape[0]
    width = buffer.shape[1]
    groups = 4
    return pl.pallas_call(
        _ffn_out_back_kernel,
        grid=(groups,),
        in_specs=[
            pl.BlockSpec((tokens, width), lambda j: (0, 0)),
            pl.BlockSpec((None, width, width), lambda j: (which, 0, first_block + j)),
        ],
        out_specs=pl.BlockSpec((tokens, width), lambda j: (0, j)),
        out_shape=jax.ShapeDtypeStruct((tokens, width * groups), jnp.float32),
        cost_estimate=pl.CostEstimate(
            flops=2 * tokens * width * width * groups,
            bytes_accessed=2 * width * width * groups + 2 * tokens * width + 4 * tokens * width * groups,
            transcendentals=0,
        ),
    )(grad_bf, buffer)


def group_columns(x, groups):
    tokens = x.shape[0]
    return x.reshape(tokens, -1, groups).transpose(0, 2, 1).reshape(tokens, -1)


def ungroup_columns(x, groups):
    tokens = x.shape[0]
    return x.reshape(tokens, groups, -1).transpose(0, 2, 1).reshape(tokens, -1)


def batched(form, left, right):
    return jnp.einsum(form, left, right, preferred_element_type=jnp.float32)


def layer_norm(residual, gain, shift):
    row_mean = jnp.mean(residual, axis=-1, keepdims=True)
    centered = residual - row_mean
    variance = jnp.mean(centered * centered, axis=-1, keepdims=True)
    inv_std = lax.rsqrt(variance + EPS)
    normed = centered * inv_std
    return (normed * gain.astype(jnp.float32) + shift.astype(jnp.float32), normed, inv_std)


def norm_backward(upstream, normed, inv_std, gain):
    grad_gain = jnp.sum(upstream * normed, axis=0)
    grad_shift = jnp.sum(upstream, axis=0)
    scaled = upstream * gain.astype(jnp.float32)
    grad_res = inv_std * (
        scaled
        - jnp.mean(scaled, axis=-1, keepdims=True)
        - normed * jnp.mean(scaled * normed, axis=-1, keepdims=True)
    )
    return (grad_res, grad_gain, grad_shift)


def attention_scores(query_bf, key_bf, key_valid):
    scores = batched("bqhe,bkhe->bhqk", query_bf, key_bf) * (1.0 / math.sqrt(HEAD_DIM))
    return jnp.where(key_valid[:, None, None, :], scores, -1e30)


def layer_forward(hidden, hidden_bf, params, key_valid, batch_size):
    (
        w_qkv,
        b_qv,
        w_att,
        b_att,
        gain_one,
        shift_one,
        w_in,
        b_in,
        w_out,
        b_out,
        gain_two,
        shift_two,
    ) = params
    model_width = hidden.shape[1]
    seq_count = hidden.shape[0] // batch_size
    shape_heads = (batch_size, seq_count, model_width // HEAD_DIM, HEAD_DIM)
    packed = jnp.dot(hidden_bf, w_qkv, preferred_element_type=jnp.float32)
    bias_qv = b_qv.astype(jnp.float32)
    query_bf = (packed[:, :model_width] + bias_qv[0]).astype(jnp.bfloat16).reshape(shape_heads)
    key_bf = packed[:, model_width : 2 * model_width].astype(jnp.bfloat16).reshape(shape_heads)
    value_bf = (packed[:, 2 * model_width :] + bias_qv[1]).astype(jnp.bfloat16).reshape(shape_heads)
    scores = attention_scores(query_bf, key_bf, key_valid)
    row_max = jnp.max(scores, axis=-1, keepdims=True)
    row_lse = row_max + jnp.log(jnp.sum(jnp.exp(scores - row_max), axis=-1, keepdims=True))
    probs_bf = jnp.exp(scores - row_lse).astype(jnp.bfloat16)
    context_bf = (
        batched("bhqk,bkhe->bqhe", probs_bf, value_bf).astype(jnp.bfloat16).reshape(-1, model_width)
    )
    first = (
        hidden
        + jnp.dot(context_bf, w_att, preferred_element_type=jnp.float32)
        + b_att.astype(jnp.float32)
    )
    middle, normed_one, inv_one = layer_norm(first, gain_one, shift_one)
    middle_bf = middle.astype(jnp.bfloat16)
    pre_act = jnp.dot(middle_bf, w_in, preferred_element_type=jnp.float32) + b_in.astype(
        jnp.float32
    )
    act_bf = (pre_act * 0.5 * (1.0 + jax.scipy.special.erf(pre_act * ROOT_HALF))).astype(
        jnp.bfloat16
    )
    second = (
        middle
        + ffn_out(act_bf, w_out)
        + b_out.astype(jnp.float32)
    )
    result, normed_two, inv_two = layer_norm(second, gain_two, shift_two)
    stored = (
        hidden_bf,
        query_bf,
        key_bf,
        value_bf,
        row_lse,
        context_bf,
        normed_one,
        inv_one,
        middle_bf,
        pre_act,
        act_bf,
        normed_two,
        inv_two,
    )
    return (result, stored)


def layer_backward(upstream, stored, params, key_valid):
    (
        w_qkv,
        b_qv,
        w_att,
        b_att,
        gain_one,
        shift_one,
        w_in,
        b_in,
        w_out,
        b_out,
        gain_two,
        shift_two,
    ) = params
    (
        hidden_bf,
        query_bf,
        key_bf,
        value_bf,
        row_lse,
        context_bf,
        normed_one,
        inv_one,
        middle_bf,
        pre_act,
        act_bf,
        normed_two,
        inv_two,
    ) = stored
    model_width = upstream.shape[1]
    shape_heads = query_bf.shape
    grad_second, grad_gain_two, grad_shift_two = norm_backward(
        upstream, normed_two, inv_two, gain_two
    )
    grad_b_out = jnp.sum(grad_second, axis=0)
    second_bf = grad_second.astype(jnp.bfloat16)
    back_act = ffn_out_back(second_bf, w_out)
    cumulative = 0.5 * (1.0 + jax.scipy.special.erf(pre_act * ROOT_HALF))
    density = jnp.exp(-0.5 * pre_act * pre_act) * INV_ROOT_TWO_PI
    grad_pre = back_act * (cumulative + pre_act * density)
    pre_bf = grad_pre.astype(jnp.bfloat16)
    grad_b_in = jnp.sum(grad_pre, axis=0)
    grad_middle = grad_second + jnp.dot(pre_bf, w_in.T, preferred_element_type=jnp.float32)
    grad_first, grad_gain_one, grad_shift_one = norm_backward(
        grad_middle, normed_one, inv_one, gain_one
    )
    grad_b_att = jnp.sum(grad_first, axis=0)
    first_bf = grad_first.astype(jnp.bfloat16)
    grad_context = (
        jnp.dot(first_bf, w_att.T, preferred_element_type=jnp.float32)
        .astype(jnp.bfloat16)
        .reshape(shape_heads)
    )
    scores = attention_scores(query_bf, key_bf, key_valid)
    probs = jnp.exp(scores - row_lse)
    grad_value = batched("bhqk,bqhe->bkhe", probs.astype(jnp.bfloat16), grad_context).reshape(
        -1, model_width
    )
    grad_probs = batched("bqhe,bkhe->bhqk", grad_context, value_bf)
    inner = jnp.sum(probs * grad_probs, axis=-1, keepdims=True)
    grad_scores = (probs * (grad_probs - inner) * (1.0 / math.sqrt(HEAD_DIM))).astype(jnp.bfloat16)
    grad_query = batched("bhqk,bkhe->bqhe", grad_scores, key_bf).reshape(-1, model_width)
    grad_key = batched("bhqk,bqhe->bkhe", grad_scores, query_bf).reshape(-1, model_width)
    grad_b_qv = jnp.stack([jnp.sum(grad_query, axis=0), jnp.sum(grad_value, axis=0)])
    packed_bf = jnp.concatenate([grad_query, grad_key, grad_value], axis=1).astype(jnp.bfloat16)
    grad_hidden = grad_first + jnp.dot(packed_bf, w_qkv.T, preferred_element_type=jnp.float32)
    terms = (
        (hidden_bf, packed_bf),
        grad_b_qv,
        (context_bf, first_bf),
        grad_b_att,
        grad_gain_one,
        grad_shift_one,
        (middle_bf, pre_bf),
        grad_b_in,
        (act_bf, second_bf),
        grad_b_out,
        grad_gain_two,
        grad_shift_two,
    )
    return (grad_hidden, terms)


SHARD_AXES = ("y", "xl", "z")
PAIR_AXES = ("xh", "core")


def pack_halves(w_qkv, w_att, w_in, w_out, small):
    rows = w_qkv.shape[0]
    split = w_qkv.shape[1]
    pad = jnp.zeros((rows, small.shape[1]), w_qkv.dtype)
    first = jnp.concatenate([w_qkv, w_in[:, :split], pad], axis=1)
    second = jnp.concatenate(
        [w_att, w_in[:, split:], w_out.reshape(rows, -1), small], axis=1
    )
    return first, second


def unpack_halves(first, second, width, ff):
    split = 3 * width
    w_qkv = first[:, :split]
    w_in = jnp.concatenate([first[:, split : 2 * split], second[:, width : width + ff - split]], axis=1)
    at = width + ff - split
    w_att = second[:, :width]
    w_out = second[:, at : at + ff]
    small = second[:, at + ff :]
    return w_qkv, w_att, w_in, w_out, small


def body(
    inputs,
    lengths,
    cotangent,
    w_qkv,
    b_qv,
    w_att,
    b_att,
    norm1_gain,
    norm1_bias,
    w_in,
    b_in,
    w_out,
    b_out,
    norm2_gain,
    norm2_bias,
):
    batch_size, seq_count, model_width = inputs.shape
    ff = w_in.shape[2]
    rows = w_qkv.shape[1]
    core = lax.axis_index("core")
    key_valid = lax.broadcasted_iota(jnp.int32, (batch_size, seq_count), 1) < lengths[:, None]
    hidden = inputs.astype(jnp.float32).reshape(-1, model_width)
    hidden_bf = inputs.reshape(-1, model_width)
    small = jnp.concatenate(
        [
            b_qv[0].T,
            b_att[0][:, None],
            norm1_gain[0][:, None],
            norm1_bias[0][:, None],
            b_out[0][:, None],
            norm2_gain[0][:, None],
            norm2_bias[0][:, None],
            b_in[0].reshape(rows, -1),
        ],
        axis=1,
    )
    first, second = pack_halves(w_qkv[0], w_att[0], group_columns(w_in[0], 4), w_out[0], small)
    mine = jnp.where(core == 0, first, second)
    gathered = lax.all_gather(mine, SHARD_AXES, axis=0, tiled=True)
    both = lax.all_gather(gathered, "core", axis=0, tiled=False)
    f_qkv, f_att, f_in, f_out, f_small = unpack_halves(both[0], both[1], model_width, ff)
    f_out = (both, 1, (model_width + ff - 3 * model_width) // model_width)
    f_bqv = f_small[:, 0:2].T
    f_bin = group_columns(f_small[:, 8:].reshape(1, ff), 4)[0]
    params = (
        f_qkv,
        f_bqv,
        f_att,
        f_small[:, 2],
        f_small[:, 3],
        f_small[:, 4],
        f_in,
        f_bin,
        f_out,
        f_small[:, 5],
        f_small[:, 6],
        f_small[:, 7],
    )
    hidden, stored = layer_forward(hidden, hidden_bf, params, key_valid, batch_size)
    outputs = hidden.astype(jnp.bfloat16).reshape(inputs.shape)
    upstream = cotangent.astype(jnp.float32).reshape(-1, model_width)
    upstream, terms = layer_backward(upstream, stored, params, key_valid)
    (g_qkv, g_bqv, g_att, g_batt, g_n1g, g_n1b, g_in, g_bin, g_out, g_bout, g_n2g, g_n2b) = terms
    g_small = jnp.concatenate(
        [
            g_bqv.T,
            g_batt[:, None],
            g_n1g[:, None],
            g_n1b[:, None],
            g_bout[:, None],
            g_n2g[:, None],
            g_n2b[:, None],
            ungroup_columns(g_bin[None], 4)[0].reshape(model_width, -1),
        ],
        axis=1,
    )
    tokens = g_qkv[0].shape[0]
    col = lambda b, c: b[:, c * model_width : (c + 1) * model_width]
    hi = g_small.astype(jnp.bfloat16)
    rest = g_small - hi.astype(jnp.float32)
    mid_part = rest.astype(jnp.bfloat16)
    low = (rest - mid_part.astype(jnp.float32)).astype(jnp.bfloat16)
    n_small = g_small.shape[1]
    pieces = jnp.concatenate([hi.T, mid_part.T, low.T], axis=0)
    enc_left = jnp.zeros((tokens, model_width), jnp.bfloat16).at[: 3 * n_small].set(pieces)
    picks = lax.broadcasted_iota(jnp.int32, (tokens, model_width), 1) == (
        lax.broadcasted_iota(jnp.int32, (tokens, model_width), 0) % n_small
    )
    rows_used = lax.broadcasted_iota(jnp.int32, (tokens, model_width), 0) < 3 * n_small
    enc_right = (picks & rows_used).astype(jnp.bfloat16)
    zero = jnp.zeros((tokens, model_width), jnp.bfloat16)
    mine_first = core == 0

    def stacks(lefts, rights):
        return (
            jnp.stack([jnp.stack(side) for side in lefts]),
            jnp.stack([jnp.stack(side) for side in rights]),
        )

    def products(stacked, pick_first):
        stacked_left, stacked_right = stacked
        left = jnp.where(pick_first, stacked_left[0], stacked_left[1])
        right = jnp.where(pick_first, stacked_right[0], stacked_right[1])
        return jnp.einsum("btk,btn->bkn", left, right, preferred_element_type=jnp.float32)

    def handed_over(stacked):
        sent = products(stacked, jnp.logical_not(mine_first)).astype(jnp.bfloat16)
        return lax.ppermute(sent, "core", perm=[(0, 1), (1, 0)])

    early = stacks(
        [[g_in[0]] * 4, [col(g_out[0], j) for j in range(4)]],
        [[col(g_in[1], c) for c in range(4)], [g_out[1]] * 4],
    )
    late = stacks(
        [[g_qkv[0]] * 3, [g_att[0], enc_left, zero]],
        [[col(g_qkv[1], c) for c in range(3)], [g_att[1], enc_right, zero]],
    )
    received = jnp.concatenate([handed_over(early), handed_over(late)], axis=0)
    every = tuple(jnp.concatenate([a, b], axis=1) for a, b in zip(early, late))
    half = products(every, mine_first) + received.astype(jnp.float32)
    part = lax.psum_scatter(half, SHARD_AXES, scatter_dimension=1, tiled=True)
    part = lax.psum(part, "xh")
    res = lax.all_gather(part, "core", axis=0, tiled=False)
    r0, r1 = res[0], res[1]
    r_in = ungroup_columns(jnp.concatenate([r0[0], r0[1], r0[2], r0[3]], axis=1), 4)
    r_qkv = jnp.concatenate([r0[4], r0[5], r0[6]], axis=1)
    r_out = jnp.stack([r1[0], r1[1], r1[2], r1[3]], axis=1)
    r_att = r1[4]
    r_small = r1[5][:, :n_small]
    grad_inputs = upstream.reshape(inputs.shape)
    return (
        outputs,
        grad_inputs,
        r_qkv[None],
        r_small[:, 0:2].T[None],
        r_att[None],
        r_small[:, 2][None],
        r_small[:, 3][None],
        r_small[:, 4][None],
        r_in[None],
        r_small[:, 8:].reshape(-1)[None],
        r_out.reshape(-1, model_width)[None],
        r_small[:, 5][None],
        r_small[:, 6][None],
        r_small[:, 7][None],
    )


def solution(mesh):
    devices = mesh.devices.reshape(2, 2, 4, 2, 4)
    fine = jax.sharding.Mesh(devices, ("xh", "core", "y", "xl", "z"))
    seqs = P(("xh", "core", "y", "xl", "z"), None, None)
    rows = P(None, SHARD_AXES, None)
    vec = P(None, SHARD_AXES)
    return jax.shard_map(
        body,
        mesh=fine,
        in_specs=(
            seqs,
            P(("xh", "core", "y", "xl", "z")),
            seqs,
            rows,
            P(None, None, SHARD_AXES),
            rows,
            vec,
            vec,
            vec,
            rows,
            vec,
            rows,
            vec,
            vec,
            vec,
        ),
        out_specs=(
            seqs,
            seqs,
            rows,
            P(None, None, SHARD_AXES),
            rows,
            vec,
            vec,
            vec,
            rows,
            vec,
            rows,
            vec,
            vec,
            vec,
        ),
        check_vma=False,
    )
```

```python
import math

import jax
import jax.numpy as jnp
from jax import lax
from jax.experimental import pallas as pl
from jax.experimental.pallas import tpu as pltpu
from jax.sharding import PartitionSpec as P

HEAD_DIM = 64
LAYERS = 1


EPS = 1e-12
ROOT_HALF = 0.7071067811865476
INV_ROOT_TWO_PI = 0.3989422804014327


def _ffn_out_kernel(act_ref, w_ref, out_ref):
    @pl.when(pl.program_id(0) == 0)
    def _():
        out_ref[...] = jnp.zeros_like(out_ref)

    out_ref[...] += jnp.dot(act_ref[...], w_ref[...], preferred_element_type=jnp.float32)


def ffn_out(act_grouped, w_out):
    buffer, which, first_block = w_out
    tokens = act_grouped.shape[0]
    width = buffer.shape[1]
    groups = act_grouped.shape[1] // width
    return pl.pallas_call(
        _ffn_out_kernel,
        grid=(groups,),
        in_specs=[
            pl.BlockSpec((tokens, width), lambda j: (0, j)),
            pl.BlockSpec((None, width, width), lambda j: (which, 0, first_block + j)),
        ],
        out_specs=pl.BlockSpec((tokens, width), lambda j: (0, 0)),
        out_shape=jax.ShapeDtypeStruct((tokens, width), jnp.float32),
        cost_estimate=pl.CostEstimate(
            flops=2 * tokens * width * width * groups,
            bytes_accessed=2 * width * width * groups + 2 * tokens * width * groups + 4 * tokens * width,
            transcendentals=0,
        ),
    )(act_grouped, buffer)


def _ffn_out_back_kernel(grad_ref, w_ref, out_ref):
    out_ref[...] = lax.dot_general(
        grad_ref[...],
        w_ref[...],
        (((1,), (1,)), ((), ())),
        preferred_element_type=jnp.float32,
    )


def ffn_out_back(grad_bf, w_out):
    buffer, which, first_block = w_out
    tokens = grad_bf.shape[0]
    width = buffer.shape[1]
    groups = 4
    return pl.pallas_call(
        _ffn_out_back_kernel,
        grid=(groups,),
        in_specs=[
            pl.BlockSpec((tokens, width), lambda j: (0, 0)),
            pl.BlockSpec((None, width, width), lambda j: (which, 0, first_block + j)),
        ],
        out_specs=pl.BlockSpec((tokens, width), lambda j: (0, j)),
        out_shape=jax.ShapeDtypeStruct((tokens, width * groups), jnp.float32),
        cost_estimate=pl.CostEstimate(
            flops=2 * tokens * width * width * groups,
            bytes_accessed=2 * width * width * groups + 2 * tokens * width + 4 * tokens * width * groups,
            transcendentals=0,
        ),
    )(grad_bf, buffer)


def group_columns(x, groups):
    tokens = x.shape[0]
    return x.reshape(tokens, -1, groups).transpose(0, 2, 1).reshape(tokens, -1)


def ungroup_columns(x, groups):
    tokens = x.shape[0]
    return x.reshape(tokens, groups, -1).transpose(0, 2, 1).reshape(tokens, -1)


def batched(form, left, right):
    return jnp.einsum(form, left, right, preferred_element_type=jnp.float32)


def layer_norm(residual, gain, shift):
    row_mean = jnp.mean(residual, axis=-1, keepdims=True)
    centered = residual - row_mean
    variance = jnp.mean(centered * centered, axis=-1, keepdims=True)
    inv_std = lax.rsqrt(variance + EPS)
    normed = centered * inv_std
    return (normed * gain.astype(jnp.float32) + shift.astype(jnp.float32), normed, inv_std)


def norm_backward(upstream, normed, inv_std, gain):
    grad_gain = jnp.sum(upstream * normed, axis=0)
    grad_shift = jnp.sum(upstream, axis=0)
    scaled = upstream * gain.astype(jnp.float32)
    grad_res = inv_std * (
        scaled
        - jnp.mean(scaled, axis=-1, keepdims=True)
        - normed * jnp.mean(scaled * normed, axis=-1, keepdims=True)
    )
    return (grad_res, grad_gain, grad_shift)


def attention_scores(query_bf, key_bf, key_valid):
    scores = batched("bqhe,bkhe->bhqk", query_bf, key_bf) * (1.0 / math.sqrt(HEAD_DIM))
    return jnp.where(key_valid[:, None, None, :], scores, -1e30)


def layer_forward(hidden, hidden_bf, params, key_valid, batch_size):
    (
        w_qkv,
        b_qv,
        w_att,
        b_att,
        gain_one,
        shift_one,
        w_in,
        b_in,
        w_out,
        b_out,
        gain_two,
        shift_two,
    ) = params
    model_width = hidden.shape[1]
    seq_count = hidden.shape[0] // batch_size
    shape_heads = (batch_size, seq_count, model_width // HEAD_DIM, HEAD_DIM)
    packed = jnp.dot(hidden_bf, w_qkv, preferred_element_type=jnp.float32)
    bias_qv = b_qv.astype(jnp.float32)
    query_bf = (packed[:, :model_width] + bias_qv[0]).astype(jnp.bfloat16).reshape(shape_heads)
    key_bf = packed[:, model_width : 2 * model_width].astype(jnp.bfloat16).reshape(shape_heads)
    value_bf = (packed[:, 2 * model_width :] + bias_qv[1]).astype(jnp.bfloat16).reshape(shape_heads)
    scores = attention_scores(query_bf, key_bf, key_valid)
    row_max = jnp.max(scores, axis=-1, keepdims=True)
    row_lse = row_max + jnp.log(jnp.sum(jnp.exp(scores - row_max), axis=-1, keepdims=True))
    probs_bf = jnp.exp(scores - row_lse).astype(jnp.bfloat16)
    context_bf = (
        batched("bhqk,bkhe->bqhe", probs_bf, value_bf).astype(jnp.bfloat16).reshape(-1, model_width)
    )
    first = (
        hidden
        + jnp.dot(context_bf, w_att, preferred_element_type=jnp.float32)
        + b_att.astype(jnp.float32)
    )
    middle, normed_one, inv_one = layer_norm(first, gain_one, shift_one)
    middle_bf = middle.astype(jnp.bfloat16)
    pre_act = jnp.dot(middle_bf, w_in, preferred_element_type=jnp.float32) + b_in.astype(
        jnp.float32
    )
    act_bf = (pre_act * 0.5 * (1.0 + jax.scipy.special.erf(pre_act * ROOT_HALF))).astype(
        jnp.bfloat16
    )
    second = (
        middle
        + ffn_out(act_bf, w_out)
        + b_out.astype(jnp.float32)
    )
    result, normed_two, inv_two = layer_norm(second, gain_two, shift_two)
    stored = (
        hidden_bf,
        query_bf,
        key_bf,
        value_bf,
        row_lse,
        context_bf,
        normed_one,
        inv_one,
        middle_bf,
        pre_act,
        act_bf,
        normed_two,
        inv_two,
    )
    return (result, stored)


def layer_backward(upstream, stored, params, key_valid):
    (
        w_qkv,
        b_qv,
        w_att,
        b_att,
        gain_one,
        shift_one,
        w_in,
        b_in,
        w_out,
        b_out,
        gain_two,
        shift_two,
    ) = params
    (
        hidden_bf,
        query_bf,
        key_bf,
        value_bf,
        row_lse,
        context_bf,
        normed_one,
        inv_one,
        middle_bf,
        pre_act,
        act_bf,
        normed_two,
        inv_two,
    ) = stored
    model_width = upstream.shape[1]
    shape_heads = query_bf.shape
    grad_second, grad_gain_two, grad_shift_two = norm_backward(
        upstream, normed_two, inv_two, gain_two
    )
    grad_b_out = jnp.sum(grad_second, axis=0)
    second_bf = grad_second.astype(jnp.bfloat16)
    back_act = ffn_out_back(second_bf, w_out)
    cumulative = 0.5 * (1.0 + jax.scipy.special.erf(pre_act * ROOT_HALF))
    density = jnp.exp(-0.5 * pre_act * pre_act) * INV_ROOT_TWO_PI
    grad_pre = back_act * (cumulative + pre_act * density)
    pre_bf = grad_pre.astype(jnp.bfloat16)
    grad_b_in = jnp.sum(grad_pre, axis=0)
    grad_middle = grad_second + jnp.dot(pre_bf, w_in.T, preferred_element_type=jnp.float32)
    grad_first, grad_gain_one, grad_shift_one = norm_backward(
        grad_middle, normed_one, inv_one, gain_one
    )
    grad_b_att = jnp.sum(grad_first, axis=0)
    first_bf = grad_first.astype(jnp.bfloat16)
    grad_context = (
        jnp.dot(first_bf, w_att.T, preferred_element_type=jnp.float32)
        .astype(jnp.bfloat16)
        .reshape(shape_heads)
    )
    scores = attention_scores(query_bf, key_bf, key_valid)
    probs = jnp.exp(scores - row_lse)
    grad_value = batched("bhqk,bqhe->bkhe", probs.astype(jnp.bfloat16), grad_context).reshape(
        -1, model_width
    )
    grad_probs = batched("bqhe,bkhe->bhqk", grad_context, value_bf)
    inner = jnp.sum(probs * grad_probs, axis=-1, keepdims=True)
    grad_scores = (probs * (grad_probs - inner) * (1.0 / math.sqrt(HEAD_DIM))).astype(jnp.bfloat16)
    grad_query = batched("bhqk,bkhe->bqhe", grad_scores, key_bf).reshape(-1, model_width)
    grad_key = batched("bhqk,bqhe->bkhe", grad_scores, query_bf).reshape(-1, model_width)
    grad_b_qv = jnp.stack([jnp.sum(grad_query, axis=0), jnp.sum(grad_value, axis=0)])
    packed_bf = jnp.concatenate([grad_query, grad_key, grad_value], axis=1).astype(jnp.bfloat16)
    grad_hidden = grad_first + jnp.dot(packed_bf, w_qkv.T, preferred_element_type=jnp.float32)
    terms = (
        (hidden_bf, packed_bf),
        grad_b_qv,
        (context_bf, first_bf),
        grad_b_att,
        grad_gain_one,
        grad_shift_one,
        (middle_bf, pre_bf),
        grad_b_in,
        (act_bf, second_bf),
        grad_b_out,
        grad_gain_two,
        grad_shift_two,
    )
    return (grad_hidden, terms)


SHARD_AXES = ("y", "xl", "z")
PAIR_AXES = ("xh", "core")


def pack_halves(w_qkv, w_att, w_in, w_out, small):
    rows = w_qkv.shape[0]
    split = w_qkv.shape[1]
    pad = jnp.zeros((rows, small.shape[1]), w_qkv.dtype)
    first = jnp.concatenate([w_qkv, w_in[:, :split], pad], axis=1)
    second = jnp.concatenate(
        [w_att, w_in[:, split:], w_out.reshape(rows, -1), small], axis=1
    )
    return first, second


def unpack_halves(first, second, width, ff):
    split = 3 * width
    w_qkv = first[:, :split]
    w_in = jnp.concatenate([first[:, split : 2 * split], second[:, width : width + ff - split]], axis=1)
    at = width + ff - split
    w_att = second[:, :width]
    w_out = second[:, at : at + ff]
    small = second[:, at + ff :]
    return w_qkv, w_att, w_in, w_out, small


def body(
    inputs,
    lengths,
    cotangent,
    w_qkv,
    b_qv,
    w_att,
    b_att,
    norm1_gain,
    norm1_bias,
    w_in,
    b_in,
    w_out,
    b_out,
    norm2_gain,
    norm2_bias,
):
    batch_size, seq_count, model_width = inputs.shape
    ff = w_in.shape[2]
    rows = w_qkv.shape[1]
    core = lax.axis_index("core")
    key_valid = lax.broadcasted_iota(jnp.int32, (batch_size, seq_count), 1) < lengths[:, None]
    hidden = inputs.astype(jnp.float32).reshape(-1, model_width)
    hidden_bf = inputs.reshape(-1, model_width)
    small = jnp.concatenate(
        [
            b_qv[0].T,
            b_att[0][:, None],
            norm1_gain[0][:, None],
            norm1_bias[0][:, None],
            b_out[0][:, None],
            norm2_gain[0][:, None],
            norm2_bias[0][:, None],
            b_in[0].reshape(rows, -1),
        ],
        axis=1,
    )
    first, second = pack_halves(w_qkv[0], w_att[0], group_columns(w_in[0], 4), w_out[0], small)
    mine = jnp.where(core == 0, first, second)
    gathered = lax.all_gather(mine, SHARD_AXES, axis=0, tiled=True)
    both = lax.all_gather(gathered, "core", axis=0, tiled=False)
    f_qkv, f_att, f_in, f_out, f_small = unpack_halves(both[0], both[1], model_width, ff)
    f_out = (both, 1, (model_width + ff - 3 * model_width) // model_width)
    f_bqv = f_small[:, 0:2].T
    f_bin = group_columns(f_small[:, 8:].reshape(1, ff), 4)[0]
    params = (
        f_qkv,
        f_bqv,
        f_att,
        f_small[:, 2],
        f_small[:, 3],
        f_small[:, 4],
        f_in,
        f_bin,
        f_out,
        f_small[:, 5],
        f_small[:, 6],
        f_small[:, 7],
    )
    hidden, stored = layer_forward(hidden, hidden_bf, params, key_valid, batch_size)
    outputs = hidden.astype(jnp.bfloat16).reshape(inputs.shape)
    upstream = cotangent.astype(jnp.float32).reshape(-1, model_width)
    upstream, terms = layer_backward(upstream, stored, params, key_valid)
    (g_qkv, g_bqv, g_att, g_batt, g_n1g, g_n1b, g_in, g_bin, g_out, g_bout, g_n2g, g_n2b) = terms
    g_small = jnp.concatenate(
        [
            g_bqv.T,
            g_batt[:, None],
            g_n1g[:, None],
            g_n1b[:, None],
            g_bout[:, None],
            g_n2g[:, None],
            g_n2b[:, None],
            ungroup_columns(g_bin[None], 4)[0].reshape(model_width, -1),
        ],
        axis=1,
    )
    tokens = g_qkv[0].shape[0]
    col = lambda b, c: b[:, c * model_width : (c + 1) * model_width]
    hi = g_small.astype(jnp.bfloat16)
    rest = g_small - hi.astype(jnp.float32)
    mid_part = rest.astype(jnp.bfloat16)
    low = (rest - mid_part.astype(jnp.float32)).astype(jnp.bfloat16)
    n_small = g_small.shape[1]
    pieces = jnp.concatenate([hi.T, mid_part.T, low.T], axis=0)
    enc_left = jnp.zeros((tokens, model_width), jnp.bfloat16).at[: 3 * n_small].set(pieces)
    picks = lax.broadcasted_iota(jnp.int32, (tokens, model_width), 1) == (
        lax.broadcasted_iota(jnp.int32, (tokens, model_width), 0) % n_small
    )
    rows_used = lax.broadcasted_iota(jnp.int32, (tokens, model_width), 0) < 3 * n_small
    enc_right = (picks & rows_used).astype(jnp.bfloat16)
    zero = jnp.zeros((tokens, model_width), jnp.bfloat16)
    mine_first = core == 0

    def stacks(lefts, rights):
        return (
            jnp.stack([jnp.stack(side) for side in lefts]),
            jnp.stack([jnp.stack(side) for side in rights]),
        )

    def products(stacked, pick_first):
        stacked_left, stacked_right = stacked
        left = jnp.where(pick_first, stacked_left[0], stacked_left[1])
        right = jnp.where(pick_first, stacked_right[0], stacked_right[1])
        return jnp.einsum("btk,btn->bkn", left, right, preferred_element_type=jnp.float32)

    def handed_over(stacked):
        sent = products(stacked, jnp.logical_not(mine_first)).astype(jnp.bfloat16)
        return lax.ppermute(sent, "core", perm=[(0, 1), (1, 0)])

    early = stacks(
        [[g_in[0]] * 4, [col(g_out[0], j) for j in range(4)]],
        [[col(g_in[1], c) for c in range(4)], [g_out[1]] * 4],
    )
    late = stacks(
        [[g_qkv[0]] * 3, [g_att[0], enc_left, zero]],
        [[col(g_qkv[1], c) for c in range(3)], [g_att[1], enc_right, zero]],
    )
    received = jnp.concatenate([handed_over(early), handed_over(late)], axis=0)
    every = tuple(jnp.concatenate([a, b], axis=1) for a, b in zip(early, late))
    half = products(every, mine_first) + received.astype(jnp.float32)
    part = lax.psum_scatter(half, SHARD_AXES, scatter_dimension=1, tiled=True)
    swap = [(0, 1), (1, 0)]
    part = part + lax.ppermute(part, "xh", perm=swap)
    other = lax.ppermute(part, "core", perm=swap)
    r0 = jnp.where(mine_first, part, other)
    r1 = jnp.where(mine_first, other, part)
    r_in = ungroup_columns(jnp.concatenate([r0[0], r0[1], r0[2], r0[3]], axis=1), 4)
    r_qkv = jnp.concatenate([r0[4], r0[5], r0[6]], axis=1)
    r_out = jnp.stack([r1[0], r1[1], r1[2], r1[3]], axis=1)
    r_att = r1[4]
    r_small = r1[5][:, :n_small]
    grad_inputs = upstream.reshape(inputs.shape)
    return (
        outputs,
        grad_inputs,
        r_qkv[None],
        r_small[:, 0:2].T[None],
        r_att[None],
        r_small[:, 2][None],
        r_small[:, 3][None],
        r_small[:, 4][None],
        r_in[None],
        r_small[:, 8:].reshape(-1)[None],
        r_out.reshape(-1, model_width)[None],
        r_small[:, 5][None],
        r_small[:, 6][None],
        r_small[:, 7][None],
    )


def solution(mesh):
    devices = mesh.devices.reshape(2, 2, 4, 2, 4)
    fine = jax.sharding.Mesh(devices, ("xh", "core", "y", "xl", "z"))
    seqs = P(("xh", "core", "y", "xl", "z"), None, None)
    rows = P(None, SHARD_AXES, None)
    vec = P(None, SHARD_AXES)
    return jax.shard_map(
        body,
        mesh=fine,
        in_specs=(
            seqs,
            P(("xh", "core", "y", "xl", "z")),
            seqs,
            rows,
            P(None, None, SHARD_AXES),
            rows,
            vec,
            vec,
            vec,
            rows,
            vec,
            rows,
            vec,
            vec,
            vec,
        ),
        out_specs=(
            seqs,
            seqs,
            rows,
            P(None, None, SHARD_AXES),
            rows,
            vec,
            vec,
            vec,
            rows,
            vec,
            rows,
            vec,
            vec,
            vec,
        ),
        check_vma=False,
    )
```

```python
import math

import jax
import jax.numpy as jnp
from jax import lax
from jax.experimental import pallas as pl
from jax.experimental.pallas import tpu as pltpu
from jax.sharding import PartitionSpec as P

HEAD_DIM = 64
LAYERS = 1


EPS = 1e-12
ROOT_HALF = 0.7071067811865476
INV_ROOT_TWO_PI = 0.3989422804014327


def _ffn_out_kernel(act_ref, w_ref, out_ref):
    @pl.when(pl.program_id(0) == 0)
    def _():
        out_ref[...] = jnp.zeros_like(out_ref)

    out_ref[...] += jnp.dot(act_ref[...], w_ref[...], preferred_element_type=jnp.float32)


def ffn_out(act_grouped, w_out):
    buffer, which, first_block = w_out
    tokens = act_grouped.shape[0]
    width = buffer.shape[1]
    groups = act_grouped.shape[1] // width
    return pl.pallas_call(
        _ffn_out_kernel,
        grid=(groups,),
        in_specs=[
            pl.BlockSpec((tokens, width), lambda j: (0, j)),
            pl.BlockSpec((None, width, width), lambda j: (which, 0, first_block + j)),
        ],
        out_specs=pl.BlockSpec((tokens, width), lambda j: (0, 0)),
        out_shape=jax.ShapeDtypeStruct((tokens, width), jnp.float32),
        cost_estimate=pl.CostEstimate(
            flops=2 * tokens * width * width * groups,
            bytes_accessed=2 * width * width * groups + 2 * tokens * width * groups + 4 * tokens * width,
            transcendentals=0,
        ),
    )(act_grouped, buffer)


def _ffn_out_back_kernel(grad_ref, w_ref, out_ref):
    out_ref[...] = lax.dot_general(
        grad_ref[...],
        w_ref[...],
        (((1,), (1,)), ((), ())),
        preferred_element_type=jnp.float32,
    )


def ffn_out_back(grad_bf, w_out):
    buffer, which, first_block = w_out
    tokens = grad_bf.shape[0]
    width = buffer.shape[1]
    groups = 4
    return pl.pallas_call(
        _ffn_out_back_kernel,
        grid=(groups,),
        in_specs=[
            pl.BlockSpec((tokens, width), lambda j: (0, 0)),
            pl.BlockSpec((None, width, width), lambda j: (which, 0, first_block + j)),
        ],
        out_specs=pl.BlockSpec((tokens, width), lambda j: (0, j)),
        out_shape=jax.ShapeDtypeStruct((tokens, width * groups), jnp.float32),
        cost_estimate=pl.CostEstimate(
            flops=2 * tokens * width * width * groups,
            bytes_accessed=2 * width * width * groups + 2 * tokens * width + 4 * tokens * width * groups,
            transcendentals=0,
        ),
    )(grad_bf, buffer)


def group_columns(x, groups):
    tokens = x.shape[0]
    return x.reshape(tokens, -1, groups).transpose(0, 2, 1).reshape(tokens, -1)


def ungroup_columns(x, groups):
    tokens = x.shape[0]
    return x.reshape(tokens, groups, -1).transpose(0, 2, 1).reshape(tokens, -1)


def batched(form, left, right):
    return jnp.einsum(form, left, right, preferred_element_type=jnp.float32)


def layer_norm(residual, gain, shift):
    row_mean = jnp.mean(residual, axis=-1, keepdims=True)
    centered = residual - row_mean
    variance = jnp.mean(centered * centered, axis=-1, keepdims=True)
    inv_std = lax.rsqrt(variance + EPS)
    normed = centered * inv_std
    return (normed * gain.astype(jnp.float32) + shift.astype(jnp.float32), normed, inv_std)


def norm_backward(upstream, normed, inv_std, gain):
    grad_gain = jnp.sum(upstream * normed, axis=0)
    grad_shift = jnp.sum(upstream, axis=0)
    scaled = upstream * gain.astype(jnp.float32)
    grad_res = inv_std * (
        scaled
        - jnp.mean(scaled, axis=-1, keepdims=True)
        - normed * jnp.mean(scaled * normed, axis=-1, keepdims=True)
    )
    return (grad_res, grad_gain, grad_shift)


def attention_scores(query_bf, key_bf, key_valid):
    scores = batched("bqhe,bkhe->bhqk", query_bf, key_bf) * (1.0 / math.sqrt(HEAD_DIM))
    return jnp.where(key_valid[:, None, None, :], scores, -1e30)


def layer_forward(hidden, hidden_bf, params, key_valid, batch_size):
    (
        w_qkv,
        b_qv,
        w_att,
        b_att,
        gain_one,
        shift_one,
        w_in,
        b_in,
        w_out,
        b_out,
        gain_two,
        shift_two,
    ) = params
    model_width = hidden.shape[1]
    seq_count = hidden.shape[0] // batch_size
    shape_heads = (batch_size, seq_count, model_width // HEAD_DIM, HEAD_DIM)
    packed = jnp.dot(hidden_bf, w_qkv, preferred_element_type=jnp.float32)
    bias_qv = b_qv.astype(jnp.float32)
    query_bf = (packed[:, :model_width] + bias_qv[0]).astype(jnp.bfloat16).reshape(shape_heads)
    key_bf = packed[:, model_width : 2 * model_width].astype(jnp.bfloat16).reshape(shape_heads)
    value_bf = (packed[:, 2 * model_width :] + bias_qv[1]).astype(jnp.bfloat16).reshape(shape_heads)
    scores = attention_scores(query_bf, key_bf, key_valid)
    row_max = jnp.max(scores, axis=-1, keepdims=True)
    row_lse = row_max + jnp.log(jnp.sum(jnp.exp(scores - row_max), axis=-1, keepdims=True))
    probs_bf = jnp.exp(scores - row_lse).astype(jnp.bfloat16)
    context_bf = (
        batched("bhqk,bkhe->bqhe", probs_bf, value_bf).astype(jnp.bfloat16).reshape(-1, model_width)
    )
    first = (
        hidden
        + jnp.dot(context_bf, w_att, preferred_element_type=jnp.float32)
        + b_att.astype(jnp.float32)
    )
    middle, normed_one, inv_one = layer_norm(first, gain_one, shift_one)
    middle_bf = middle.astype(jnp.bfloat16)
    pre_act = jnp.dot(middle_bf, w_in, preferred_element_type=jnp.float32) + b_in.astype(
        jnp.float32
    )
    act_bf = (pre_act * 0.5 * (1.0 + jax.scipy.special.erf(pre_act * ROOT_HALF))).astype(
        jnp.bfloat16
    )
    second = (
        middle
        + ffn_out(act_bf, w_out)
        + b_out.astype(jnp.float32)
    )
    result, normed_two, inv_two = layer_norm(second, gain_two, shift_two)
    stored = (
        hidden_bf,
        query_bf,
        key_bf,
        value_bf,
        row_lse,
        context_bf,
        normed_one,
        inv_one,
        middle_bf,
        pre_act,
        act_bf,
        normed_two,
        inv_two,
    )
    return (result, stored)


def layer_backward(upstream, stored, params, key_valid):
    (
        w_qkv,
        b_qv,
        w_att,
        b_att,
        gain_one,
        shift_one,
        w_in,
        b_in,
        w_out,
        b_out,
        gain_two,
        shift_two,
    ) = params
    (
        hidden_bf,
        query_bf,
        key_bf,
        value_bf,
        row_lse,
        context_bf,
        normed_one,
        inv_one,
        middle_bf,
        pre_act,
        act_bf,
        normed_two,
        inv_two,
    ) = stored
    model_width = upstream.shape[1]
    shape_heads = query_bf.shape
    grad_second, grad_gain_two, grad_shift_two = norm_backward(
        upstream, normed_two, inv_two, gain_two
    )
    grad_b_out = jnp.sum(grad_second, axis=0)
    second_bf = grad_second.astype(jnp.bfloat16)
    back_act = ffn_out_back(second_bf, w_out)
    cumulative = 0.5 * (1.0 + jax.scipy.special.erf(pre_act * ROOT_HALF))
    density = jnp.exp(-0.5 * pre_act * pre_act) * INV_ROOT_TWO_PI
    grad_pre = back_act * (cumulative + pre_act * density)
    pre_bf = grad_pre.astype(jnp.bfloat16)
    grad_b_in = jnp.sum(grad_pre, axis=0)
    grad_middle = grad_second + jnp.dot(pre_bf, w_in.T, preferred_element_type=jnp.float32)
    grad_first, grad_gain_one, grad_shift_one = norm_backward(
        grad_middle, normed_one, inv_one, gain_one
    )
    grad_b_att = jnp.sum(grad_first, axis=0)
    first_bf = grad_first.astype(jnp.bfloat16)
    grad_context = (
        jnp.dot(first_bf, w_att.T, preferred_element_type=jnp.float32)
        .astype(jnp.bfloat16)
        .reshape(shape_heads)
    )
    scores = attention_scores(query_bf, key_bf, key_valid)
    probs = jnp.exp(scores - row_lse)
    grad_value = batched("bhqk,bqhe->bkhe", probs.astype(jnp.bfloat16), grad_context).reshape(
        -1, model_width
    )
    grad_probs = batched("bqhe,bkhe->bhqk", grad_context, value_bf)
    inner = jnp.sum(probs * grad_probs, axis=-1, keepdims=True)
    grad_scores = (probs * (grad_probs - inner) * (1.0 / math.sqrt(HEAD_DIM))).astype(jnp.bfloat16)
    grad_query = batched("bhqk,bkhe->bqhe", grad_scores, key_bf).reshape(-1, model_width)
    grad_key = batched("bhqk,bqhe->bkhe", grad_scores, query_bf).reshape(-1, model_width)
    grad_b_qv = jnp.stack([jnp.sum(grad_query, axis=0), jnp.sum(grad_value, axis=0)])
    packed_bf = jnp.concatenate([grad_query, grad_key, grad_value], axis=1).astype(jnp.bfloat16)
    grad_hidden = grad_first + jnp.dot(packed_bf, w_qkv.T, preferred_element_type=jnp.float32)
    terms = (
        (hidden_bf, packed_bf),
        grad_b_qv,
        (context_bf, first_bf),
        grad_b_att,
        grad_gain_one,
        grad_shift_one,
        (middle_bf, pre_bf),
        grad_b_in,
        (act_bf, second_bf),
        grad_b_out,
        grad_gain_two,
        grad_shift_two,
    )
    return (grad_hidden, terms)


SHARD_AXES = ("y", "xl", "z")
PAIR_AXES = ("xh", "core")


def pack_halves(w_qkv, w_att, w_in, w_out, small):
    rows = w_qkv.shape[0]
    split = w_qkv.shape[1]
    pad = jnp.zeros((rows, small.shape[1]), w_qkv.dtype)
    first = jnp.concatenate([w_qkv, w_in[:, :split], pad], axis=1)
    second = jnp.concatenate(
        [w_att, w_in[:, split:], w_out.reshape(rows, -1), small], axis=1
    )
    return first, second


def unpack_halves(first, second, width, ff):
    split = 3 * width
    w_qkv = first[:, :split]
    w_in = jnp.concatenate([first[:, split : 2 * split], second[:, width : width + ff - split]], axis=1)
    at = width + ff - split
    w_att = second[:, :width]
    w_out = second[:, at : at + ff]
    small = second[:, at + ff :]
    return w_qkv, w_att, w_in, w_out, small


def body(
    inputs,
    lengths,
    cotangent,
    w_qkv,
    b_qv,
    w_att,
    b_att,
    norm1_gain,
    norm1_bias,
    w_in,
    b_in,
    w_out,
    b_out,
    norm2_gain,
    norm2_bias,
):
    batch_size, seq_count, model_width = inputs.shape
    ff = w_in.shape[2]
    rows = w_qkv.shape[1]
    core = lax.axis_index("core")
    key_valid = lax.broadcasted_iota(jnp.int32, (batch_size, seq_count), 1) < lengths[:, None]
    hidden = inputs.astype(jnp.float32).reshape(-1, model_width)
    hidden_bf = inputs.reshape(-1, model_width)
    small = jnp.concatenate(
        [
            b_qv[0].T,
            b_att[0][:, None],
            norm1_gain[0][:, None],
            norm1_bias[0][:, None],
            b_out[0][:, None],
            norm2_gain[0][:, None],
            norm2_bias[0][:, None],
            b_in[0].reshape(rows, -1),
        ],
        axis=1,
    )
    first, second = pack_halves(w_qkv[0], w_att[0], group_columns(w_in[0], 4), w_out[0], small)
    mine = jnp.where(core == 0, first, second)
    gathered = lax.all_gather(mine, SHARD_AXES, axis=0, tiled=True)
    both = lax.all_gather(gathered, "core", axis=0, tiled=False)
    f_qkv, f_att, f_in, f_out, f_small = unpack_halves(both[0], both[1], model_width, ff)
    f_out = (both, 1, (model_width + ff - 3 * model_width) // model_width)
    f_bqv = f_small[:, 0:2].T
    f_bin = group_columns(f_small[:, 8:].reshape(1, ff), 4)[0]
    params = (
        f_qkv,
        f_bqv,
        f_att,
        f_small[:, 2],
        f_small[:, 3],
        f_small[:, 4],
        f_in,
        f_bin,
        f_out,
        f_small[:, 5],
        f_small[:, 6],
        f_small[:, 7],
    )
    hidden, stored = layer_forward(hidden, hidden_bf, params, key_valid, batch_size)
    outputs = hidden.astype(jnp.bfloat16).reshape(inputs.shape)
    upstream = cotangent.astype(jnp.float32).reshape(-1, model_width)
    upstream, terms = layer_backward(upstream, stored, params, key_valid)
    (g_qkv, g_bqv, g_att, g_batt, g_n1g, g_n1b, g_in, g_bin, g_out, g_bout, g_n2g, g_n2b) = terms
    g_small = jnp.concatenate(
        [
            g_bqv.T,
            g_batt[:, None],
            g_n1g[:, None],
            g_n1b[:, None],
            g_bout[:, None],
            g_n2g[:, None],
            g_n2b[:, None],
            ungroup_columns(g_bin[None], 4)[0].reshape(model_width, -1),
        ],
        axis=1,
    )
    tokens = g_qkv[0].shape[0]
    col = lambda b, c: b[:, c * model_width : (c + 1) * model_width]
    hi = g_small.astype(jnp.bfloat16)
    rest = g_small - hi.astype(jnp.float32)
    mid_part = rest.astype(jnp.bfloat16)
    low = (rest - mid_part.astype(jnp.float32)).astype(jnp.bfloat16)
    n_small = g_small.shape[1]
    pieces = jnp.concatenate([hi.T, mid_part.T, low.T], axis=0)
    enc_left = jnp.zeros((tokens, model_width), jnp.bfloat16).at[: 3 * n_small].set(pieces)
    picks = lax.broadcasted_iota(jnp.int32, (tokens, model_width), 1) == (
        lax.broadcasted_iota(jnp.int32, (tokens, model_width), 0) % n_small
    )
    rows_used = lax.broadcasted_iota(jnp.int32, (tokens, model_width), 0) < 3 * n_small
    enc_right = (picks & rows_used).astype(jnp.bfloat16)
    zero = jnp.zeros((tokens, model_width), jnp.bfloat16)
    mine_first = core == 0

    def stacks(lefts, rights):
        return (
            jnp.stack([jnp.stack(side) for side in lefts]),
            jnp.stack([jnp.stack(side) for side in rights]),
        )

    def products(stacked, pick_first):
        stacked_left, stacked_right = stacked
        left = jnp.where(pick_first, stacked_left[0], stacked_left[1])
        right = jnp.where(pick_first, stacked_right[0], stacked_right[1])
        return jnp.einsum("btk,btn->bkn", left, right, preferred_element_type=jnp.float32)

    def handed_over(stacked):
        sent = products(stacked, jnp.logical_not(mine_first)).astype(jnp.bfloat16)
        return lax.ppermute(sent, "core", perm=[(0, 1), (1, 0)])

    early = stacks(
        [[g_in[0]] * 4 + [zero], [col(g_out[0], j) for j in range(4)] + [g_att[0]]],
        [[col(g_in[1], c) for c in range(4)] + [zero], [g_out[1]] * 4 + [g_att[1]]],
    )
    late = stacks(
        [[g_qkv[0]] * 2, [g_qkv[0], enc_left]],
        [[col(g_qkv[1], 0), col(g_qkv[1], 1)], [col(g_qkv[1], 2), enc_right]],
    )
    received = jnp.concatenate([handed_over(early), handed_over(late)], axis=0)
    every = tuple(jnp.concatenate([a, b], axis=1) for a, b in zip(early, late))
    half = products(every, mine_first) + received.astype(jnp.float32)
    part = lax.psum_scatter(half, SHARD_AXES, scatter_dimension=1, tiled=True)
    swap = [(0, 1), (1, 0)]
    part = part + lax.ppermute(part, "xh", perm=swap)
    other = lax.ppermute(part, "core", perm=swap)
    r0 = jnp.where(mine_first, part, other)
    r1 = jnp.where(mine_first, other, part)
    r_in = ungroup_columns(jnp.concatenate([r0[0], r0[1], r0[2], r0[3]], axis=1), 4)
    r_qkv = jnp.concatenate([r0[5], r0[6], r1[5]], axis=1)
    r_out = jnp.stack([r1[0], r1[1], r1[2], r1[3]], axis=1)
    r_att = r1[4]
    r_small = r1[6][:, :n_small]
    grad_inputs = upstream.reshape(inputs.shape)
    return (
        outputs,
        grad_inputs,
        r_qkv[None],
        r_small[:, 0:2].T[None],
        r_att[None],
        r_small[:, 2][None],
        r_small[:, 3][None],
        r_small[:, 4][None],
        r_in[None],
        r_small[:, 8:].reshape(-1)[None],
        r_out.reshape(-1, model_width)[None],
        r_small[:, 5][None],
        r_small[:, 6][None],
        r_small[:, 7][None],
    )


def solution(mesh):
    devices = mesh.devices.reshape(2, 2, 4, 2, 4)
    fine = jax.sharding.Mesh(devices, ("xh", "core", "y", "xl", "z"))
    seqs = P(("xh", "core", "y", "xl", "z"), None, None)
    rows = P(None, SHARD_AXES, None)
    vec = P(None, SHARD_AXES)
    return jax.shard_map(
        body,
        mesh=fine,
        in_specs=(
            seqs,
            P(("xh", "core", "y", "xl", "z")),
            seqs,
            rows,
            P(None, None, SHARD_AXES),
            rows,
            vec,
            vec,
            vec,
            rows,
            vec,
            rows,
            vec,
            vec,
            vec,
        ),
        out_specs=(
            seqs,
            seqs,
            rows,
            P(None, None, SHARD_AXES),
            rows,
            vec,
            vec,
            vec,
            rows,
            vec,
            rows,
            vec,
            vec,
            vec,
        ),
        check_vma=False,
    )
```
